32 devices in a mesh: dp: 2 (over y), tensor: 16 (over z, x, core).
Axes of the slice: x: 2, y: 2, z: 4, core: 2. Of those that a mesh axis runs over, the one named last changes fastest.
Arguments:
- inputs: float32 [256, 4096], P('dp', 'tensor'), may hold values from -6 to 6
- out_grad: float32 [256, 4096], P('dp', 'tensor'), may hold values from -6 to 6
- up_weight: float32 [768, 128, 128], P('tensor'), may hold values from -0.25 to 0.25
- down_weight: float32 [768, 128, 128], P('tensor'), may hold values from -0.109375 to 0.109375
- up_left: float32 [4096, 128], P('tensor'), may hold values from -0.09375 to 0.09375
- up_right: float32 [128, 16384], P(None, 'tensor'), may hold values from -0.5 to 0.5
- down_left: float32 [16384, 128], P('tensor'), may hold values from -0.046875 to 0.046875
- down_right: float32 [128, 4096], P(None, 'tensor'), may hold values from -0.5 to 0.5
- model_block: int32 [768], P('tensor'), may hold values from 0 to 31, as said below
- hidden_block: int32 [768], P('tensor'), may hold values from 0 to 7
- live_slots: int32 [16], P('tensor'), may hold values from 24 to 48, as said below
Outputs:
- result: float32 [256, 4096], P('dp', 'tensor')
- input_grad: float32 [256, 4096], P('dp', 'tensor')
- up_grad: float32 [768, 128, 128], P('tensor', 'dp')
- down_grad: float32 [768, 128, 128], P('tensor', 'dp')
- up_left_grad: float32 [4096, 128], P(('tensor', 'dp'))
- up_right_grad: float32 [128, 16384], P('dp', 'tensor')
- down_left_grad: float32 [16384, 128], P(('tensor', 'dp'))
- down_right_grad: float32 [128, 4096], P('dp', 'tensor')
The draws below stay inside these ranges and needn't reach their ends.
Inputs may be any that keep to these rules, and one draw needn't show every extreme that they name: `model_block`: with g the slot's hidden block counted over all owners, the slot's model block differs from g mod 32 in at most one bit. `live_slots`: at least one owner has all 48 slots live.
All inputs are finite; a program needn't handle non-finite values.
Results may differ from the reference program's by a relative error of at most 0.0003.
Values sent between devices are 32-bit elements; how exact they have to be, the bound alone decides.
A program may use at most 64 MiB of HBM per device.

```python
import jax
import jax.numpy as jnp
from jax import lax

D = 4096
FF = 16384
BLK = 128
RANK = 128
TOKENS = 256
DBLOCKS = 32
HBLOCKS = 8
CAP = 48
OWNERS = 16
SLOTS = 768


def slot_pattern(key):
    folded = jax.random.fold_in(key, 7)
    key_hidden, key_level = jax.random.split(folded)
    hidden = jax.random.randint(key_hidden, (SLOTS,), 0, HBLOCKS, dtype=jnp.int32)
    levels = DBLOCKS.bit_length() - 1
    section_bit = jax.random.randint(key_level, (SLOTS,), 0, levels + 1, dtype=jnp.int32)
    owner_id = jnp.arange(SLOTS, dtype=jnp.int32) // CAP
    column = (owner_id * HBLOCKS + hidden) % DBLOCKS
    toggled = jnp.where(section_bit == levels, jnp.int32(0), jnp.left_shift(jnp.int32(1), jnp.minimum(section_bit, levels - 1)))
    return (hidden, jnp.bitwise_xor(column, toggled))


def draw_model_block(key, part):
    return slot_pattern(key)[1]


def draw_hidden_block(key, part):
    return slot_pattern(key)[0]


def draw_live_slots(key, part):
    folded = jax.random.fold_in(key, 13)
    key_count, key_full = jax.random.split(folded)
    counted = jax.random.randint(key_count, (OWNERS,), CAP // 2, CAP + 1, dtype=jnp.int32)
    full_owner = jax.random.randint(key_full, (), 0, OWNERS, dtype=jnp.int32)
    return jnp.where(jnp.arange(OWNERS, dtype=jnp.int32) == full_owner, jnp.int32(CAP), counted)


def level_of(stream_key, shape, cuts, least, top_value):
    def one(axis_at, blocks):
        draws = jax.random.uniform(jax.random.fold_in(jax.random.fold_in(stream_key, 6), axis_at), (blocks,), jnp.float32, least / len(cuts), top_value / len(cuts))
        return jnp.repeat(jnp.exp(draws), shape[axis_at] // blocks).reshape((-1,) + (1,) * (len(shape) - axis_at - 1))

    level = one(*cuts[0])
    for cut in cuts[1:]:
        level = level * one(*cut)
    return level


def gaussian(rng, shape, width, reach, cuts=(), kind=jnp.bfloat16):
    loudness = level_of(rng, shape, cuts, -0.22, 0.18) if cuts else 1.0
    array = jax.random.normal(rng, shape, jnp.float32) * width * loudness
    return jnp.minimum(jnp.maximum(array, -reach), reach).astype(kind)


def setup_inputs(seed: int = 0) -> dict:
    key_of = jax.random.split(jax.random.key(seed), 12)
    return {
        "inputs": gaussian(key_of[0], (TOKENS, D), 1.0, 6.0, ((0, 2), (1, 16)), jnp.float32),
        "out_grad": gaussian(key_of[1], (TOKENS, D), 1.0, 6.0, ((0, 2), (1, 16)), jnp.float32),
        "up_weight": gaussian(key_of[2], (SLOTS, BLK, BLK), (5 * BLK) ** -0.5, 0.25, ((0, 16),), jnp.float32),
        "down_weight": gaussian(key_of[3], (SLOTS, BLK, BLK), (SLOTS * BLK // DBLOCKS) ** -0.5, 0.109375, ((0, 16),), jnp.float32),
        "up_left": gaussian(key_of[4], (D, RANK), D ** -0.5, 0.09375, ((0, 16),), jnp.float32),
        "up_right": gaussian(key_of[5], (RANK, FF), RANK ** -0.5, 0.5, ((1, 16),), jnp.float32),
        "down_left": gaussian(key_of[6], (FF, RANK), FF ** -0.5, 0.046875, ((0, 16),), jnp.float32),
        "down_right": gaussian(key_of[7], (RANK, D), RANK ** -0.5, 0.5, ((1, 16),), jnp.float32),
        "model_block": draw_model_block(jax.random.fold_in(key_of[11], 71), 0),
        "hidden_block": draw_hidden_block(jax.random.fold_in(key_of[11], 71), 0),
        "live_slots": draw_live_slots(jax.random.fold_in(key_of[11], 71), 0),
    }


highest = lax.Precision.HIGHEST

def activation(values):
    return jax.nn.gelu(values, approximate=True)

def onehot(indices, extent):
    return (indices[:, None] == jnp.arange(extent, dtype=jnp.int32)[None, :]).astype(jnp.float32)

def reference(inputs, out_grad, up_weight, down_weight, up_left, up_right, down_left, down_right, model_block, hidden_block, live_slots):
    row_count = inputs.shape[0]
    hidden_width = HBLOCKS * BLK
    slot_index = jnp.arange(SLOTS, dtype=jnp.int32)
    owner_id = slot_index // CAP
    alive_mask = (slot_index % CAP < live_slots[owner_id]).astype(jnp.float32)
    up_live = (up_weight * alive_mask[:, None, None]).reshape(OWNERS, CAP, BLK, BLK)
    down_live = (down_weight * alive_mask[:, None, None]).reshape(OWNERS, CAP, BLK, BLK)
    model_owned = model_block.reshape(OWNERS, CAP)
    hidden_owned = hidden_block.reshape(OWNERS, CAP)
    alive_owned = alive_mask.reshape(OWNERS, CAP)
    right_owned = up_right.reshape(RANK, OWNERS, hidden_width).transpose(1, 0, 2)
    left_owned = down_left.reshape(OWNERS, hidden_width, RANK)
    split_in = inputs.reshape(row_count, DBLOCKS, BLK)
    split_grad = out_grad.reshape(row_count, DBLOCKS, BLK)
    low_in = jnp.dot(inputs, up_left, precision=highest)

    def forward_up(running, pieces):
        weight, models, hiddens, right = pieces
        chosen = jnp.take(split_in, models, axis=1)
        slot_out = jnp.einsum('tsk,skn->tsn', chosen, weight, precision=highest)
        merged = jnp.einsum('tsn,sh->thn', slot_out, onehot(hiddens, HBLOCKS), precision=highest)
        return (running, merged.reshape(row_count, hidden_width) + jnp.dot(low_in, right, precision=highest))
    _, preact = lax.scan(forward_up, jnp.zeros((), jnp.float32), (up_live, model_owned, hidden_owned, right_owned))
    hidden = activation(preact)
    low_mid = jnp.einsum('otw,owr->tr', hidden, left_owned, precision=highest)

    def forward_down(running, pieces):
        weight, models, hiddens, hidden_part = pieces
        chosen = jnp.take(hidden_part.reshape(row_count, HBLOCKS, BLK), hiddens, axis=1)
        slot_out = jnp.einsum('tsk,skn->tsn', chosen, weight, precision=highest)
        placed = jnp.einsum('tsn,sm->tmn', slot_out, onehot(models, DBLOCKS), precision=highest)
        return (running + placed.reshape(row_count, D), jnp.zeros((), jnp.float32))
    sparse_out, _ = lax.scan(forward_down, jnp.zeros((row_count, D), jnp.float32), (down_live, model_owned, hidden_owned, hidden))
    result = sparse_out + jnp.dot(low_mid, down_right, precision=highest)
    back_mid = jnp.dot(out_grad, down_right.T, precision=highest)

    def backward_down(running, pieces):
        weight, models, hiddens, alive, hidden_part, preact_part, left = pieces
        chosen_grad = jnp.take(split_grad, models, axis=1)
        slot_back = jnp.einsum('tsn,skn->tsk', chosen_grad, weight, precision=highest)
        merged = jnp.einsum('tsk,sh->thk', slot_back, onehot(hiddens, HBLOCKS), precision=highest)
        hidden_grad = merged.reshape(row_count, hidden_width) + jnp.dot(back_mid, left.T, precision=highest)
        _, pullback = jax.vjp(activation, preact_part)
        preact_grad = pullback(hidden_grad)[0]
        chosen_hidden = jnp.take(hidden_part.reshape(row_count, HBLOCKS, BLK), hiddens, axis=1)
        weight_grad = jnp.einsum('tsk,tsn->skn', chosen_hidden, chosen_grad, precision=highest) * alive[:, None, None]
        left_grad = jnp.dot(hidden_part.T, back_mid, precision=highest)
        return (running, (preact_grad, weight_grad, left_grad))
    _, (preact_grad, down_grad, down_left_grad) = lax.scan(backward_down, jnp.zeros((), jnp.float32), (down_live, model_owned, hidden_owned, alive_owned, hidden, preact, left_owned))
    back_in = jnp.einsum('otw,orw->tr', preact_grad, right_owned, precision=highest)

    def backward_up(running, pieces):
        weight, models, hiddens, alive, grad_part = pieces
        chosen_grad = jnp.take(grad_part.reshape(row_count, HBLOCKS, BLK), hiddens, axis=1)
        slot_back = jnp.einsum('tsn,skn->tsk', chosen_grad, weight, precision=highest)
        placed = jnp.einsum('tsk,sm->tmk', slot_back, onehot(models, DBLOCKS), precision=highest)
        chosen_in = jnp.take(split_in, models, axis=1)
        weight_grad = jnp.einsum('tsk,tsn->skn', chosen_in, chosen_grad, precision=highest) * alive[:, None, None]
        return (running + placed.reshape(row_count, D), weight_grad)
    sparse_in, up_grad = lax.scan(backward_up, jnp.zeros((row_count, D), jnp.float32), (up_live, model_owned, hidden_owned, alive_owned, preact_grad))
    input_grad = sparse_in + jnp.dot(back_in, up_left.T, precision=highest)
    up_left_grad = jnp.dot(inputs.T, back_in, precision=highest)
    up_right_grad = jnp.einsum('tr,otw->row', low_in, preact_grad, precision=highest).reshape(RANK, FF)
    down_right_grad = jnp.dot(low_mid.T, out_grad, precision=highest)
    return (result, input_grad, up_grad.reshape(SLOTS, BLK, BLK), down_grad.reshape(SLOTS, BLK, BLK), up_left_grad, up_right_grad, down_left_grad.reshape(FF, RANK), down_right_grad)
```

```python
import functools

import jax
import jax.numpy as jnp
from jax import lax
from jax.experimental import pallas as pl
from jax.experimental.pallas import tpu as pltpu
from jax.sharding import PartitionSpec as P

MESH = pl.DeviceIdType.MESH
VM = pl.BlockSpec(memory_space=pltpu.VMEM)
SM = pl.BlockSpec(memory_space=pltpu.SMEM)
f32 = jnp.float32


def halves(v):
    hi = v.astype(jnp.bfloat16)
    lo = (v - hi.astype(f32)).astype(jnp.bfloat16)
    return hi, lo


def left3(v, axis):
    hi, lo = halves(v)
    return jnp.concatenate([hi, hi, lo], axis=axis)


def right3(v, axis):
    hi, lo = halves(v)
    return jnp.concatenate([hi, lo, hi], axis=axis)


def contract(a, b, da, db):
    return lax.dot_general(a, b, (((da,), (db,)), ((), ())), preferred_element_type=f32)


def dot3(a, b, da, db):
    return contract(left3(a, da), right3(b, db), da, db)


def flip(a, k, size):
    out, bit = 0, 1
    while bit < size:
        out = out + (((a // bit) % 2 + (k // bit) % 2) % 2) * bit
        bit *= 2
    return out


class Copies:
    def __init__(self, sems):
        self.sems, self.count, self.made = sems, 0, []

    def send(self, src, dst, recv, where, cond=None):
        sem = self.sems.at[self.count]
        self.count += 1
        copy = pltpu.make_async_remote_copy(
            src_ref=src, dst_ref=dst, send_sem=sem, recv_sem=recv, device_id=where, device_id_type=MESH
        )
        if cond is None:
            copy.start()
        else:
            pl.when(cond)(copy.start)
        self.made.append((copy, cond))

    def drain(self):
        for copy, cond in self.made:
            if cond is None:
                copy.wait_send()
            else:
                pl.when(cond)(copy.wait_send)


def arrived(ref, recv, where, cond=None):
    copy = pltpu.make_async_remote_copy(
        src_ref=ref, dst_ref=ref, send_sem=recv, recv_sem=recv, device_id=where, device_id_type=MESH
    )
    if cond is None:
        copy.wait_recv()
    else:
        pl.when(cond)(copy.wait_recv)


def line_steps(a, A):
    out = [(a, 0, None)]
    for k in range(1, A):
        out.append(((a + A - k) % A, -1, a >= k))
        out.append(((a + k) % A, 1, a + k < A))
    return out


def greet(d, t, dp, T):
    barrier = pltpu.get_barrier_semaphore()
    for k in range(1, T):
        pl.semaphore_signal(barrier, inc=1, device_id=(d, lax.rem(t + k, T)), device_id_type=MESH)
    for k in range(1, dp):
        pl.semaphore_signal(barrier, inc=1, device_id=(lax.rem(d + k, dp), t), device_id_type=MESH)
    pl.semaphore_wait(barrier, T - 1 + dp - 1)


class Total:
    def __init__(self, out, d, t, T, part, inbox, copies, in_sem, out_sem):
        self.out, self.d, self.t, self.T, self.part, self.inbox = out, d, t, T, part, inbox
        self.copies, self.in_sem, self.out_sem = copies, in_sem, out_sem
        rank = part.shape[1]
        self.rows = max(8, rank // T)
        self.count = rank // self.rows

    def cond(self, j):
        return None if self.count >= self.T else j < self.count

    def piece(self, ref, j):
        return ref.at[:, pl.ds(pl.multiple_of(j * self.rows, self.rows), self.rows), :]

    def begin(self):
        for k in range(1, self.T):
            j = lax.rem(self.t + k, self.T)
            cond = self.cond(j)
            at = j if cond is None else lax.rem(j, self.count)
            self.copies.send(
                self.piece(self.part, at), self.inbox.at[self.T - k], self.in_sem.at[self.T - k], (self.d, j), cond
            )

    def reduce(self):
        cond = self.cond(self.t)
        at = self.t if cond is None else lax.rem(self.t, self.count)

        def work():
            span = pl.ds(pl.multiple_of(at * self.rows, self.rows), self.rows)
            total = self.part[:, span, :]
            for k in range(1, self.T):
                arrived(self.inbox.at[k], self.in_sem.at[k], (self.d, self.t))
                total = total + self.inbox[k]
            self.out[:, span, :] = total

        if cond is None:
            work()
        else:
            pl.when(cond)(work)
        for k in range(1, self.T):
            j = lax.rem(self.t + k, self.T)
            self.copies.send(
                self.piece(self.out, at), self.piece(self.out, at), self.out_sem.at[self.T - k], (self.d, j), cond
            )

    def finish(self):
        for k in range(1, self.T):
            j = lax.rem(self.t + k, self.T)
            cond = self.cond(j)
            at = j if cond is None else lax.rem(j, self.count)
            wait = functools.partial(arrived, self.piece(self.out, at), self.out_sem.at[k], (self.d, j))
            if cond is None:
                wait()
            else:
                pl.when(cond)(wait)


def gather_kernel(
    dp, T, inp_ref, og_ref, upl_ref, dnr_ref,
    full, peer_g, peer_own, red, peer_red,
    x_ref, g_ref, part, inbox, send_sem, full_sem, pg_sem, po_sem, in_sem, out_sem, pr_sem,
):
    d, t = lax.axis_index("dp"), lax.axis_index("tensor")
    c, b, a = t % 2, (t // 2) % 2, t // 4
    A = T // 4
    bps, blk = x_ref.shape[0], x_ref.shape[1]
    for j in range(bps):
        x_ref[j] = inp_ref[:, j * blk : (j + 1) * blk].T
        g_ref[j] = og_ref[:, j * blk : (j + 1) * blk].T
    core, side = (d, a * 4 + b * 2 + 1 - c), (d, a * 4 + (1 - b) * 2 + c)
    before, after = (d, (t + T - 4) % T), (d, (t + 4) % T)
    copies = Copies(send_sem)
    greet(d, t, dp, T)

    def to_peers(src_g, s, cond=None):
        for k in range(dp - 1):
            copies.send(src_g, peer_g.at[k, s], pg_sem.at[k, s], (lax.rem(d + k + 1, dp), t), cond)

    def two(src_x, src_g, s, where, cond=None):
        copies.send(src_x, full.at[s, 0], full_sem.at[s, 0], where, cond)
        copies.send(src_g, full.at[s, 1], full_sem.at[s, 1], where, cond)

    def got(s, where, cond=None):
        arrived(full.at[s, 0], full_sem.at[s, 0], where, cond)
        arrived(full.at[s, 1], full_sem.at[s, 1], where, cond)

    two(x_ref, g_ref, t, before, a >= 1)
    two(x_ref, g_ref, t, after, a + 1 < A)
    two(x_ref, g_ref, t, side)
    to_peers(g_ref, t)
    two(x_ref, g_ref, t, core)
    feats = bps * blk
    part[0] = dot3(upl_ref[...], x_ref[...].reshape(feats, x_ref.shape[2]), 0, 0)
    part[1] = dot3(dnr_ref[...], g_ref[...].reshape(feats, x_ref.shape[2]), 1, 0)
    total = Total(red, d, t, T, part, inbox, copies, in_sem, out_sem)
    total.begin()
    full[t, 0] = x_ref[...]
    full[t, 1] = g_ref[...]
    mine = []
    for row, way, here in line_steps(a, A):
        s = row * 4 + b * 2 + c
        if way != 0:
            got(s, side, here)
            onward = (here & (a + 1 < A)) if way < 0 else (here & (a >= 1))
            two(full.at[s, 0], full.at[s, 1], s, after if way < 0 else before, onward)
            two(full.at[s, 0], full.at[s, 1], s, side, here)
            to_peers(full.at[s, 1], s, here)
            two(full.at[s, 0], full.at[s, 1], s, core, here)
        mine.append((s, here))
        s = row * 4 + (1 - b) * 2 + c
        got(s, side, here)
        to_peers(full.at[s, 1], s, here)
        two(full.at[s, 0], full.at[s, 1], s, core, here)
        mine.append((s, here))
        if way == 0:
            total.reduce()
    total.finish()
    for k in range(dp - 1):
        copies.send(red, peer_red.at[k], pr_sem.at[k], (lax.rem(d + k + 1, dp), t))
        copies.send(x_ref, peer_own.at[k], po_sem.at[k], (lax.rem(d + k + 1, dp), t))
    for s, here in mine:
        for k in range(dp - 1):
            arrived(peer_g.at[k, s], pg_sem.at[k, s], core, here)
            copies.send(peer_g.at[k, s], peer_g.at[k, s], pg_sem.at[k, s], core, here)
    for k in range(2 * A):
        s = k * 2 + 1 - c
        got(s, core)
        for p in range(dp - 1):
            arrived(peer_g.at[p, s], pg_sem.at[p, s], core)
    for k in range(dp - 1):
        arrived(peer_own.at[k], po_sem.at[k], core)
        arrived(peer_red.at[k], pr_sem.at[k], core)
    copies.drain()


def scatter_kernel(
    dp, T, unroll, mb_ref, hb_ref, live_ref, terms, low, hd, full, peer_g,
    summed, red, peer_hd, peer_red, peer_x, dng,
    core_box, stage, side_box, acc, line_box, inbox,
    send_sem, core_sem, side_sem, line_sem, hd_sem, px_sem, in_sem, out_sem, pr_sem,
):
    d, t = lax.axis_index("dp"), lax.axis_index("tensor")
    c, b, a = t % 2, (t // 2) % 2, t // 4
    A = T // 4
    core, side = (d, a * 4 + b * 2 + 1 - c), (d, a * 4 + (1 - b) * 2 + c)
    copies = Copies(send_sem)
    greet(d, t, dp, T)
    order = [flip(a, k, A) for k in range(A)][::-1]
    for far in (1, 0):
        for row in order:
            col = (1 - b) if far else b
            i = row * 2 + col
            copies.send(terms.at[i * 2 + 1 - c], core_box.at[i], core_sem.at[i], core)
    for k in range(dp - 1):
        for n in range(2):
            copies.send(hd.at[n], peer_hd.at[k, n], hd_sem.at[k, n], (lax.rem(d + k + 1, dp), t))
    total = Total(red, d, t, T, low, inbox, copies, in_sem, out_sem)
    total.begin()
    part_rows = peer_x.shape[3]
    for n in range(2 * A):
        for k in range(dp - 1):
            other = lax.rem(d + k + 1, dp)
            rows = pl.ds(pl.multiple_of(other * part_rows, part_rows), part_rows)
            s = n * 2 + c
            copies.send(full.at[s, 0, :, rows, :], peer_x.at[k, s], px_sem.at[k, s], (other, t))
    for row in order:
        i = row * 2 + 1 - b
        arrived(core_box.at[i], core_sem.at[i], core)
        stage[row] = terms[i * 2 + c] + core_box[i]
        copies.send(stage.at[row], side_box.at[row], side_sem.at[row], side)
    total.reduce()
    for n, row in enumerate(order):
        i = row * 2 + b
        k = A - 1 - n
        arrived(core_box.at[i], core_sem.at[i], core)
        arrived(side_box.at[row], side_sem.at[row], side)
        acc[row] = terms[i * 2 + c] + core_box[i] + side_box[row]
        if k > 0:
            copies.send(acc.at[row], line_box.at[k], line_sem.at[k], (d, row * 4 + b * 2 + c))
    total.finish()
    for k in range(dp - 1):
        copies.send(red, peer_red.at[k], pr_sem.at[k], (lax.rem(d + k + 1, dp), t))
    for k in range(dp - 1):
        arrived(peer_hd.at[k, 0], hd_sem.at[k, 0], core)
        arrived(peer_hd.at[k, 1], hd_sem.at[k, 1], core)
    slots, half, _ = dng.shape
    bps = full.shape[2]
    live = live_ref[0]
    mine = pl.ds(pl.multiple_of(d * half, half), half)

    @pl.loop(0, slots // unroll)
    def _(i):
        for j in range(unroll):
            s = i * unroll + j
            keep = (s < live).astype(f32)
            m, h = mb_ref[s], hb_ref[s]
            hidden = [hd[0, h, mine, :]] + [peer_hd[k, 0, h, mine, :] for k in range(dp - 1)]
            g = [full[m // bps, 1, m % bps]] + [peer_g[k, m // bps, m % bps] for k in range(dp - 1)]
            dng[s] = dot3(jnp.concatenate(hidden, axis=1), jnp.concatenate(g, axis=1), 1, 1) * keep

    result = acc[a]
    for k in range(1, A):
        arrived(line_box.at[k], line_sem.at[k], core)
        result = result + line_box[k]
    summed[...] = result
    for n in range(2 * A):
        for k in range(dp - 1):
            s = n * 2 + c
            arrived(peer_x.at[k, s], px_sem.at[k, s], core)
            copies.send(peer_x.at[k, s], peer_x.at[k, s], px_sem.at[k, s], core)
    for k in range(dp - 1):
        for n in range(2 * A):
            s = n * 2 + 1 - c
            arrived(peer_x.at[k, s], px_sem.at[k, s], core)
        arrived(peer_red.at[k], pr_sem.at[k], core)
    copies.drain()


def layer_kernel(
    unroll, mb_ref, hb_ref, live_ref, full, red, upw, dnw, upr, dnl,
    terms, low, hd,
    split_x, split_g, split_hd, pre, grad,
):
    slots, blk = upw.shape[0], upw.shape[1]
    bps, tokens = full.shape[2], full.shape[4]
    blocks = hd.shape[1]
    live = live_ref[0]

    @pl.loop(0, full.shape[0])
    def _(s):
        for j in range(bps):
            split_x[s * bps + j] = right3(full[s, 0, j], 0)
            split_g[s * bps + j] = right3(full[s, 1, j], 0)
            terms[s, 0, j] = jnp.zeros((blk, tokens), f32)
            terms[s, 1, j] = jnp.zeros((blk, tokens), f32)

    low_in, back_mid = right3(red[0], 0), right3(red[1], 0)
    for h in range(blocks):
        pre[h] = contract(left3(upr[:, h * blk : (h + 1) * blk], 0), low_in, 0, 0)
        grad[h] = contract(left3(dnl[h * blk : (h + 1) * blk, :], 1), back_mid, 1, 0)

    @pl.loop(0, pl.cdiv(live, unroll))
    def _(i):
        done = []
        for j in range(unroll):
            s = i * unroll + j
            keep = (s < live).astype(f32)
            m = mb_ref[s]
            up = contract(left3(upw[s] * keep, 0), split_x[m], 0, 0)
            dn = contract(left3(dnw[s] * keep, 1), split_g[m], 1, 0)
            done.append((hb_ref[s], up, dn))
        for h, up, dn in done:
            pre[h] += up
            grad[h] += dn

    scale = 0.7978845608028654
    for h in range(blocks):
        v = pre[h]
        th = jnp.tanh(scale * (v + 0.044715 * (v * v * v)))
        hidden = 0.5 * v * (1.0 + th)
        slope = 0.5 * (1.0 + th) + 0.5 * v * (1.0 - th * th) * (scale * (1.0 + 3 * 0.044715 * (v * v)))
        back = grad[h] * slope
        hd[0, h] = hidden
        hd[1, h] = back
        hs, bs = right3(hidden, 0), right3(back, 0)
        split_hd[0, h] = hs
        split_hd[1, h] = bs
        lm = contract(left3(dnl[h * blk : (h + 1) * blk, :], 0), hs, 0, 0)
        bi = contract(left3(upr[:, h * blk : (h + 1) * blk], 1), bs, 1, 0)
        if h == 0:
            low[0] = lm
            low[1] = bi
        else:
            low[0] += lm
            low[1] += bi

    @pl.loop(0, pl.cdiv(live, unroll))
    def _(i):
        done = []
        for j in range(unroll):
            s = i * unroll + j
            keep = (s < live).astype(f32)
            h = hb_ref[s]
            dn = contract(left3(dnw[s] * keep, 0), split_hd[0, h], 0, 0)
            up = contract(left3(upw[s] * keep, 1), split_hd[1, h], 1, 0)
            done.append((mb_ref[s], dn, up))
        for m, dn, up in done:
            terms[m // bps, 0, m % bps] += dn
            terms[m // bps, 1, m % bps] += up


def grads_kernel(
    dp, unroll, mb_ref, hb_ref, live_ref,
    full, peer_g, peer_x, hd, peer_hd,
    peer_own, red, peer_red, low, peer_low, summed, upl, dnr,
    res, ing, upg, uplg, uprg, dnlg, dnrg,
):
    slots, rows, blk = upg.shape
    bps = full.shape[2]
    blocks = hd.shape[1]
    d, t = lax.axis_index("dp"), lax.axis_index("tensor")
    live = live_ref[0]
    mine = pl.ds(pl.multiple_of(d * rows, rows), rows)
    peers = range(dp - 1)

    def cat(first, rest):
        return jnp.concatenate([first] + rest, axis=1)

    @pl.loop(0, slots // unroll)
    def _(i):
        for j in range(unroll):
            s = i * unroll + j
            keep = (s < live).astype(f32)
            m, h = mb_ref[s], hb_ref[s]
            q, r = m // bps, m % bps
            x = cat(full[q, 0, r, mine, :], [peer_x[k, q, r] for k in peers])
            back = cat(hd[1, h], [peer_hd[k, 1, h] for k in peers])
            upg[s] = dot3(x, back, 1, 1) * keep

    for j in range(bps):
        span = slice(j * blk, (j + 1) * blk)
        res[:, span] = (summed[0, j] + dot3(dnr[:, span], low[0], 0, 0)).T
        ing[:, span] = (summed[1, j] + dot3(upl[span, :], low[1], 1, 0)).T
    back_in = right3(cat(low[1], [peer_low[k, 1] for k in peers]), 1)
    n = uplg.shape[0]
    step = min(n, blk)
    for j in range(n // step):
        at = d * n + j * step
        q = at // blk
        inner = pl.ds(pl.multiple_of(at % blk, step), step)
        x = cat(full[t, 0, q, inner, :], [peer_own[k, q, inner, :] for k in peers])
        uplg[j * step : (j + 1) * step, :] = contract(left3(x, 1), back_in, 1, 1)
    n = uprg.shape[0]
    span = pl.ds(pl.multiple_of(d * n, n), n)
    left_in = left3(cat(red[0, span, :], [peer_red[k, 0, span, :] for k in peers]), 1)
    left_mid = left3(cat(low[0, span, :], [peer_low[k, 0, span, :] for k in peers]), 1)
    for h in range(blocks):
        back = cat(hd[1, h], [peer_hd[k, 1, h] for k in peers])
        uprg[:, h * blk : (h + 1) * blk] = contract(left_in, right3(back, 1), 1, 1)
    for j in range(bps):
        g = cat(full[t, 1, j], [peer_g[k, t, j] for k in peers])
        dnrg[:, j * blk : (j + 1) * blk] = contract(left_mid, right3(g, 1), 1, 1)
    back_mid = right3(cat(red[1], [peer_red[k, 1] for k in peers]), 1)
    n = dnlg.shape[0]
    step = min(n, blk)
    for j in range(n // step):
        at = d * n + j * step
        h = at // blk
        inner = pl.ds(pl.multiple_of(at % blk, step), step)
        hidden = cat(hd[0, h, inner, :], [peer_hd[k, 0, h, inner, :] for k in peers])
        dnlg[j * step : (j + 1) * step, :] = contract(left3(hidden, 1), back_mid, 1, 1)


def shards(
    dp, T,
    inputs, out_grad, up_weight, down_weight, up_left, up_right, down_left, down_right,
    model_block, hidden_block, live_slots,
):
    tokens, feats = inputs.shape
    slots, blk = up_weight.shape[0], up_weight.shape[1]
    width = up_right.shape[1]
    rank = up_left.shape[1]
    blocks = width // blk
    bps = feats // blk
    A = T // 4
    peers = dp - 1
    unroll = 4 if slots % 4 == 0 else 1
    DMA = pltpu.SemaphoreType.DMA
    sds = lambda *shape: jax.ShapeDtypeStruct(shape, f32)
    steps = 2 * A - 1
    sends = 4 + 2 + 2 + 2 * 3 * (steps - 1) + 2 * steps + peers * (2 * steps + 2 * steps + 2) + 2 * (T - 1)
    rows = max(8, rank // T)
    limit = 24 << 20
    full, peer_g, peer_own, red, peer_red = pl.pallas_call(
        functools.partial(gather_kernel, dp, T),
        out_shape=(
            sds(T, 2, bps, blk, tokens),
            sds(peers, T, bps, blk, tokens),
            sds(peers, bps, blk, tokens),
            sds(2, rank, tokens),
            sds(peers, 2, rank, tokens),
        ),
        in_specs=[VM] * 4,
        out_specs=[VM] * 5,
        scratch_shapes=[
            pltpu.VMEM((bps, blk, tokens), f32),
            pltpu.VMEM((bps, blk, tokens), f32),
            pltpu.VMEM((2, rank, tokens), f32),
            pltpu.VMEM((T, 2, rows, tokens), f32),
            DMA((sends,)), DMA((T, 2)), DMA((peers, T)), DMA((peers,)),
            DMA((T,)), DMA((T,)), DMA((peers,)),
        ],
        compiler_params=pltpu.CompilerParams(collective_id=0, has_side_effects=True, vmem_limit_bytes=limit),
    )(inputs, out_grad, up_left, down_right)
    terms, low, hd = pl.pallas_call(
        functools.partial(layer_kernel, unroll),
        out_shape=(
            sds(T, 2, bps, blk, tokens),
            sds(2, rank, tokens),
            sds(2, blocks, blk, tokens),
        ),
        in_specs=[SM] * 3 + [VM] * 6,
        out_specs=[VM] * 3,
        scratch_shapes=[
            pltpu.VMEM((T * bps, 3 * blk, tokens), jnp.bfloat16),
            pltpu.VMEM((T * bps, 3 * blk, tokens), jnp.bfloat16),
            pltpu.VMEM((2, blocks, 3 * blk, tokens), jnp.bfloat16),
            pltpu.VMEM((blocks, blk, tokens), f32),
            pltpu.VMEM((blocks, blk, tokens), f32),
        ],
        compiler_params=pltpu.CompilerParams(vmem_limit_bytes=limit),
    )(model_block, hidden_block, live_slots, full, red, up_weight, down_weight, up_right, down_left)
    sends = 2 * A + A + (A - 1) + peers * (3 + 4 * A) + 2 * (T - 1)
    summed, low_total, peer_hd, peer_low, peer_x, dng = pl.pallas_call(
        functools.partial(scatter_kernel, dp, T, unroll),
        out_shape=(
            sds(2, bps, blk, tokens),
            sds(2, rank, tokens),
            sds(peers, 2, blocks, blk, tokens),
            sds(peers, 2, rank, tokens),
            sds(peers, T, bps, blk // dp, tokens),
            sds(slots, blk // dp, blk),
        ),
        in_specs=[SM] * 3 + [VM] * 5,
        out_specs=[VM] * 6,
        scratch_shapes=[
            pltpu.VMEM((2 * A, 2, bps, blk, tokens), f32),
            pltpu.VMEM((A, 2, bps, blk, tokens), f32),
            pltpu.VMEM((A, 2, bps, blk, tokens), f32),
            pltpu.VMEM((A, 2, bps, blk, tokens), f32),
            pltpu.VMEM((A, 2, bps, blk, tokens), f32),
            pltpu.VMEM((T, 2, rows, tokens), f32),
            DMA((sends,)), DMA((2 * A,)), DMA((A,)), DMA((A,)), DMA((peers, 2)), DMA((peers, T)),
            DMA((T,)), DMA((T,)), DMA((peers,)),
        ],
        compiler_params=pltpu.CompilerParams(collective_id=1, has_side_effects=True, vmem_limit_bytes=limit),
    )(model_block, hidden_block, live_slots, terms, low, hd, full, peer_g)
    res, ing, upg, uplg, uprg, dnlg, dnrg = pl.pallas_call(
        functools.partial(grads_kernel, dp, unroll),
        out_shape=(
            sds(tokens, feats),
            sds(tokens, feats),
            sds(slots, blk // dp, blk),
            sds(feats // dp, rank),
            sds(rank // dp, width),
            sds(width // dp, rank),
            sds(rank // dp, feats),
        ),
        in_specs=[SM] * 3 + [VM] * 13,
        out_specs=[VM] * 7,
        compiler_params=pltpu.CompilerParams(vmem_limit_bytes=limit),
    )(
        model_block, hidden_block, live_slots,
        full, peer_g, peer_x, hd, peer_hd,
        peer_own, red, peer_red, low_total, peer_low, summed, up_left, down_right,
    )
    return res, ing, upg, dng, uplg, uprg, dnlg, dnrg


def solution(mesh):
    return jax.shard_map(
        functools.partial(shards, mesh.shape["dp"], mesh.shape["tensor"]),
        mesh=mesh,
        in_specs=(
            P("dp", "tensor"),
            P("dp", "tensor"),
            P("tensor", None, None),
            P("tensor", None, None),
            P("tensor", None),
            P(None, "tensor"),
            P("tensor", None),
            P(None, "tensor"),
            P("tensor"),
            P("tensor"),
            P("tensor"),
        ),
        out_specs=(
            P("dp", "tensor"),
            P("dp", "tensor"),
            P("tensor", "dp", None),
            P("tensor", "dp", None),
            P(("tensor", "dp"), None),
            P("dp", "tensor"),
            P(("tensor", "dp"), None),
            P("dp", "tensor"),
        ),
        check_vma=False,
    )
```

```python
import functools

import jax
import jax.numpy as jnp
from jax import lax
from jax.experimental import pallas as pl
from jax.experimental.pallas import tpu as pltpu
from jax.sharding import PartitionSpec as P

MESH = pl.DeviceIdType.MESH
VM = pl.BlockSpec(memory_space=pltpu.VMEM)
HB = pl.BlockSpec(memory_space=pltpu.HBM)
SM = pl.BlockSpec(memory_space=pltpu.SMEM)
f32 = jnp.float32


def halves(v):
    hi = v.astype(jnp.bfloat16)
    lo = (v - hi.astype(f32)).astype(jnp.bfloat16)
    return hi, lo


def left3(v, axis):
    hi, lo = halves(v)
    return jnp.concatenate([hi, hi, lo], axis=axis)


def right3(v, axis):
    hi, lo = halves(v)
    return jnp.concatenate([hi, lo, hi], axis=axis)


def contract(a, b, da, db):
    return lax.dot_general(a, b, (((da,), (db,)), ((), ())), preferred_element_type=f32)


def dot3(a, b, da, db):
    return contract(left3(a, da), right3(b, db), da, db)


def flip(a, k, size):
    out, bit = 0, 1
    while bit < size:
        out = out + (((a // bit) % 2 + (k // bit) % 2) % 2) * bit
        bit *= 2
    return out


class Copies:
    def __init__(self, sems):
        self.sems, self.count, self.made = sems, 0, []

    def send(self, src, dst, recv, where, cond=None):
        sem = self.sems.at[self.count]
        self.count += 1
        copy = pltpu.make_async_remote_copy(
            src_ref=src, dst_ref=dst, send_sem=sem, recv_sem=recv, device_id=where, device_id_type=MESH
        )
        if cond is None:
            copy.start()
        else:
            pl.when(cond)(copy.start)
        self.made.append((copy, cond))

    def drain(self):
        for copy, cond in self.made:
            if cond is None:
                copy.wait_send()
            else:
                pl.when(cond)(copy.wait_send)


def arrived(ref, recv, where, cond=None):
    copy = pltpu.make_async_remote_copy(
        src_ref=ref, dst_ref=ref, send_sem=recv, recv_sem=recv, device_id=where, device_id_type=MESH
    )
    if cond is None:
        copy.wait_recv()
    else:
        pl.when(cond)(copy.wait_recv)


def line_steps(a, A):
    out = [(a, 0, None)]
    for k in range(1, A):
        out.append(((a + A - k) % A, -1, a >= k))
        out.append(((a + k) % A, 1, a + k < A))
    return out


def greet(d, t, dp, T):
    barrier = pltpu.get_barrier_semaphore()
    for k in range(1, T):
        pl.semaphore_signal(barrier, inc=1, device_id=(d, lax.rem(t + k, T)), device_id_type=MESH)
    for k in range(1, dp):
        pl.semaphore_signal(barrier, inc=1, device_id=(lax.rem(d + k, dp), t), device_id_type=MESH)
    pl.semaphore_wait(barrier, T - 1 + dp - 1)


class Total:
    def __init__(self, out, d, t, T, part, inbox, copies, in_sem, out_sem):
        self.out, self.d, self.t, self.T, self.part, self.inbox = out, d, t, T, part, inbox
        self.copies, self.in_sem, self.out_sem = copies, in_sem, out_sem
        rank = part.shape[1]
        self.rows = max(8, rank // T)
        self.count = rank // self.rows

    def cond(self, j):
        return None if self.count >= self.T else j < self.count

    def piece(self, ref, j):
        return ref.at[:, pl.ds(pl.multiple_of(j * self.rows, self.rows), self.rows), :]

    def begin(self):
        for k in range(1, self.T):
            j = lax.rem(self.t + k, self.T)
            cond = self.cond(j)
            at = j if cond is None else lax.rem(j, self.count)
            self.copies.send(
                self.piece(self.part, at), self.inbox.at[self.T - k], self.in_sem.at[self.T - k], (self.d, j), cond
            )

    def reduce(self):
        cond = self.cond(self.t)
        at = self.t if cond is None else lax.rem(self.t, self.count)

        def work():
            span = pl.ds(pl.multiple_of(at * self.rows, self.rows), self.rows)
            total = self.part[:, span, :]
            for k in range(1, self.T):
                arrived(self.inbox.at[k], self.in_sem.at[k], (self.d, self.t))
                total = total + self.inbox[k]
            self.out[:, span, :] = total

        if cond is None:
            work()
        else:
            pl.when(cond)(work)
        for k in range(1, self.T):
            j = lax.rem(self.t + k, self.T)
            self.copies.send(
                self.piece(self.out, at), self.piece(self.out, at), self.out_sem.at[self.T - k], (self.d, j), cond
            )

    def finish(self):
        for k in range(1, self.T):
            j = lax.rem(self.t + k, self.T)
            cond = self.cond(j)
            at = j if cond is None else lax.rem(j, self.count)
            wait = functools.partial(arrived, self.piece(self.out, at), self.out_sem.at[k], (self.d, j))
            if cond is None:
                wait()
            else:
                pl.when(cond)(wait)


def power(r):
    return r > 0 and r & (r - 1) == 0


def mine(r):
    return r == 0 or power(r)


def pair_of(m, g, levels):
    j = 0
    for k in range(levels):
        bit = 1 << k
        j = j + (k + 1) * (((m // bit) % 2 + (g // bit) % 2) % 2)
    return j


def layer_kernel(
    dp, T, live_ref, mb_any, hb_any, inp_any, og_any, upw_ref, dnw_ref, upl_any, upr_any, dnl_any, dnr_any,
    full, peer_g, peer_x, hd, peer_hd, peer_own, red, peer_red, low, peer_low, summed, dpair, upl_ref, dnr_ref, ps,
    mb_ref, hb_ref, inp_ref, og_ref, upr, dnl, small_sem,
    wup, wdn, wsem, idx_v, idx_s, isem, part, inbox, lpart, linbox, slope, split_x, split_hd,
    terms, core_box, stage, side_box, acc, line_box,
    send_sem, full_sem, pg_sem, px_sem, po_sem, in_sem, out_sem, pr_sem,
    lin_sem, lout_sem, pl_sem, hd_sem, core_sem, side_sem, line_sem,
):
    d, t = lax.axis_index("dp"), lax.axis_index("tensor")
    c, b, a = t % 2, (t // 2) % 2, t // 4
    A = T // 4
    q = t % A
    slots, blk = upw_ref.shape[0], upw_ref.shape[1]
    bps, n = full.shape[2], full.shape[4]
    blocks = hd.shape[1]
    rank = red.shape[1]
    half = dpair.shape[1]
    total_blocks = T * bps
    levels = total_blocks.bit_length() - 1
    low_levels = blocks.bit_length() - 1
    J = levels + 1
    U = 2
    peers = dp - 1
    core, side = (d, a * 4 + b * 2 + 1 - c), (d, a * 4 + (1 - b) * 2 + c)
    before, after = (d, (t + T - 4) % T), (d, (t + 4) % T)
    copies = Copies(send_sem)

    pairs = (
        (inp_any, inp_ref), (og_any, og_ref), (upl_any, upl_ref), (dnr_any, dnr_ref),
        (mb_any, mb_ref), (hb_any, hb_ref), (upr_any, upr), (dnl_any, dnl),
    )
    loads = [pltpu.make_async_copy(src, dst, small_sem.at[i]) for i, (src, dst) in enumerate(pairs)]
    for load in loads:
        load.start()
    load_up = pltpu.make_async_copy(upw_ref, wup.at[pl.ds(0, slots)], wsem.at[0])
    load_dn = pltpu.make_async_copy(dnw_ref, wdn.at[pl.ds(0, slots)], wsem.at[1])
    load_up.start()
    load_dn.start()
    loads[0].wait()
    loads[1].wait()
    for j in range(bps):
        full[t, 0, j] = inp_ref[:, j * blk : (j + 1) * blk].T
        full[t, 1, j] = og_ref[:, j * blk : (j + 1) * blk].T
    greet(d, t, dp, T)

    def other(k):
        return lax.rem(d + k + 1, dp)

    def send(i, s, where, cond=None):
        copies.send(full.at[s, i], full.at[s, i], full_sem.at[s, i], where, cond)

    def got(i, s, where, cond=None):
        arrived(full.at[s, i], full_sem.at[s, i], where, cond)

    def across(i, s, cond=None):
        for k in range(peers):
            o = other(k)
            if i:
                copies.send(full.at[s, 1], peer_g.at[k, s], pg_sem.at[k, s], (o, t), cond)
            else:
                rows = pl.ds(pl.multiple_of(o * half, half), half)
                copies.send(full.at[s, 0, :, rows, :], peer_x.at[k, s], px_sem.at[k, s], (o, t), cond)

    own_rows = peer_own.shape[1]

    def first(i):
        send(i, t, before, a >= 1)
        send(i, t, after, a + 1 < A)
        send(i, t, side)
        send(i, t, core)
        across(i, t)

    mine_list = [(t, None)]

    def relay(i, k):
        if k == 0:
            steps = [(a, 0, None)]
        else:
            steps = [((a + A - k) % A, -1, a >= k), ((a + k) % A, 1, a + k < A)]
        for row, way, here in steps:
            s = row * 4 + b * 2 + c
            if way != 0:
                got(i, s, side, here)
                if k < A - 1:
                    onward = (here & (a + 1 < A)) if way < 0 else (here & (a >= 1))
                    send(i, s, after if way < 0 else before, onward)
                send(i, s, side, here)
                send(i, s, core, here)
                across(i, s, here)
                if i == 0:
                    mine_list.append((s, here))
        for row, way, here in steps:
            s = row * 4 + (1 - b) * 2 + c
            got(i, s, side, here)
            send(i, s, core, here)
            across(i, s, here)
            if i == 0:
                mine_list.append((s, here))

    first(0)
    loads[2].wait()
    loads[3].wait()
    part[0] = dot3(upl_ref[...], full[t, 0].reshape(bps * blk, n), 0, 0)
    part[1] = dot3(dnr_ref[...], full[t, 1].reshape(bps * blk, n), 1, 0)
    total = Total(red, d, t, T, part, inbox, copies, in_sem, out_sem)
    total.begin()
    first(1)
    for k in range(peers):
        o = other(k)
        at = o * own_rows * peer_own.shape[2]
        for j in range(own_rows):
            pos = at + j * peer_own.shape[2]
            inner = pl.ds(pl.multiple_of(pos % blk, peer_own.shape[2]), peer_own.shape[2])
            copies.send(full.at[t, 0, pos // blk, inner, :], peer_own.at[k, j], po_sem.at[k, j], (o, t))

    for load in loads[4:]:
        load.wait()

    @pl.loop(0, slots)
    def _(s):
        h = hb_ref[s]
        g = (t * blocks + h) % total_blocks
        ps[s] = jnp.where(s < live_ref[0], h * J + pair_of(mb_ref[s], g, levels), -1)

    lane = lax.broadcasted_iota(jnp.int32, (8, 128), 1)
    row_of = lax.fori_loop(0, slots, lambda s, v: jnp.where(lane == s, ps[s], v), jnp.full((8, 128), -2, jnp.int32))

    def link(s, v):
        prev, last = v
        p = ps[s]
        prev = jnp.where((lane > s) & (row_of == p), s, prev)
        last = jnp.where(lane == p, s, last)
        return prev, last

    none = jnp.full((8, 128), slots, jnp.int32)
    prev, last = lax.fori_loop(0, slots, link, (none, none))
    idx_v[0] = prev
    idx_v[1] = last
    to_scalar = pltpu.make_async_copy(idx_v, idx_s, isem.at[0])
    to_scalar.start()
    relay(0, 0)
    total.reduce()
    to_scalar.wait()
    load_up.wait()
    load_dn.wait()
    wup[slots] = jnp.zeros((blk, blk), f32)
    wdn[slots] = jnp.zeros((blk, blk), f32)
    relay(0, 1)

    @pl.loop(0, slots)
    def _(s):
        before_it = idx_s[0, 0, s]
        wup[s] = wup[s] + wup[before_it]
        wdn[s] = wdn[s] + wdn[before_it]

    for k in range(2, A):
        relay(0, k)
    total.finish()
    for k in range(peers):
        copies.send(red.at[c], peer_red.at[k, c], pr_sem.at[k, c], (other(k), t))
    relay(1, 0)

    def from_core(i):
        for k in range(2 * A):
            got(i, k * 2 + 1 - c, core)

    far = [1 << k for k in range(levels - low_levels)]

    def weight(w, h, j):
        return w[idx_s[1, 0, h * J + j]]

    def split_in(i):
        @pl.loop(0, blocks)
        def _(m):
            split_x[m] = right3(full[q * 4 + m // bps, i, m % bps], 0)

    def gather_up(i, h, w, axis, start):
        v = start + contract(left3(weight(w, h, 0), axis), split_x[h], axis, 0)
        for k in range(low_levels):
            v = v + contract(left3(weight(w, h, 1 + k), axis), split_x[flip(h, 1 << k, blocks)], axis, 0)
        for k, r in enumerate(far):
            x = right3(full[flip(q, r, A) * 4 + h // bps, i, h % bps], 0)
            v = v + contract(left3(weight(w, h, 1 + low_levels + k), axis), x, axis, 0)
        return v

    def span(h):
        return pl.ds(pl.multiple_of(h * blk, blk), blk)

    from_core(0)
    split_in(0)
    low_in = right3(red[0], 0)
    scale = 0.7978845608028654
    for k in range(1, A):
        relay(1, k)

    @pl.loop(0, blocks // U)
    def _(i):
        for j in range(U):
            h = i * U + j
            v = gather_up(0, h, wup, 0, contract(left3(upr[:, span(h)], 0), low_in, 0, 0))
            th = jnp.tanh(scale * (v + 0.044715 * (v * v * v)))
            hidden = 0.5 * v * (1.0 + th)
            slope[h] = 0.5 * (1.0 + th) + 0.5 * v * (1.0 - th * th) * (scale * (1.0 + 3 * 0.044715 * (v * v)))
            hd[0, h] = hidden
            split_hd[h] = right3(hidden, 0)

    def send_hidden(p):
        for k in range(peers):
            for j in range(2):
                rows = pl.ds(j * (blocks // 2), blocks // 2)
                copies.send(hd.at[p, rows], peer_hd.at[k, p, rows], hd_sem.at[k, p, j], (other(k), t))

    def spread_out(p, w, axis):
        for k, r in enumerate(far):
            row = flip(q, r, A)

            @pl.loop(0, blocks // U)
            def _(i):
                for j in range(U):
                    h = i * U + j
                    u = h // bps
                    terms[row, p, u % 2, u // 2, h % bps] = contract(
                        left3(weight(w, h, 1 + low_levels + k), axis), split_hd[h], axis, 0
                    )

        @pl.loop(0, blocks // U)
        def _(i):
            for j in range(U):
                m = i * U + j
                u = m // bps
                v = contract(left3(weight(w, m, 0), axis), split_hd[m], axis, 0)
                for k in range(low_levels):
                    h = flip(m, 1 << k, blocks)
                    v = v + contract(left3(weight(w, h, 1 + k), axis), split_hd[h], axis, 0)
                terms[q, p, u % 2, u // 2, m % bps] = v

        for r in order:
            row = flip(q, r, A)
            if mine(r):
                copies.send(terms.at[row, p, 1 - c], core_box.at[row, p], core_sem.at[row, p], core)

    order = []
    for r in range(A):
        if r % 4 < 2:
            order += [r + 2, r] if A > 2 else [r]

    def to_side(p):
        for r in order:
            row = flip(q, r, A)
            theirs = mine(r ^ 1)
            if theirs:
                arrived(core_box.at[row, p], core_sem.at[row, p], core)
            if mine(r) and not theirs:
                src = terms.at[row, p, c, 1 - b]
            elif theirs and not mine(r):
                src = core_box.at[row, p, 1 - b]
            else:
                src = stage.at[row, p]
                if theirs:
                    stage[row, p] = terms[row, p, c, 1 - b] + core_box[row, p, 1 - b]
                else:
                    stage[row, p] = jnp.zeros(stage.shape[2:], f32)
            copies.send(src, side_box.at[row, p], side_sem.at[row, p], side)

    def to_line(p):
        for r in order:
            row = flip(q, r, A)
            arrived(side_box.at[row, p], side_sem.at[row, p], side)
            v = side_box[row, p]
            if mine(r):
                v = v + terms[row, p, c, b]
            if mine(r ^ 1):
                v = v + core_box[row, p, b]
            acc[row, p] = v
            k = flip(row, a, A)
            copies.send(
                acc.at[row, p], line_box.at[k, p], line_sem.at[k, p], (d, row * 4 + b * 2 + c), row != a
            )

    send_hidden(0)
    spread_out(0, wdn, 0)
    to_side(0)
    lpart[0] = jnp.zeros((rank, n), f32)
    lpart[1] = jnp.zeros((rank, n), f32)
    from_core(1)
    split_in(1)
    back_mid = right3(red[1], 0)

    @pl.loop(0, blocks // U)
    def _(i):
        for j in range(U):
            h = i * U + j
            lpart[0] += contract(left3(dnl[span(h), :], 0), split_hd[h], 0, 0)
            v = gather_up(1, h, wdn, 1, contract(left3(dnl[span(h), :], 1), back_mid, 1, 0))
            back = v * slope[h]
            hd[1, h] = back
            bs = right3(back, 0)
            split_hd[h] = bs
            lpart[1] += contract(left3(upr[:, span(h)], 1), bs, 1, 0)

    send_hidden(1)
    low_total = Total(low, d, t, T, lpart, linbox, copies, lin_sem, lout_sem)
    low_total.begin()
    spread_out(1, wup, 1)
    to_side(1)
    to_line(0)
    low_total.reduce()
    for s, here in mine_list:
        for k in range(peers):
            arrived(peer_x.at[k, s], px_sem.at[k, s], core, here)
            copies.send(peer_x.at[k, s], peer_x.at[k, s], px_sem.at[k, s], core, here)
    for k in range(peers):
        arrived(peer_red.at[k, c], pr_sem.at[k, c], core)
        copies.send(peer_red.at[k, c], peer_red.at[k, c], pr_sem.at[k, c], core)
    low_total.finish()
    for k in range(peers):
        copies.send(low.at[c], peer_low.at[k, c], pl_sem.at[k, c], (other(k), t))
    for s, here in mine_list:
        for k in range(peers):
            arrived(peer_g.at[k, s], pg_sem.at[k, s], core, here)
            copies.send(peer_g.at[k, s], peer_g.at[k, s], pg_sem.at[k, s], core, here)
    to_line(1)
    for k in range(peers):
        for i in range(2 * A):
            s = i * 2 + 1 - c
            arrived(peer_g.at[k, s], pg_sem.at[k, s], core)
            arrived(peer_x.at[k, s], px_sem.at[k, s], core)
        for j in range(2):
            rows = pl.ds(j * (blocks // 2), blocks // 2)
            arrived(peer_hd.at[k, 0, rows], hd_sem.at[k, 0, j], core)
    here_rows = pl.ds(pl.multiple_of(d * half, half), half)

    def hidden_rows(h):
        rows = [hd[0, h, here_rows, :]] + [peer_hd[k, 0, h, here_rows, :] for k in range(peers)]
        return left3(jnp.concatenate(rows, axis=1), 1)

    def grad_cols(plane, m):
        s = plane * 4 + m // bps
        g = [full[s, 1, m % bps]] + [peer_g[k, s, m % bps] for k in range(peers)]
        return right3(jnp.concatenate(g, axis=1), 1)

    @pl.loop(0, blocks)
    def _(m):
        g = grad_cols(q, m)
        left = jnp.concatenate(
            [hidden_rows(m)] + [hidden_rows(flip(m, 1 << k, blocks)) for k in range(low_levels)], axis=0
        )
        v = contract(left, g, 1, 1)
        dpair[m * J] = v[:half]
        for k in range(low_levels):
            dpair[flip(m, 1 << k, blocks) * J + 1 + k] = v[(k + 1) * half : (k + 2) * half]
        for k, r in enumerate(far):
            dpair[m * J + 1 + low_levels + k] = contract(hidden_rows(m), grad_cols(flip(q, r, A), m), 1, 1)

    for p in range(2):
        v = acc[a, p]
        for k in range(1, A):
            arrived(line_box.at[k, p], line_sem.at[k, p], core)
            v = v + line_box[k, p]
        summed[p] = v
    for k in range(peers):
        arrived(peer_low.at[k, c], pl_sem.at[k, c], core)
        copies.send(peer_low.at[k, c], peer_low.at[k, c], pl_sem.at[k, c], core)
    for k in range(peers):
        for j in range(2):
            rows = pl.ds(j * (blocks // 2), blocks // 2)
            arrived(peer_hd.at[k, 1, rows], hd_sem.at[k, 1, j], core)
        for j in range(own_rows):
            arrived(peer_own.at[k, j], po_sem.at[k, j], core)
        arrived(peer_red.at[k, 1 - c], pr_sem.at[k, 1 - c], core)
        arrived(peer_low.at[k, 1 - c], pl_sem.at[k, 1 - c], core)
    copies.drain()


def grads_kernel(
    dp, full, peer_g, peer_x, hd, peer_hd,
    peer_own, red, peer_red, low, peer_low, summed, dpair, upl, dnr, ps,
    res, ing, upg, dng, uplg, uprg, dnlg, dnrg, upair,
):
    slots, half, blk = upg.shape
    T, bps = full.shape[0], full.shape[2]
    A = T // 4
    blocks = hd.shape[1]
    total_blocks = T * bps
    levels = total_blocks.bit_length() - 1
    low_levels = blocks.bit_length() - 1
    J = levels + 1
    far = [1 << k for k in range(levels - low_levels)]
    d, t = lax.axis_index("dp"), lax.axis_index("tensor")
    q = t % A
    here_rows = pl.ds(pl.multiple_of(d * half, half), half)
    peers = range(dp - 1)

    def cat(first, rest):
        return jnp.concatenate([first] + rest, axis=1)

    def rows(plane, m):
        s = plane * 4 + m // bps
        return left3(cat(full[s, 0, m % bps, here_rows, :], [peer_x[k, s, m % bps] for k in peers]), 1)

    for h in range(blocks):
        back = right3(cat(hd[1, h], [peer_hd[k, 1, h] for k in peers]), 1)
        left = [rows(q, h)] + [rows(q, h ^ (1 << k)) for k in range(low_levels)]
        left += [rows(flip(q, r, A), h) for r in far]
        v = contract(jnp.concatenate(left, axis=0), back, 1, 1)
        for j in range(J):
            upair[h * J + j] = v[j * half : (j + 1) * half]

    unroll = 4 if slots % 4 == 0 else 1

    @pl.loop(0, slots // unroll)
    def _(i):
        for j in range(unroll):
            s = i * unroll + j
            p = ps[s]
            keep = (p >= 0).astype(f32)
            p = jnp.maximum(p, 0)
            upg[s] = upair[p] * keep
            dng[s] = dpair[p] * keep

    for j in range(bps):
        span = slice(j * blk, (j + 1) * blk)
        res[:, span] = (summed[0, j] + dot3(dnr[:, span], low[0], 0, 0)).T
        ing[:, span] = (summed[1, j] + dot3(upl[span, :], low[1], 1, 0)).T
    back_in = right3(cat(low[1], [peer_low[k, 1] for k in peers]), 1)
    n = uplg.shape[0]
    step = min(n, blk)
    for j in range(n // step):
        at = d * n + j * step
        inner = pl.ds(pl.multiple_of(at % blk, step), step)
        x = cat(full[t, 0, at // blk, inner, :], [peer_own[k, j] for k in peers])
        uplg[j * step : (j + 1) * step, :] = contract(left3(x, 1), back_in, 1, 1)
    n = uprg.shape[0]
    span = pl.ds(pl.multiple_of(d * n, n), n)
    left_in = left3(cat(red[0, span, :], [peer_red[k, 0, span, :] for k in peers]), 1)
    left_mid = left3(cat(low[0, span, :], [peer_low[k, 0, span, :] for k in peers]), 1)
    for h in range(blocks):
        back = cat(hd[1, h], [peer_hd[k, 1, h] for k in peers])
        uprg[:, h * blk : (h + 1) * blk] = contract(left_in, right3(back, 1), 1, 1)
    for j in range(bps):
        g = cat(full[t, 1, j], [peer_g[k, t, j] for k in peers])
        dnrg[:, j * blk : (j + 1) * blk] = contract(left_mid, right3(g, 1), 1, 1)
    back_mid = right3(cat(red[1], [peer_red[k, 1] for k in peers]), 1)
    n = dnlg.shape[0]
    step = min(n, blk)
    for j in range(n // step):
        at = d * n + j * step
        inner = pl.ds(pl.multiple_of(at % blk, step), step)
        hidden = cat(hd[0, at // blk, inner, :], [peer_hd[k, 0, at // blk, inner, :] for k in peers])
        dnlg[j * step : (j + 1) * step, :] = contract(left3(hidden, 1), back_mid, 1, 1)


def shards(
    dp, T,
    inputs, out_grad, up_weight, down_weight, up_left, up_right, down_left, down_right,
    model_block, hidden_block, live_slots,
):
    tokens, feats = inputs.shape
    slots, blk = up_weight.shape[0], up_weight.shape[1]
    width = up_right.shape[1]
    rank = up_left.shape[1]
    blocks = width // blk
    bps = feats // blk
    A = T // 4
    peers = dp - 1
    half = blk // dp
    pairs = blocks * (T * bps).bit_length()
    own = feats // dp
    own_step = min(own, blk)
    own_rows = own // own_step
    DMA = pltpu.SemaphoreType.DMA
    sds = lambda *shape: jax.ShapeDtypeStruct(shape, f32)
    vmem = lambda *shape: pltpu.VMEM(shape, f32)
    bf16 = jnp.bfloat16
    sends = 4 * T + 8 * A * (6 + 2 * peers) + 8 * A + 64 + peers * (8 * A + 16)
    rows = max(8, rank // T)
    outs = pl.pallas_call(
        functools.partial(layer_kernel, dp, T),
        out_shape=(
            sds(T, 2, bps, blk, tokens),
            sds(peers, T, bps, blk, tokens),
            sds(peers, T, bps, half, tokens),
            sds(2, blocks, blk, tokens),
            sds(peers, 2, blocks, blk, tokens),
            sds(peers, own_rows, own_step, tokens),
            sds(2, rank, tokens),
            sds(peers, 2, rank, tokens),
            sds(2, rank, tokens),
            sds(peers, 2, rank, tokens),
            sds(2, bps, blk, tokens),
            sds(pairs, half, blk),
            sds(feats, rank),
            sds(rank, feats),
            jax.ShapeDtypeStruct((slots,), jnp.int32),
        ),
        in_specs=[SM] + [HB] * 10,
        out_specs=[VM] * 14 + [SM],
        scratch_shapes=[
            pltpu.SMEM((slots,), jnp.int32), pltpu.SMEM((slots,), jnp.int32),
            vmem(tokens, feats), vmem(tokens, feats), vmem(rank, width), vmem(width, rank), DMA((8,)),
            vmem(slots + 1, blk, blk), vmem(slots + 1, blk, blk), DMA((2,)),
            pltpu.VMEM((2, 8, 128), jnp.int32), pltpu.SMEM((2, 8, 128), jnp.int32),
            DMA((1,)),
            vmem(2, rank, tokens), vmem(T, 2, rows, tokens),
            vmem(2, rank, tokens), vmem(T, 2, rows, tokens),
            vmem(blocks, blk, tokens),
            pltpu.VMEM((blocks, 3 * blk, tokens), bf16),
            pltpu.VMEM((blocks, 3 * blk, tokens), bf16),
            vmem(A, 2, 2, 2, bps, blk, tokens),
            vmem(A, 2, 2, bps, blk, tokens),
            vmem(A, 2, bps, blk, tokens),
            vmem(A, 2, bps, blk, tokens),
            vmem(A, 2, bps, blk, tokens),
            vmem(A, 2, bps, blk, tokens),
            DMA((sends,)), DMA((T, 2)), DMA((peers, T)), DMA((peers, T)), DMA((peers, own_rows)),
            DMA((T,)), DMA((T,)), DMA((peers, 2)),
            DMA((T,)), DMA((T,)), DMA((peers, 2)), DMA((peers, 2, 2)),
            DMA((A, 2)), DMA((A, 2)), DMA((A, 2)),
        ],
        compiler_params=pltpu.CompilerParams(collective_id=0, has_side_effects=True, vmem_limit_bytes=36 << 20),
    )(
        live_slots,
        *(
            pltpu.with_memory_space_constraint(v, pltpu.HBM)
            for v in (
                model_block, hidden_block, inputs, out_grad, up_weight, down_weight,
                up_left, up_right, down_left, down_right,
            )
        )
    )
    return pl.pallas_call(
        functools.partial(grads_kernel, dp),
        out_shape=(
            sds(tokens, feats),
            sds(tokens, feats),
            sds(slots, half, blk),
            sds(slots, half, blk),
            sds(feats // dp, rank),
            sds(rank // dp, width),
            sds(width // dp, rank),
            sds(rank // dp, feats),
        ),
        in_specs=[VM] * 14 + [SM],
        out_specs=[VM] * 8,
        scratch_shapes=[vmem(pairs, half, blk)],
        compiler_params=pltpu.CompilerParams(vmem_limit_bytes=24 << 20),
    )(*outs)


def solution(mesh):
    return jax.shard_map(
        functools.partial(shards, mesh.shape["dp"], mesh.shape["tensor"]),
        mesh=mesh,
        in_specs=(
            P("dp", "tensor"),
            P("dp", "tensor"),
            P("tensor", None, None),
            P("tensor", None, None),
            P("tensor", None),
            P(None, "tensor"),
            P("tensor", None),
            P(None, "tensor"),
            P("tensor"),
            P("tensor"),
            P("tensor"),
        ),
        out_specs=(
            P("dp", "tensor"),
            P("dp", "tensor"),
            P("tensor", "dp", None),
            P("tensor", "dp", None),
            P(("tensor", "dp"), None),
            P("dp", "tensor"),
            P(("tensor", "dp"), None),
            P("dp", "tensor"),
        ),
        check_vma=False,
    )
```

```python
import functools

import jax
import jax.numpy as jnp
from jax import lax
from jax.experimental import pallas as pl
from jax.experimental.pallas import tpu as pltpu
from jax.sharding import PartitionSpec as P

MESH = pl.DeviceIdType.MESH
VM = pl.BlockSpec(memory_space=pltpu.VMEM)
HB = pl.BlockSpec(memory_space=pltpu.HBM)
SM = pl.BlockSpec(memory_space=pltpu.SMEM)
f32 = jnp.float32


def halves(v):
    hi = v.astype(jnp.bfloat16)
    lo = (v - hi.astype(f32)).astype(jnp.bfloat16)
    return hi, lo


def left3(v, axis):
    hi, lo = halves(v)
    return jnp.concatenate([hi, hi, lo], axis=axis)


def right3(v, axis):
    hi, lo = halves(v)
    return jnp.concatenate([hi, lo, hi], axis=axis)


def contract(a, b, da, db):
    return lax.dot_general(a, b, (((da,), (db,)), ((), ())), preferred_element_type=f32)


def dot3(a, b, da, db):
    return contract(left3(a, da), right3(b, db), da, db)


def flip(a, k, size):
    out, bit = 0, 1
    while bit < size:
        out = out + (((a // bit) % 2 + (k // bit) % 2) % 2) * bit
        bit *= 2
    return out


class Copies:
    def __init__(self, sems):
        self.sems, self.count, self.made = sems, 0, []

    def send(self, src, dst, recv, where, cond=None):
        sem = self.sems.at[self.count]
        self.count += 1
        copy = pltpu.make_async_remote_copy(
            src_ref=src, dst_ref=dst, send_sem=sem, recv_sem=recv, device_id=where, device_id_type=MESH
        )
        if cond is None:
            copy.start()
        else:
            pl.when(cond)(copy.start)
        self.made.append((copy, cond))

    def drain(self):
        for copy, cond in self.made:
            if cond is None:
                copy.wait_send()
            else:
                pl.when(cond)(copy.wait_send)


def arrived(ref, recv, where, cond=None):
    copy = pltpu.make_async_remote_copy(
        src_ref=ref, dst_ref=ref, send_sem=recv, recv_sem=recv, device_id=where, device_id_type=MESH
    )
    if cond is None:
        copy.wait_recv()
    else:
        pl.when(cond)(copy.wait_recv)


def line_steps(a, A):
    out = [(a, 0, None)]
    for k in range(1, A):
        out.append(((a + A - k) % A, -1, a >= k))
        out.append(((a + k) % A, 1, a + k < A))
    return out


def greet(d, t, dp, T):
    barrier = pltpu.get_barrier_semaphore()
    for k in range(1, T):
        pl.semaphore_signal(barrier, inc=1, device_id=(d, lax.rem(t + k, T)), device_id_type=MESH)
    for k in range(1, dp):
        pl.semaphore_signal(barrier, inc=1, device_id=(lax.rem(d + k, dp), t), device_id_type=MESH)
    pl.semaphore_wait(barrier, T - 1 + dp - 1)


class Total:
    def __init__(self, out, peer_out, dp, d, t, T, part, mid, core_in, side_in, line_in, copies, sems):
        self.out, self.peer_out, self.dp, self.d, self.t, self.A = out, peer_out, dp, d, t, T // 4
        self.part, self.mid, self.core_in, self.side_in, self.line_in = part, mid, core_in, side_in, line_in
        self.copies = copies
        self.one_sem, self.line_sem, self.peer_sem = sems
        self.c, self.b, self.a = t % 2, (t // 2) % 2, t // 4
        self.core, self.side = (d, self.place(self.a, 0, 1)), (d, self.place(self.a, 1, 0))

    def place(self, row, b, c):
        return row * 4 + (self.b + b) % 2 * 2 + (self.c + c) % 2

    def to_core(self):
        self.copies.send(self.part.at[1 - self.c], self.core_in, self.one_sem.at[0], self.core)

    def to_side(self):
        arrived(self.core_in, self.one_sem.at[0], self.core)
        self.mid[0] = self.part[self.c] + self.core_in[...]
        self.copies.send(self.mid.at[0], self.side_in, self.one_sem.at[1], self.side)

    def to_line(self):
        arrived(self.side_in, self.one_sem.at[1], self.side)
        self.mid[1] = self.mid[0] + self.side_in[...]
        for k in range(1, self.A):
            row = (self.a + k) % self.A
            self.copies.send(
                self.mid.at[1], self.line_in.at[self.A - k], self.line_sem.at[self.A - k],
                (self.d, self.place(row, 0, 0)),
            )

    def reduce(self):
        total = self.mid[1]
        for k in range(1, self.A):
            arrived(self.line_in.at[k], self.line_sem.at[k], self.core)
            total = total + self.line_in[k]
        self.out[self.c] = total
        whole = self.out.at[self.c]
        self.copies.send(whole, whole, self.one_sem.at[2], self.core)
        for p in range(self.dp - 1):
            self.copies.send(
                whole, self.peer_out.at[p, self.c], self.peer_sem.at[p, self.c],
                (lax.rem(self.d + p + 1, self.dp), self.t),
            )

    def finish(self):
        arrived(self.out.at[1 - self.c], self.one_sem.at[2], self.core)

    def pass_peers(self):
        for p in range(self.dp - 1):
            box = self.peer_out.at[p, self.c]
            arrived(box, self.peer_sem.at[p, self.c], self.core)
            self.copies.send(box, box, self.peer_sem.at[p, self.c], self.core)

    def finish_peers(self):
        for p in range(self.dp - 1):
            arrived(self.peer_out.at[p, 1 - self.c], self.peer_sem.at[p, 1 - self.c], self.core)


def power(r):
    return r > 0 and r & (r - 1) == 0


def mine(r):
    return r == 0 or power(r)


def pair_of(m, g, levels):
    diff = m ^ g
    return sum((diff >= (1 << k)).astype(jnp.int32) for k in range(levels))


def by_distance(a, A):
    table = [sorted(range(A), key=lambda r: (abs(r - v), r)) for v in range(A)]
    rows = []
    for i in range(A):
        row = table[0][i]
        for v in range(1, A):
            row = jnp.where(a == v, table[v][i], row)
        rows.append(row)
    return rows


def layer_kernel(
    dp, T, live_ref, mb_any, hb_any, inp_any, og_any, upw_ref, dnw_ref, upl_any, upr_any, dnl_any, dnr_any,
    own_out, peer_g_out, hd_out, peer_hd_out, peer_own_out, red_out, peer_red_out,
    low_out, peer_low_out, summed_out, dpair_out, upair_out, upl_out, dnr_out, ps,
    full, peer_g, peer_x, hd, peer_hd, peer_own, red, peer_red, low, peer_low, summed, dpair, upair, upl_ref, dnr_ref, keep_sem,
    mb_ref, hb_ref, inp_ref, og_ref, upr, dnl, small_sem,
    wup, wdn, wsem, idx_v, idx_s, isem,
    part, mid, core_in, side_in, line_in, lpart, lmid, lcore_in, lside_in, lline_in, slope, split_x, split_hd,
    terms, core_box, stage, side_box, acc, line_box, far_part, far_box, far_sem,
    send_sem, full_sem, pg_sem, px_sem, po_sem, one_sem, tline_sem, pr_sem,
    lone_sem, lline_sem, pl_sem, hd_sem, core_sem, side_sem, line_sem,
):
    d, t = lax.axis_index("dp"), lax.axis_index("tensor")
    c, b, a = t % 2, (t // 2) % 2, t // 4
    A = T // 4
    q = t % A
    slots, blk = upw_ref.shape[0], upw_ref.shape[1]
    bps, n = full.shape[2], full.shape[4]
    blocks = hd.shape[1]
    rank = red.shape[1]
    half = dpair.shape[1]
    total_blocks = T * bps
    levels = total_blocks.bit_length() - 1
    low_levels = blocks.bit_length() - 1
    J = levels + 1
    U = 2
    peers = dp - 1
    core, side = (d, a * 4 + b * 2 + 1 - c), (d, a * 4 + (1 - b) * 2 + c)
    copies = Copies(send_sem)
    kept = []

    def keep(src, dst):
        copy = pltpu.make_async_copy(src, dst, keep_sem.at[len(kept)])
        copy.start()
        kept.append(copy)

    pairs = (
        (inp_any, inp_ref), (og_any, og_ref), (upl_any, upl_ref), (dnr_any, dnr_ref),
        (mb_any, mb_ref), (hb_any, hb_ref), (upr_any, upr), (dnl_any, dnl),
    )
    loads = [pltpu.make_async_copy(src, dst, small_sem.at[i]) for i, (src, dst) in enumerate(pairs)]
    for load in loads:
        load.start()
    load_up = pltpu.make_async_copy(upw_ref, wup.at[pl.ds(0, slots)], wsem.at[0])
    load_dn = pltpu.make_async_copy(dnw_ref, wdn.at[pl.ds(0, slots)], wsem.at[1])
    load_up.start()
    load_dn.start()
    loads[0].wait()
    loads[1].wait()
    for j in range(bps):
        full[t, 0, j] = inp_ref[:, j * blk : (j + 1) * blk].T
        full[t, 1, j] = og_ref[:, j * blk : (j + 1) * blk].T
    loads[2].wait()
    loads[3].wait()
    part[0] = dot3(upl_ref[...], full[t, 0].reshape(bps * blk, n), 0, 0)
    part[1] = dot3(dnr_ref[...], full[t, 1].reshape(bps * blk, n), 1, 0)
    greet(d, t, dp, T)

    def other(k):
        return lax.rem(d + k + 1, dp)

    def send(i, s, where, cond=None):
        copies.send(full.at[s, i], full.at[s, i], full_sem.at[s, i], where, cond)

    def got(i, s, where, cond=None):
        arrived(full.at[s, i], full_sem.at[s, i], where, cond)

    def across(i, s, cond=None):
        for k in range(peers):
            o = other(k)
            if i:
                copies.send(full.at[s, 1], peer_g.at[k, s], pg_sem.at[k, s], (o, t), cond)
            else:
                rows = pl.ds(pl.multiple_of(o * half, half), half)
                copies.send(full.at[s, 0, :, rows, :], peer_x.at[k, s], px_sem.at[k, s], (o, t), cond)

    own_rows = peer_own.shape[1]

    rows_near = by_distance(a, A)

    def gap(row):
        return jnp.where(row > a, row - a, a - row)

    def down_line(i):
        for k, row in enumerate(rows_near[1:]):
            send(i, t, (d, row * 4 + b * 2 + c), None if k == 0 else gap(row) <= 2)

    def near(s):
        return s // 8 == q // 2

    near_rows = [q // 2 * 2, q // 2 * 2 + 1]

    def place(k, col):
        return rows_near[k] * 4 + col * 2 + c

    def from_line(i, k):
        s = place(k, b)
        got(i, s, side)
        if k >= 2:
            row = rows_near[k]
            onward = jnp.where(row > a, a - 1, a + 1)
            inside = (gap(row) >= 2) & (onward >= 0) & (onward < A)
            send(i, s, (d, lax.rem(onward + A, A) * 4 + b * 2 + c), inside)
        send(i, s, side)
        across(i, s, near(s) if i else None)
        send(i, s, core)

    def from_side(i, k):
        s = place(k, 1 - b)
        got(i, s, side)
        across(i, s, near(s) if i else None)
        send(i, s, core)

    my_places = [t, place(0, 1 - b)]
    for k in range(1, A):
        my_places += [place(k, b), place(k, 1 - b)]

    total = Total(
        red, peer_red, dp, d, t, T, part, mid, core_in, side_in, line_in, copies,
        (one_sem, tline_sem, pr_sem),
    )
    total.to_core()
    down_line(0)
    across(0, t)
    total.to_side()
    send(0, t, side)
    send(0, t, core)
    total.to_line()
    send(1, t, side)
    down_line(1)
    across(1, t)
    send(1, t, core)
    for k in range(peers):
        o = other(k)
        at = o * own_rows * peer_own.shape[2]
        for j in range(own_rows):
            pos = at + j * peer_own.shape[2]
            inner = pl.ds(pl.multiple_of(pos % blk, peer_own.shape[2]), peer_own.shape[2])
            copies.send(full.at[t, 0, pos // blk, inner, :], peer_own.at[k, j], po_sem.at[k, j], (o, t))

    for load in loads[4:]:
        load.wait()

    lane = lax.broadcasted_iota(jnp.int32, (8, 128), 1)
    wide = 8 if slots % 8 == 0 else 1

    def number(s, v):
        h = hb_ref[s]
        p = h * J + pair_of(mb_ref[s], (t * blocks + h) % total_blocks, levels)
        p = jnp.where(s < live_ref[0], p, -1)
        ps[s] = p
        return jnp.where(lane == s, p, v)

    row_of = lax.fori_loop(0, slots, number, jnp.full((8, 128), -2, jnp.int32), unroll=wide)

    def link(s, v):
        prev, last = v
        p = ps[s]
        prev = jnp.where((lane > s) & (row_of == p), s, prev)
        last = jnp.where(lane == p, s, last)
        return prev, last

    none = jnp.full((8, 128), slots, jnp.int32)
    prev, last = lax.fori_loop(0, slots, link, (none, none), unroll=wide)
    idx_v[0] = prev
    idx_v[1] = last
    to_scalar = pltpu.make_async_copy(idx_v, idx_s, isem.at[0])
    to_scalar.start()
    keep(upl_ref, upl_out)
    keep(dnr_ref, dnr_out)
    from_line(0, 1)
    from_side(0, 0)
    for k in range(2, A):
        from_line(0, k)
    for k in range(1, A):
        from_side(0, k)
    total.reduce()
    to_scalar.wait()
    load_up.wait()
    load_dn.wait()
    wup[slots] = jnp.zeros((blk, blk), f32)
    wdn[slots] = jnp.zeros((blk, blk), f32)

    @pl.loop(0, slots)
    def _(s):
        before_it = idx_s[0, 0, s]
        wup[s] = wup[s] + wup[before_it]
        wdn[s] = wdn[s] + wdn[before_it]

    from_line(1, 1)
    from_side(1, 0)

    def from_core(i):
        for k in range(2 * A):
            got(i, k * 2 + 1 - c, core)

    far = [1 << k for k in range(levels - low_levels)]

    def weight(w, h, j):
        return w[idx_s[1, 0, h * J + j]]

    def split_in(i):
        @pl.loop(0, blocks)
        def _(m):
            split_x[m] = right3(full[q * 4 + m // bps, i, m % bps], 0)

    def gather_up(i, h, w, axis, start):
        v = start + contract(left3(weight(w, h, 0), axis), split_x[h], axis, 0)
        for k in range(low_levels):
            v = v + contract(left3(weight(w, h, 1 + k), axis), split_x[flip(h, 1 << k, blocks)], axis, 0)
        for k, r in enumerate(far):
            x = right3(full[flip(q, r, A) * 4 + h // bps, i, h % bps], 0)
            v = v + contract(left3(weight(w, h, 1 + low_levels + k), axis), x, axis, 0)
        return v

    def span(h):
        return pl.ds(pl.multiple_of(h * blk, blk), blk)

    from_core(0)
    total.finish()
    split_in(0)
    low_in = right3(red[0], 0)
    scale = 0.7978845608028654

    @pl.loop(0, blocks // U)
    def _(i):
        for j in range(U):
            h = i * U + j
            v = gather_up(0, h, wup, 0, contract(left3(upr[:, span(h)], 0), low_in, 0, 0))
            th = jnp.tanh(scale * (v + 0.044715 * (v * v * v)))
            hidden = 0.5 * v * (1.0 + th)
            slope[h] = 0.5 * (1.0 + th) + 0.5 * v * (1.0 - th * th) * (scale * (1.0 + 3 * 0.044715 * (v * v)))
            hd[0, h] = hidden
            split_hd[h] = right3(hidden, 0)

    part_blocks = blocks // 2
    halved = dp == 2 and blocks % 2 == 0

    def hidden_parts(p, o):
        if p == 0 and halved:
            rows = pl.ds(pl.multiple_of(o * half, half), half)
            return [(pl.ds(o * part_blocks, part_blocks),), (pl.ds((1 - o) * part_blocks, part_blocks), rows)]
        return [(pl.ds(j * part_blocks, part_blocks),) for j in range(2)]

    def send_hidden(p):
        for k in range(peers):
            for j, at in enumerate(hidden_parts(p, other(k))):
                copies.send(hd.at[(p,) + at], peer_hd.at[(k, p) + at], hd_sem.at[k, p, j], (other(k), t))

    def to_partner(p, rows):
        for r in rows:
            row = flip(q, r, A)
            copies.send(terms.at[row, p, 1 - c], core_box.at[row, p], core_sem.at[row, p], core)

    def spread_far(p, w, axis):
        for k, r in enumerate(far):
            row = flip(q, r, A)

            @pl.loop(0, blocks // U)
            def _(i):
                for j in range(U):
                    h = i * U + j
                    u = h // bps
                    terms[row, p, u % 2, u // 2, h % bps] = contract(
                        left3(weight(w, h, 1 + low_levels + k), axis), split_hd[h], axis, 0
                    )

        to_partner(p, far)

    def spread_near(p, w, axis):
        @pl.loop(0, blocks // U)
        def _(i):
            for j in range(U):
                m = i * U + j
                u = m // bps
                v = contract(left3(weight(w, m, 0), axis), split_hd[m], axis, 0)
                for k in range(low_levels):
                    h = flip(m, 1 << k, blocks)
                    v = v + contract(left3(weight(w, h, 1 + k), axis), split_hd[h], axis, 0)
                terms[q, p, u % 2, u // 2, m % bps] = v

        to_partner(p, [0])

    order = []
    for r in range(A):
        if r % 4 < 2:
            order += [r + 2, r] if A > 2 else [r]

    def to_side(p, some):
        for r in some:
            row = flip(q, r, A)
            theirs = mine(r ^ 1)
            if theirs:
                arrived(core_box.at[row, p], core_sem.at[row, p], core)
            if mine(r) and not theirs:
                src = terms.at[row, p, c, 1 - b]
            elif theirs and not mine(r):
                src = core_box.at[row, p, 1 - b]
            else:
                src = stage.at[row, p]
                if theirs:
                    stage[row, p] = terms[row, p, c, 1 - b] + core_box[row, p, 1 - b]
                else:
                    stage[row, p] = jnp.zeros(stage.shape[2:], f32)
            copies.send(src, side_box.at[row, p], side_sem.at[row, p], side)

    def to_line(p, some):
        for r in some:
            row = flip(q, r, A)
            arrived(side_box.at[row, p], side_sem.at[row, p], side)
            v = side_box[row, p]
            if mine(r):
                v = v + terms[row, p, c, b]
            if mine(r ^ 1):
                v = v + core_box[row, p, b]
            acc[row, p] = v
            k = flip(row, a, A)
            copies.send(
                acc.at[row, p], line_box.at[k, p], line_sem.at[k, p], (d, row * 4 + b * 2 + c), row != a
            )

    def pass_stage(box, sem, places):
        for s in places:
            for k in range(peers):
                arrived(box.at[k, s], sem.at[k, s], core)
                copies.send(box.at[k, s], box.at[k, s], sem.at[k, s], core)

    def passed_stage(box, sem, rows):
        for k in range(peers):
            for row in rows:
                for col in range(2):
                    s = row * 4 + col * 2 + 1 - c
                    arrived(box.at[k, s], sem.at[k, s], core)

    def far_stage():
        for i, r in enumerate(far[1:]):
            row = flip(q, r, A)

            @pl.loop(0, blocks)
            def _(h):
                g = right3(full[row * 4 + h // bps, 1, h % bps], 1)
                for k in range(peers):
                    rows = pl.ds(pl.multiple_of(other(k) * half, half), half)
                    far_part[k, i, h] = contract(left3(hd[0, h, rows, :], 1), g, 1, 1)

        for k in range(peers):
            copies.send(far_part.at[k], far_box.at[k], far_sem.at[k], (other(k), t))

    def far_wait_stage():
        for k in range(peers):
            arrived(far_box.at[k], far_sem.at[k], core)

    def hidden_stage(p):
        for k in range(peers):
            for j, at in enumerate(hidden_parts(p, d)):
                arrived(peer_hd.at[(k, p) + at], hd_sem.at[k, p, j], core)

    here_rows = pl.ds(pl.multiple_of(d * half, half), half)

    def hidden_rows(h):
        rows = [hd[0, h, here_rows, :]] + [peer_hd[k, 0, h, here_rows, :] for k in range(peers)]
        return left3(jnp.concatenate(rows, axis=1), 1)

    def grad_cols(plane, m):
        s = plane * 4 + m // bps
        g = [full[s, 1, m % bps]] + [peer_g[k, s, m % bps] for k in range(peers)]
        return right3(jnp.concatenate(g, axis=1), 1)

    def down_stage():
        @pl.loop(0, blocks)
        def _(m):
            g = grad_cols(q, m)
            left = jnp.concatenate(
                [hidden_rows(m)] + [hidden_rows(flip(m, 1 << k, blocks)) for k in range(low_levels)], axis=0
            )
            v = contract(left, g, 1, 1)
            dpair[m * J] = v[:half]
            for k in range(low_levels):
                dpair[flip(m, 1 << k, blocks) * J + 1 + k] = v[(k + 1) * half : (k + 2) * half]
            dpair[m * J + 1 + low_levels] = contract(hidden_rows(m), grad_cols(flip(q, 1, A), m), 1, 1)
            own_hidden = left3(hd[0, m, here_rows, :], 1)
            for i, r in enumerate(far[1:]):
                g = right3(full[flip(q, r, A) * 4 + m // bps, 1, m % bps], 1)
                v = contract(own_hidden, g, 1, 1)
                for k in range(peers):
                    v = v + far_box[k, i, m]
                dpair[m * J + 2 + low_levels + i] = v

    def data_rows(plane, m):
        s = plane * 4 + m // bps
        x = [full[s, 0, m % bps, here_rows, :]] + [peer_x[k, s, m % bps] for k in range(peers)]
        return left3(jnp.concatenate(x, axis=1), 1)

    def up_stage():
        @pl.loop(0, blocks)
        def _(h):
            back = [hd[1, h]] + [peer_hd[k, 1, h] for k in range(peers)]
            back = right3(jnp.concatenate(back, axis=1), 1)
            left = [data_rows(q, h)] + [data_rows(q, flip(h, 1 << k, blocks)) for k in range(low_levels)]
            left += [data_rows(flip(q, r, A), h) for r in far]
            v = contract(jnp.concatenate(left, axis=0), back, 1, 1)
            for j in range(J):
                upair[h * J + j] = v[j * half : (j + 1) * half]

    def sum_stage():
        for p in range(2):
            v = acc[a, p]
            for k in range(1, A):
                arrived(line_box.at[k, p], line_sem.at[k, p], core)
                v = v + line_box[k, p]
            summed[p] = v

    def own_stage():
        for k in range(peers):
            for j in range(own_rows):
                arrived(peer_own.at[k, j], po_sem.at[k, j], core)

    send_hidden(0)
    keep(hd.at[0], hd_out.at[0])
    from_line(1, 2)
    spread_far(0, wdn, 0)
    to_side(0, order[:1])
    spread_near(0, wdn, 0)
    for k in range(3, A):
        from_line(1, k)
    to_side(0, order[1:])
    for k in range(1, A):
        from_side(1, k)
    lpart[0] = jnp.zeros((rank, n), f32)
    lpart[1] = jnp.zeros((rank, n), f32)
    from_core(1)
    split_in(1)
    back_mid = right3(red[1], 0)

    @pl.loop(0, blocks // U)
    def _(i):
        for j in range(U):
            h = i * U + j
            lpart[0] += contract(left3(dnl[span(h), :], 0), split_hd[h], 0, 0)
            v = gather_up(1, h, wdn, 1, contract(left3(dnl[span(h), :], 1), back_mid, 1, 0))
            back = v * slope[h]
            hd[1, h] = back
            bs = right3(back, 0)
            split_hd[h] = bs
            lpart[1] += contract(left3(upr[:, span(h)], 1), bs, 1, 0)

    send_hidden(1)
    low_total = Total(
        low, peer_low, dp, d, t, T, lpart, lmid, lcore_in, lside_in, lline_in, copies,
        (lone_sem, lline_sem, pl_sem),
    )
    low_total.to_core()
    keep(hd.at[1], hd_out.at[1])
    to_line(0, order[:2])
    far_stage()
    spread_far(1, wup, 1)
    low_total.to_side()
    to_side(1, order[:1])
    to_line(0, order[2:])
    spread_near(1, wup, 1)
    to_side(1, order[1:])
    low_total.to_line()

    pass_stage(peer_x, px_sem, my_places)
    total.pass_peers()
    to_line(1, order[:2])
    pass_stage(peer_g, pg_sem, [row * 4 + col * 2 + c for row in near_rows for col in range(2)])
    for k in range(peers):
        arrived(peer_g.at[k, t], pg_sem.at[k, t], core, (t // 8 < q // 2) | (t // 8 > q // 2))
    passed_stage(peer_x, px_sem, range(A))
    passed_stage(peer_g, pg_sem, near_rows)
    keep(full.at[t], own_out)
    keep(peer_g.at[:, t], peer_g_out)
    to_line(1, order[2:])
    low_total.reduce()
    own_stage()
    total.finish_peers()
    keep(red, red_out)
    keep(peer_red, peer_red_out)
    keep(peer_own, peer_own_out)
    hidden_stage(0)
    if halved:
        blocks_here = pl.ds(d * part_blocks, part_blocks)
        keep(peer_hd.at[:, 0, blocks_here], peer_hd_out.at[:, 0, blocks_here])
    else:
        keep(peer_hd.at[:, 0], peer_hd_out.at[:, 0])
    hidden_stage(1)
    keep(peer_hd.at[:, 1], peer_hd_out.at[:, 1])
    up_stage()
    keep(upair, upair_out)
    far_wait_stage()
    down_stage()
    keep(dpair, dpair_out)
    low_total.finish()
    keep(low, low_out)
    low_total.pass_peers()
    sum_stage()
    keep(summed, summed_out)
    low_total.finish_peers()
    keep(peer_low, peer_low_out)
    for copy in kept:
        copy.wait()
    copies.drain()
    if copies.count != send_sem.shape[0]:
        raise ValueError(copies.count, send_sem.shape[0])


def grads_kernel(
    dp, own_in, peer_g, hd, peer_hd,
    peer_own, red, peer_red, low, peer_low, summed, dpair, upair, upl, dnr, ps,
    res, ing, upg, dng, uplg, uprg, dnlg, dnrg,
):
    slots, half, blk = upg.shape
    bps = own_in.shape[1]
    blocks = hd.shape[1]
    d = lax.axis_index("dp")
    peers = range(dp - 1)

    def cat(first, rest):
        return jnp.concatenate([first] + rest, axis=1)

    unroll = 4 if slots % 4 == 0 else 1

    @pl.loop(0, slots // unroll)
    def _(i):
        for j in range(unroll):
            s = i * unroll + j
            p = ps[s]
            keep = (p >= 0).astype(f32)
            p = jnp.maximum(p, 0)
            upg[s] = upair[p] * keep
            dng[s] = dpair[p] * keep

    for j in range(bps):
        span = slice(j * blk, (j + 1) * blk)
        res[:, span] = (summed[0, j] + dot3(dnr[:, span], low[0], 0, 0)).T
        ing[:, span] = (summed[1, j] + dot3(upl[span, :], low[1], 1, 0)).T
    back_in = right3(cat(low[1], [peer_low[k, 1] for k in peers]), 1)
    n = uplg.shape[0]
    step = min(n, blk)
    for j in range(n // step):
        at = d * n + j * step
        inner = pl.ds(pl.multiple_of(at % blk, step), step)
        x = cat(own_in[0, at // blk, inner, :], [peer_own[k, j] for k in peers])
        uplg[j * step : (j + 1) * step, :] = contract(left3(x, 1), back_in, 1, 1)
    n = uprg.shape[0]
    span = pl.ds(pl.multiple_of(d * n, n), n)
    left_in = left3(cat(red[0, span, :], [peer_red[k, 0, span, :] for k in peers]), 1)
    left_mid = left3(cat(low[0, span, :], [peer_low[k, 0, span, :] for k in peers]), 1)
    for h in range(blocks):
        back = cat(hd[1, h], [peer_hd[k, 1, h] for k in peers])
        uprg[:, h * blk : (h + 1) * blk] = contract(left_in, right3(back, 1), 1, 1)
    for j in range(bps):
        g = cat(own_in[1, j], [peer_g[k, j] for k in peers])
        dnrg[:, j * blk : (j + 1) * blk] = contract(left_mid, right3(g, 1), 1, 1)
    back_mid = right3(cat(red[1], [peer_red[k, 1] for k in peers]), 1)
    n = dnlg.shape[0]
    step = min(n, blk)
    for j in range(n // step):
        at = d * n + j * step
        inner = pl.ds(pl.multiple_of(at % blk, step), step)
        hidden = cat(hd[0, at // blk, inner, :], [peer_hd[k, 0, at // blk, inner, :] for k in peers])
        dnlg[j * step : (j + 1) * step, :] = contract(left3(hidden, 1), back_mid, 1, 1)


def shards(
    dp, T,
    inputs, out_grad, up_weight, down_weight, up_left, up_right, down_left, down_right,
    model_block, hidden_block, live_slots,
):
    tokens, feats = inputs.shape
    slots, blk = up_weight.shape[0], up_weight.shape[1]
    width = up_right.shape[1]
    rank = up_left.shape[1]
    blocks = width // blk
    bps = feats // blk
    A = T // 4
    peers = dp - 1
    half = blk // dp
    pairs = blocks * (T * bps).bit_length()
    own = feats // dp
    own_step = min(own, blk)
    own_rows = own // own_step
    DMA = pltpu.SemaphoreType.DMA
    sds = lambda *shape: jax.ShapeDtypeStruct(shape, f32)
    vmem = lambda *shape: pltpu.VMEM(shape, f32)
    bf16 = jnp.bfloat16
    spare = A.bit_length() - 2
    gather = 2 + A - 1 + A - 2 + peers + (A - 1) * (2 + peers) + A * (1 + peers)
    total = 3 + A - 1 + 2 * peers
    scatter = 2 * (1 + A.bit_length() - 1) + 4 * A
    sends = 2 * gather + 2 * total + scatter + peers * (own_rows + 2 * A + 9)
    outs = pl.pallas_call(
        functools.partial(layer_kernel, dp, T),
        out_shape=(
            sds(2, bps, blk, tokens),
            sds(peers, bps, blk, tokens),
            sds(2, blocks, blk, tokens),
            sds(peers, 2, blocks, blk, tokens),
            sds(peers, own_rows, own_step, tokens),
            sds(2, rank, tokens),
            sds(peers, 2, rank, tokens),
            sds(2, rank, tokens),
            sds(peers, 2, rank, tokens),
            sds(2, bps, blk, tokens),
            sds(pairs, half, blk),
            sds(pairs, half, blk),
            sds(feats, rank),
            sds(rank, feats),
            jax.ShapeDtypeStruct((slots,), jnp.int32),
        ),
        in_specs=[SM] + [HB] * 10,
        out_specs=[pl.BlockSpec(memory_space=pl.ANY)] * 14 + [SM],
        scratch_shapes=[
            vmem(T, 2, bps, blk, tokens),
            vmem(peers, T, bps, blk, tokens),
            vmem(peers, T, bps, half, tokens),
            vmem(2, blocks, blk, tokens),
            vmem(peers, 2, blocks, blk, tokens),
            vmem(peers, own_rows, own_step, tokens),
            vmem(2, rank, tokens),
            vmem(peers, 2, rank, tokens),
            vmem(2, rank, tokens),
            vmem(peers, 2, rank, tokens),
            vmem(2, bps, blk, tokens),
            vmem(pairs, half, blk),
            vmem(pairs, half, blk),
            vmem(feats, rank),
            vmem(rank, feats),
            DMA((17,)),
            pltpu.SMEM((slots,), jnp.int32), pltpu.SMEM((slots,), jnp.int32),
            vmem(tokens, feats), vmem(tokens, feats), vmem(rank, width), vmem(width, rank), DMA((8,)),
            vmem(slots + 1, blk, blk), vmem(slots + 1, blk, blk), DMA((2,)),
            pltpu.VMEM((2, 8, 128), jnp.int32), pltpu.SMEM((2, 8, 128), jnp.int32),
            DMA((1,)),
            vmem(2, rank, tokens), vmem(2, rank, tokens), vmem(rank, tokens), vmem(rank, tokens),
            vmem(A, rank, tokens),
            vmem(2, rank, tokens), vmem(2, rank, tokens), vmem(rank, tokens), vmem(rank, tokens),
            vmem(A, rank, tokens),
            vmem(blocks, blk, tokens),
            pltpu.VMEM((blocks, 3 * blk, tokens), bf16),
            pltpu.VMEM((blocks, 3 * blk, tokens), bf16),
            vmem(A, 2, 2, 2, bps, blk, tokens),
            vmem(A, 2, 2, bps, blk, tokens),
            vmem(A, 2, bps, blk, tokens),
            vmem(A, 2, bps, blk, tokens),
            vmem(A, 2, bps, blk, tokens),
            vmem(A, 2, bps, blk, tokens),
            vmem(peers, spare, blocks, half, blk), vmem(peers, spare, blocks, half, blk), DMA((peers,)),
            DMA((sends,)), DMA((T, 2)), DMA((peers, T)), DMA((peers, T)), DMA((peers, own_rows)),
            DMA((3,)), DMA((A,)), DMA((peers, 2)),
            DMA((3,)), DMA((A,)), DMA((peers, 2)), DMA((peers, 2, 2)),
            DMA((A, 2)), DMA((A, 2)), DMA((A, 2)),
        ],
        compiler_params=pltpu.CompilerParams(collective_id=0, has_side_effects=True, vmem_limit_bytes=46 << 20),
    )(
        live_slots,
        *(
            pltpu.with_memory_space_constraint(v, pltpu.HBM)
            for v in (
                model_block, hidden_block, inputs, out_grad, up_weight, down_weight,
                up_left, up_right, down_left, down_right,
            )
        )
    )
    return pl.pallas_call(
        functools.partial(grads_kernel, dp),
        out_shape=(
            sds(tokens, feats),
            sds(tokens, feats),
            sds(slots, half, blk),
            sds(slots, half, blk),
            sds(feats // dp, rank),
            sds(rank // dp, width),
            sds(width // dp, rank),
            sds(rank // dp, feats),
        ),
        in_specs=[VM] * 14 + [SM],
        out_specs=[VM] * 8,
        compiler_params=pltpu.CompilerParams(vmem_limit_bytes=24 << 20),
    )(*outs)


def solution(mesh):
    return jax.shard_map(
        functools.partial(shards, mesh.shape["dp"], mesh.shape["tensor"]),
        mesh=mesh,
        in_specs=(
            P("dp", "tensor"),
            P("dp", "tensor"),
            P("tensor", None, None),
            P("tensor", None, None),
            P("tensor", None),
            P(None, "tensor"),
            P("tensor", None),
            P(None, "tensor"),
            P("tensor"),
            P("tensor"),
            P("tensor"),
        ),
        out_specs=(
            P("dp", "tensor"),
            P("dp", "tensor"),
            P("tensor", "dp", None),
            P("tensor", "dp", None),
            P(("tensor", "dp"), None),
            P("dp", "tensor"),
            P(("tensor", "dp"), None),
            P("dp", "tensor"),
        ),
        check_vma=False,
    )
```

```python
import functools

import jax
import jax.numpy as jnp
from jax import lax
from jax.experimental import pallas as pl
from jax.experimental.pallas import tpu as pltpu
from jax.sharding import PartitionSpec as P

MESH = pl.DeviceIdType.MESH
VM = pl.BlockSpec(memory_space=pltpu.VMEM)
HB = pl.BlockSpec(memory_space=pltpu.HBM)
SM = pl.BlockSpec(memory_space=pltpu.SMEM)
f32 = jnp.float32


def halves(v):
    hi = v.astype(jnp.bfloat16)
    lo = (v - hi.astype(f32)).astype(jnp.bfloat16)
    return hi, lo


def left3(v, axis):
    hi, lo = halves(v)
    return jnp.concatenate([hi, hi, lo], axis=axis)


def right3(v, axis):
    hi, lo = halves(v)
    return jnp.concatenate([hi, lo, hi], axis=axis)


def contract(a, b, da, db):
    return lax.dot_general(a, b, (((da,), (db,)), ((), ())), preferred_element_type=f32)


def dot3(a, b, da, db):
    return contract(left3(a, da), right3(b, db), da, db)


def flip(a, k, size):
    out, bit = 0, 1
    while bit < size:
        out = out + (((a // bit) % 2 + (k // bit) % 2) % 2) * bit
        bit *= 2
    return out


class Copies:
    def __init__(self, sems):
        self.sems, self.count, self.made = sems, 0, []

    def send(self, src, dst, recv, where, cond=None):
        sem = self.sems.at[self.count]
        self.count += 1
        copy = pltpu.make_async_remote_copy(
            src_ref=src, dst_ref=dst, send_sem=sem, recv_sem=recv, device_id=where, device_id_type=MESH
        )
        if cond is None:
            copy.start()
        else:
            pl.when(cond)(copy.start)
        self.made.append((copy, cond))

    def drain(self):
        for copy, cond in self.made:
            if cond is None:
                copy.wait_send()
            else:
                pl.when(cond)(copy.wait_send)


def arrived(ref, recv, where, cond=None):
    copy = pltpu.make_async_remote_copy(
        src_ref=ref, dst_ref=ref, send_sem=recv, recv_sem=recv, device_id=where, device_id_type=MESH
    )
    if cond is None:
        copy.wait_recv()
    else:
        pl.when(cond)(copy.wait_recv)


def line_steps(a, A):
    out = [(a, 0, None)]
    for k in range(1, A):
        out.append(((a + A - k) % A, -1, a >= k))
        out.append(((a + k) % A, 1, a + k < A))
    return out


def greet(d, t, dp, T):
    barrier = pltpu.get_barrier_semaphore()
    A = T // 4
    c, b, a = t % 2, (t // 2) % 2, t // 4
    whom = [(d, a * 4 + b * 2 + 1 - c), (d, a * 4 + (1 - b) * 2 + c)]
    whom += [(d, (t + 4 * k) % T) for k in range(1, A)]
    whom += [(lax.rem(d + k, dp), t) for k in range(1, dp)]
    for where in whom:
        pl.semaphore_signal(barrier, inc=1, device_id=where, device_id_type=MESH)
    pl.semaphore_wait(barrier, len(whom))


class Total:
    def __init__(self, out, peer_out, dp, d, t, T, part, mid, mine, core_in, side_in, line_in, copies, sems):
        self.out, self.peer_out, self.dp, self.d, self.t, self.A = out, peer_out, dp, d, t, T // 4
        self.part, self.mid, self.mine, self.core_in, self.side_in, self.line_in = part, mid, mine, core_in, side_in, line_in
        self.copies = copies
        self.one_sem, self.line_sem, self.peer_sem = sems
        self.c, self.b, self.a = t % 2, (t // 2) % 2, t // 4
        self.half = part.shape[1] // 2
        self.core, self.side = (d, self.place(self.a, 0, 1)), (d, self.place(self.a, 1, 0))

    def place(self, row, b, c):
        return row * 4 + (self.b + b) % 2 * 2 + (self.c + c) % 2

    def to_core(self):
        self.copies.send(self.part.at[1 - self.c], self.core_in, self.one_sem.at[0], self.core)

    def to_side(self):
        arrived(self.core_in, self.one_sem.at[0], self.core)
        self.mid[0] = self.part[self.c] + self.core_in[...]
        self.copies.send(self.mid.at[0, self.rows(1 - self.b)], self.side_in, self.one_sem.at[1], self.side)

    def rows(self, b):
        return pl.ds(pl.multiple_of(b * self.half, self.half), self.half)

    def to_line(self):
        arrived(self.side_in, self.one_sem.at[1], self.side)
        self.mine[...] = self.mid[0, self.rows(self.b), :] + self.side_in[...]
        for k in range(1, self.A):
            row = (self.a + k) % self.A
            self.copies.send(
                self.mine, self.line_in.at[self.A - k], self.line_sem.at[self.A - k],
                (self.d, self.place(row, 0, 0)),
            )

    def reduce(self):
        total = self.mine[...]
        for k in range(1, self.A):
            arrived(self.line_in.at[k], self.line_sem.at[k], self.core)
            total = total + self.line_in[k]
        self.out[self.c, self.rows(self.b), :] = total
        piece = self.out.at[self.c, self.rows(self.b)]
        self.copies.send(piece, piece, self.one_sem.at[3], self.side)

    def share(self):
        arrived(self.out.at[self.c, self.rows(1 - self.b)], self.one_sem.at[3], self.side)
        whole = self.out.at[self.c]
        self.copies.send(whole, whole, self.one_sem.at[2], self.core)
        for p in range(self.dp - 1):
            self.copies.send(
                whole, self.peer_out.at[p, self.c], self.peer_sem.at[p, self.c],
                (lax.rem(self.d + p + 1, self.dp), self.t),
            )

    def finish(self):
        arrived(self.out.at[1 - self.c], self.one_sem.at[2], self.core)

    def pass_peers(self):
        for p in range(self.dp - 1):
            box = self.peer_out.at[p, self.c]
            arrived(box, self.peer_sem.at[p, self.c], self.core)
            self.copies.send(box, box, self.peer_sem.at[p, self.c], self.core)

    def finish_peers(self):
        for p in range(self.dp - 1):
            arrived(self.peer_out.at[p, 1 - self.c], self.peer_sem.at[p, 1 - self.c], self.core)


def power(r):
    return r > 0 and r & (r - 1) == 0


def mine(r):
    return r == 0 or power(r)


def pair_of(m, g, levels):
    diff = m ^ g
    return sum((diff >= (1 << k)).astype(jnp.int32) for k in range(levels))


def by_distance(a, A):
    table = [sorted(range(A), key=lambda r: (abs(r - v), r)) for v in range(A)]
    rows = []
    for i in range(A):
        row = table[0][i]
        for v in range(1, A):
            row = jnp.where(a == v, table[v][i], row)
        rows.append(row)
    return rows


def layer_kernel(
    dp, T, live_ref, mb_any, hb_any, inp_any, og_any, upw_ref, dnw_ref, upl_any, upr_any, dnl_any, dnr_any,
    own_out, peer_g_out, hd_out, peer_hd_out, peer_own_out, red_out, peer_red_out,
    low_out, peer_low_out, summed_out, dpair_out, upair_out, upl_out, dnr_out, ps,
    full, peer_g, peer_x, hd, peer_hd, peer_own, red, peer_red, low, peer_low, summed, dpair, upair, upl_ref, dnr_ref, keep_sem,
    mb_ref, hb_ref, inp_ref, og_ref, upr, dnl, small_sem,
    wup, wdn, wsem, idx_v, idx_s, isem,
    part, mid, own_half, core_in, side_in, line_in, lpart, lmid, lown_half, lcore_in, lside_in, lline_in, slope, split_x, split_hd,
    terms, core_box, stage, side_box, acc, line_box, far_part, far_box, far_sem,
    send_sem, full_sem, pg_sem, px_sem, po_sem, one_sem, tline_sem, pr_sem,
    lone_sem, lline_sem, pl_sem, hd_sem, core_sem, side_sem, line_sem,
):
    d, t = lax.axis_index("dp"), lax.axis_index("tensor")
    c, b, a = t % 2, (t // 2) % 2, t // 4
    A = T // 4
    q = t % A
    slots, blk = upw_ref.shape[0], upw_ref.shape[1]
    bps, n = full.shape[2], full.shape[4]
    blocks = hd.shape[1]
    rank = red.shape[1]
    half = dpair.shape[1]
    total_blocks = T * bps
    levels = total_blocks.bit_length() - 1
    low_levels = blocks.bit_length() - 1
    J = levels + 1
    U = 2
    peers = dp - 1
    core, side = (d, a * 4 + b * 2 + 1 - c), (d, a * 4 + (1 - b) * 2 + c)
    copies = Copies(send_sem)
    kept = []

    def keep(src, dst):
        copy = pltpu.make_async_copy(src, dst, keep_sem.at[len(kept)])
        copy.start()
        kept.append(copy)

    pairs = (
        (inp_any, inp_ref), (og_any, og_ref), (upl_any, upl_ref), (dnr_any, dnr_ref),
        (mb_any, mb_ref), (hb_any, hb_ref), (upr_any, upr), (dnl_any, dnl),
    )
    loads = [pltpu.make_async_copy(src, dst, small_sem.at[i]) for i, (src, dst) in enumerate(pairs)]
    for load in loads:
        load.start()
    load_up = pltpu.make_async_copy(upw_ref, wup.at[pl.ds(0, slots)], wsem.at[0])
    load_dn = pltpu.make_async_copy(dnw_ref, wdn.at[pl.ds(0, slots)], wsem.at[1])
    load_up.start()
    load_dn.start()
    loads[0].wait()
    loads[1].wait()
    for j in range(bps):
        full[t, 0, j] = inp_ref[:, j * blk : (j + 1) * blk].T
        full[t, 1, j] = og_ref[:, j * blk : (j + 1) * blk].T
    loads[2].wait()
    loads[3].wait()
    part[0] = dot3(upl_ref[...], full[t, 0].reshape(bps * blk, n), 0, 0)
    part[1] = dot3(dnr_ref[...], full[t, 1].reshape(bps * blk, n), 1, 0)
    greet(d, t, dp, T)

    def other(k):
        return lax.rem(d + k + 1, dp)

    def send(i, s, where, cond=None):
        copies.send(full.at[s, i], full.at[s, i], full_sem.at[s, i], where, cond)

    def got(i, s, where, cond=None):
        arrived(full.at[s, i], full_sem.at[s, i], where, cond)

    def across(i, s, cond=None):
        for k in range(peers):
            o = other(k)
            if i:
                copies.send(full.at[s, 1], peer_g.at[k, s], pg_sem.at[k, s], (o, t), cond)
            else:
                rows = pl.ds(pl.multiple_of(o * half, half), half)
                copies.send(full.at[s, 0, :, rows, :], peer_x.at[k, s], px_sem.at[k, s], (o, t), cond)

    own_rows = peer_own.shape[1]

    rows_near = by_distance(a, A)

    def gap(row):
        return jnp.where(row > a, row - a, a - row)

    at_end = (a == 0) | (a == A - 1)
    at_middle = (a > 0) & (a < A - 1)

    def down_line(i, rows, cond):
        for row in rows:
            send(i, t, (d, row * 4 + b * 2 + c), cond)

    def near(s):
        return s // 8 == q // 2

    near_rows = [q // 2 * 2, q // 2 * 2 + 1]

    def place(k, col):
        return rows_near[k] * 4 + col * 2 + c

    def from_line(i, k):
        s = place(k, b)
        got(i, s, side)
        onward = jnp.where(rows_near[k] > a, a - 1, a + 1)
        inside = (onward >= 0) & (onward < A)
        send(i, s, (d, lax.rem(onward + A, A) * 4 + b * 2 + c), inside)
        send(i, s, side)
        across(i, s, near(s) if i else None)
        send(i, s, core)

    def from_side(i, k):
        s = place(k, 1 - b)
        got(i, s, side)
        across(i, s, near(s) if i else None)
        send(i, s, core)

    my_places = [t, place(0, 1 - b)]
    for k in range(1, A):
        my_places += [place(k, b), place(k, 1 - b)]

    total = Total(
        red, peer_red, dp, d, t, T, part, mid, own_half, core_in, side_in, line_in, copies,
        (one_sem, tline_sem, pr_sem),
    )
    total.to_core()
    down_line(0, rows_near[1:2], None)
    down_line(0, rows_near[2:3], at_middle)
    across(0, t)
    total.to_side()
    send(0, t, side)
    send(0, t, core)
    total.to_line()
    send(1, t, side)
    across(1, t)
    send(1, t, core)
    for k in range(peers):
        o = other(k)
        at = o * own_rows * peer_own.shape[2]
        for j in range(own_rows):
            pos = at + j * peer_own.shape[2]
            inner = pl.ds(pl.multiple_of(pos % blk, peer_own.shape[2]), peer_own.shape[2])
            copies.send(full.at[t, 0, pos // blk, inner, :], peer_own.at[k, j], po_sem.at[k, j], (o, t))

    for load in loads[4:]:
        load.wait()

    lane = lax.broadcasted_iota(jnp.int32, (8, 128), 1)
    wide = 8 if slots % 8 == 0 else 1

    def number(s, v):
        h = hb_ref[s]
        p = h * J + pair_of(mb_ref[s], (t * blocks + h) % total_blocks, levels)
        p = jnp.where(s < live_ref[0], p, -1)
        ps[s] = p
        return jnp.where(lane == s, p, v)

    row_of = lax.fori_loop(0, slots, number, jnp.full((8, 128), -2, jnp.int32), unroll=wide)

    def link(s, v):
        prev, last = v
        p = ps[s]
        prev = jnp.where((lane > s) & (row_of == p), s, prev)
        last = jnp.where(lane == p, s, last)
        return prev, last

    none = jnp.full((8, 128), slots, jnp.int32)
    prev, last = lax.fori_loop(0, slots, link, (none, none), unroll=wide)
    idx_v[0] = prev
    idx_v[1] = last
    to_scalar = pltpu.make_async_copy(idx_v, idx_s, isem.at[0])
    to_scalar.start()
    keep(upl_ref, upl_out)
    keep(dnr_ref, dnr_out)
    from_line(0, 1)
    down_line(1, rows_near[1:2], at_end)
    from_side(0, 0)
    for k in range(2, A):
        from_line(0, k)
    down_line(1, rows_near[1:3], at_middle)
    total.reduce()
    from_side(0, 1)
    from_side(1, 0)
    from_side(0, 2)
    from_line(1, 1)
    for k in range(3, A):
        from_side(0, k)
    to_scalar.wait()
    load_up.wait()
    load_dn.wait()
    wup[slots] = jnp.zeros((blk, blk), f32)
    wdn[slots] = jnp.zeros((blk, blk), f32)

    @pl.loop(0, slots)
    def _(s):
        before_it = idx_s[0, 0, s]
        wup[s] = wup[s] + wup[before_it]
        wdn[s] = wdn[s] + wdn[before_it]

    from_line(1, 2)
    total.share()

    def from_core(i):
        for k in range(2 * A):
            got(i, k * 2 + 1 - c, core)

    far = [1 << k for k in range(levels - low_levels)]

    def weight(w, h, j):
        return w[idx_s[1, 0, h * J + j]]

    def split_in(i):
        @pl.loop(0, blocks)
        def _(m):
            split_x[m] = right3(full[q * 4 + m // bps, i, m % bps], 0)

    def gather_up(i, h, w, axis, start):
        v = start + contract(left3(weight(w, h, 0), axis), split_x[h], axis, 0)
        for k in range(low_levels):
            v = v + contract(left3(weight(w, h, 1 + k), axis), split_x[flip(h, 1 << k, blocks)], axis, 0)
        for k, r in enumerate(far):
            x = right3(full[flip(q, r, A) * 4 + h // bps, i, h % bps], 0)
            v = v + contract(left3(weight(w, h, 1 + low_levels + k), axis), x, axis, 0)
        return v

    def span(h):
        return pl.ds(pl.multiple_of(h * blk, blk), blk)

    from_core(0)
    total.finish()
    split_in(0)
    low_in = right3(red[0], 0)
    scale = 0.7978845608028654

    @pl.loop(0, blocks // U)
    def _(i):
        for j in range(U):
            h = i * U + j
            v = gather_up(0, h, wup, 0, contract(left3(upr[:, span(h)], 0), low_in, 0, 0))
            th = jnp.tanh(scale * (v + 0.044715 * (v * v * v)))
            hidden = 0.5 * v * (1.0 + th)
            slope[h] = 0.5 * (1.0 + th) + 0.5 * v * (1.0 - th * th) * (scale * (1.0 + 3 * 0.044715 * (v * v)))
            hd[0, h] = hidden
            split_hd[h] = right3(hidden, 0)

    part_blocks = blocks // 2
    halved = dp == 2 and blocks % 2 == 0

    def hidden_parts(p, o):
        if p == 0 and halved:
            rows = pl.ds(pl.multiple_of(o * half, half), half)
            return [(pl.ds(o * part_blocks, part_blocks),), (pl.ds((1 - o) * part_blocks, part_blocks), rows)]
        return [(pl.ds(j * part_blocks, part_blocks),) for j in range(2)]

    def send_hidden(p):
        for k in range(peers):
            for j, at in enumerate(hidden_parts(p, other(k))):
                copies.send(hd.at[(p,) + at], peer_hd.at[(k, p) + at], hd_sem.at[k, p, j], (other(k), t))

    def to_partner(p, rows):
        for r in rows:
            row = flip(q, r, A)
            copies.send(terms.at[row, p, 1 - c], core_box.at[row, p], core_sem.at[row, p], core)

    def spread_far(p, w, axis):
        for k, r in enumerate(far):
            row = flip(q, r, A)

            @pl.loop(0, blocks // U)
            def _(i):
                for j in range(U):
                    h = i * U + j
                    u = h // bps
                    terms[row, p, u % 2, u // 2, h % bps] = contract(
                        left3(weight(w, h, 1 + low_levels + k), axis), split_hd[h], axis, 0
                    )

        to_partner(p, far)

    def spread_near(p, w, axis):
        @pl.loop(0, blocks // U)
        def _(i):
            for j in range(U):
                m = i * U + j
                u = m // bps
                v = contract(left3(weight(w, m, 0), axis), split_hd[m], axis, 0)
                for k in range(low_levels):
                    h = flip(m, 1 << k, blocks)
                    v = v + contract(left3(weight(w, h, 1 + k), axis), split_hd[h], axis, 0)
                terms[q, p, u % 2, u // 2, m % bps] = v

        to_partner(p, [0])

    order = []
    for r in range(A):
        if r % 4 < 2:
            order += [r + 2, r] if A > 2 else [r]

    def to_side(p, some):
        for r in some:
            row = flip(q, r, A)
            theirs = mine(r ^ 1)
            if theirs:
                arrived(core_box.at[row, p], core_sem.at[row, p], core)
            if mine(r) and not theirs:
                src = terms.at[row, p, c, 1 - b]
            elif theirs and not mine(r):
                src = core_box.at[row, p, 1 - b]
            else:
                src = stage.at[row, p]
                if theirs:
                    stage[row, p] = terms[row, p, c, 1 - b] + core_box[row, p, 1 - b]
                else:
                    stage[row, p] = jnp.zeros(stage.shape[2:], f32)
            copies.send(src, side_box.at[row, p], side_sem.at[row, p], side)

    def to_line(p, some):
        for r in some:
            row = flip(q, r, A)
            arrived(side_box.at[row, p], side_sem.at[row, p], side)
            v = side_box[row, p]
            if mine(r):
                v = v + terms[row, p, c, b]
            if mine(r ^ 1):
                v = v + core_box[row, p, b]
            acc[row, p] = v
            k = flip(row, a, A)
            copies.send(
                acc.at[row, p], line_box.at[k, p], line_sem.at[k, p], (d, row * 4 + b * 2 + c), row != a
            )

    def pass_stage(box, sem, places):
        for s in places:
            for k in range(peers):
                arrived(box.at[k, s], sem.at[k, s], core)
                copies.send(box.at[k, s], box.at[k, s], sem.at[k, s], core)

    def passed_stage(box, sem, rows):
        for k in range(peers):
            for row in rows:
                for col in range(2):
                    s = row * 4 + col * 2 + 1 - c
                    arrived(box.at[k, s], sem.at[k, s], core)

    def far_stage():
        for i, r in enumerate(far[1:]):
            row = flip(q, r, A)

            @pl.loop(0, blocks)
            def _(h):
                g = right3(full[row * 4 + h // bps, 1, h % bps], 1)
                for k in range(peers):
                    rows = pl.ds(pl.multiple_of(other(k) * half, half), half)
                    far_part[k, i, h] = contract(left3(hd[0, h, rows, :], 1), g, 1, 1)

        for k in range(peers):
            copies.send(far_part.at[k], far_box.at[k], far_sem.at[k], (other(k), t))

    def far_wait_stage():
        for k in range(peers):
            arrived(far_box.at[k], far_sem.at[k], core)

    def hidden_stage(p):
        for k in range(peers):
            for j, at in enumerate(hidden_parts(p, d)):
                arrived(peer_hd.at[(k, p) + at], hd_sem.at[k, p, j], core)

    here_rows = pl.ds(pl.multiple_of(d * half, half), half)

    def hidden_rows(h):
        rows = [hd[0, h, here_rows, :]] + [peer_hd[k, 0, h, here_rows, :] for k in range(peers)]
        return left3(jnp.concatenate(rows, axis=1), 1)

    def grad_cols(plane, m):
        s = plane * 4 + m // bps
        g = [full[s, 1, m % bps]] + [peer_g[k, s, m % bps] for k in range(peers)]
        return right3(jnp.concatenate(g, axis=1), 1)

    def down_stage():
        @pl.loop(0, blocks)
        def _(m):
            g = grad_cols(q, m)
            left = jnp.concatenate(
                [hidden_rows(m)] + [hidden_rows(flip(m, 1 << k, blocks)) for k in range(low_levels)], axis=0
            )
            v = contract(left, g, 1, 1)
            dpair[m * J] = v[:half]
            for k in range(low_levels):
                dpair[flip(m, 1 << k, blocks) * J + 1 + k] = v[(k + 1) * half : (k + 2) * half]
            dpair[m * J + 1 + low_levels] = contract(hidden_rows(m), grad_cols(flip(q, 1, A), m), 1, 1)
            own_hidden = left3(hd[0, m, here_rows, :], 1)
            for i, r in enumerate(far[1:]):
                g = right3(full[flip(q, r, A) * 4 + m // bps, 1, m % bps], 1)
                v = contract(own_hidden, g, 1, 1)
                for k in range(peers):
                    v = v + far_box[k, i, m]
                dpair[m * J + 2 + low_levels + i] = v

    def data_rows(plane, m):
        s = plane * 4 + m // bps
        x = [full[s, 0, m % bps, here_rows, :]] + [peer_x[k, s, m % bps] for k in range(peers)]
        return left3(jnp.concatenate(x, axis=1), 1)

    def up_stage():
        @pl.loop(0, blocks)
        def _(h):
            back = [hd[1, h]] + [peer_hd[k, 1, h] for k in range(peers)]
            back = right3(jnp.concatenate(back, axis=1), 1)
            left = [data_rows(q, h)] + [data_rows(q, flip(h, 1 << k, blocks)) for k in range(low_levels)]
            left += [data_rows(flip(q, r, A), h) for r in far]
            v = contract(jnp.concatenate(left, axis=0), back, 1, 1)
            for j in range(J):
                upair[h * J + j] = v[j * half : (j + 1) * half]

    def sum_stage():
        for p in range(2):
            v = acc[a, p]
            for k in range(1, A):
                arrived(line_box.at[k, p], line_sem.at[k, p], core)
                v = v + line_box[k, p]
            summed[p] = v

    def own_stage():
        for k in range(peers):
            for j in range(own_rows):
                arrived(peer_own.at[k, j], po_sem.at[k, j], core)

    send_hidden(0)
    keep(hd.at[0], hd_out.at[0])
    for k in range(3, A):
        from_line(1, k)
    spread_far(0, wdn, 0)
    to_side(0, order[:1])
    spread_near(0, wdn, 0)
    to_side(0, order[1:])
    for k in range(1, A):
        from_side(1, k)
    lpart[0] = jnp.zeros((rank, n), f32)
    lpart[1] = jnp.zeros((rank, n), f32)
    from_core(1)
    split_in(1)
    back_mid = right3(red[1], 0)

    @pl.loop(0, blocks // U)
    def _(i):
        for j in range(U):
            h = i * U + j
            lpart[0] += contract(left3(dnl[span(h), :], 0), split_hd[h], 0, 0)
            v = gather_up(1, h, wdn, 1, contract(left3(dnl[span(h), :], 1), back_mid, 1, 0))
            back = v * slope[h]
            hd[1, h] = back
            bs = right3(back, 0)
            split_hd[h] = bs
            lpart[1] += contract(left3(upr[:, span(h)], 1), bs, 1, 0)

    send_hidden(1)
    low_total = Total(
        low, peer_low, dp, d, t, T, lpart, lmid, lown_half, lcore_in, lside_in, lline_in, copies,
        (lone_sem, lline_sem, pl_sem),
    )
    low_total.to_core()
    keep(hd.at[1], hd_out.at[1])
    to_line(0, order[:2])
    spread_far(1, wup, 1)
    low_total.to_side()
    to_side(1, order[:1])
    to_line(0, order[2:])
    spread_near(1, wup, 1)
    to_side(1, order[1:])
    low_total.to_line()
    far_stage()

    pass_stage(peer_x, px_sem, my_places)
    total.pass_peers()
    to_line(1, order[:2])
    pass_stage(peer_g, pg_sem, [row * 4 + col * 2 + c for row in near_rows for col in range(2)])
    for k in range(peers):
        arrived(peer_g.at[k, t], pg_sem.at[k, t], core, (t // 8 < q // 2) | (t // 8 > q // 2))
    passed_stage(peer_x, px_sem, range(A))
    passed_stage(peer_g, pg_sem, near_rows)
    keep(full.at[t], own_out)
    keep(peer_g.at[:, t], peer_g_out)
    to_line(1, order[2:])
    own_stage()
    total.finish_peers()
    keep(red, red_out)
    keep(peer_red, peer_red_out)
    keep(peer_own, peer_own_out)
    hidden_stage(0)
    if halved:
        blocks_here = pl.ds(d * part_blocks, part_blocks)
        keep(peer_hd.at[:, 0, blocks_here], peer_hd_out.at[:, 0, blocks_here])
    else:
        keep(peer_hd.at[:, 0], peer_hd_out.at[:, 0])
    low_total.reduce()
    hidden_stage(1)
    keep(peer_hd.at[:, 1], peer_hd_out.at[:, 1])
    up_stage()
    keep(upair, upair_out)
    low_total.share()
    far_wait_stage()
    down_stage()
    keep(dpair, dpair_out)
    low_total.finish()
    keep(low, low_out)
    low_total.pass_peers()
    sum_stage()
    keep(summed, summed_out)
    low_total.finish_peers()
    keep(peer_low, peer_low_out)
    for copy in kept:
        copy.wait()
    copies.drain()
    if copies.count != send_sem.shape[0]:
        raise ValueError(copies.count, send_sem.shape[0])


def grads_kernel(
    dp, own_in, peer_g, hd, peer_hd,
    peer_own, red, peer_red, low, peer_low, summed, dpair, upair, upl, dnr, ps,
    res, ing, upg, dng, uplg, uprg, dnlg, dnrg,
):
    slots, half, blk = upg.shape
    bps = own_in.shape[1]
    blocks = hd.shape[1]
    d = lax.axis_index("dp")
    peers = range(dp - 1)

    def cat(first, rest):
        return jnp.concatenate([first] + rest, axis=1)

    unroll = 4 if slots % 4 == 0 else 1

    @pl.loop(0, slots // unroll)
    def _(i):
        for j in range(unroll):
            s = i * unroll + j
            p = ps[s]
            keep = (p >= 0).astype(f32)
            p = jnp.maximum(p, 0)
            upg[s] = upair[p] * keep
            dng[s] = dpair[p] * keep

    for j in range(bps):
        span = slice(j * blk, (j + 1) * blk)
        res[:, span] = (summed[0, j] + dot3(dnr[:, span], low[0], 0, 0)).T
        ing[:, span] = (summed[1, j] + dot3(upl[span, :], low[1], 1, 0)).T
    back_in = right3(cat(low[1], [peer_low[k, 1] for k in peers]), 1)
    n = uplg.shape[0]
    step = min(n, blk)
    for j in range(n // step):
        at = d * n + j * step
        inner = pl.ds(pl.multiple_of(at % blk, step), step)
        x = cat(own_in[0, at // blk, inner, :], [peer_own[k, j] for k in peers])
        uplg[j * step : (j + 1) * step, :] = contract(left3(x, 1), back_in, 1, 1)
    n = uprg.shape[0]
    span = pl.ds(pl.multiple_of(d * n, n), n)
    left_in = left3(cat(red[0, span, :], [peer_red[k, 0, span, :] for k in peers]), 1)
    left_mid = left3(cat(low[0, span, :], [peer_low[k, 0, span, :] for k in peers]), 1)
    for h in range(blocks):
        back = cat(hd[1, h], [peer_hd[k, 1, h] for k in peers])
        uprg[:, h * blk : (h + 1) * blk] = contract(left_in, right3(back, 1), 1, 1)
    for j in range(bps):
        g = cat(own_in[1, j], [peer_g[k, j] for k in peers])
        dnrg[:, j * blk : (j + 1) * blk] = contract(left_mid, right3(g, 1), 1, 1)
    back_mid = right3(cat(red[1], [peer_red[k, 1] for k in peers]), 1)
    n = dnlg.shape[0]
    step = min(n, blk)
    for j in range(n // step):
        at = d * n + j * step
        inner = pl.ds(pl.multiple_of(at % blk, step), step)
        hidden = cat(hd[0, at // blk, inner, :], [peer_hd[k, 0, at // blk, inner, :] for k in peers])
        dnlg[j * step : (j + 1) * step, :] = contract(left3(hidden, 1), back_mid, 1, 1)


def shards(
    dp, T,
    inputs, out_grad, up_weight, down_weight, up_left, up_right, down_left, down_right,
    model_block, hidden_block, live_slots,
):
    tokens, feats = inputs.shape
    slots, blk = up_weight.shape[0], up_weight.shape[1]
    width = up_right.shape[1]
    rank = up_left.shape[1]
    blocks = width // blk
    bps = feats // blk
    A = T // 4
    peers = dp - 1
    half = blk // dp
    pairs = blocks * (T * bps).bit_length()
    own = feats // dp
    own_step = min(own, blk)
    own_rows = own // own_step
    DMA = pltpu.SemaphoreType.DMA
    sds = lambda *shape: jax.ShapeDtypeStruct(shape, f32)
    vmem = lambda *shape: pltpu.VMEM(shape, f32)
    bf16 = jnp.bfloat16
    spare = A.bit_length() - 2
    gather = 2 + peers + (A - 1) * (3 + peers) + A * (1 + peers)
    total = 4 + A - 1 + 2 * peers
    scatter = 2 * (1 + A.bit_length() - 1) + 4 * A
    sends = 2 * gather + 5 + 2 * total + scatter + peers * (own_rows + 2 * A + 9)
    outs = pl.pallas_call(
        functools.partial(layer_kernel, dp, T),
        out_shape=(
            sds(2, bps, blk, tokens),
            sds(peers, bps, blk, tokens),
            sds(2, blocks, blk, tokens),
            sds(peers, 2, blocks, blk, tokens),
            sds(peers, own_rows, own_step, tokens),
            sds(2, rank, tokens),
            sds(peers, 2, rank, tokens),
            sds(2, rank, tokens),
            sds(peers, 2, rank, tokens),
            sds(2, bps, blk, tokens),
            sds(pairs, half, blk),
            sds(pairs, half, blk),
            sds(feats, rank),
            sds(rank, feats),
            jax.ShapeDtypeStruct((slots,), jnp.int32),
        ),
        in_specs=[SM] + [HB] * 10,
        out_specs=[pl.BlockSpec(memory_space=pl.ANY)] * 14 + [SM],
        scratch_shapes=[
            vmem(T, 2, bps, blk, tokens),
            vmem(peers, T, bps, blk, tokens),
            vmem(peers, T, bps, half, tokens),
            vmem(2, blocks, blk, tokens),
            vmem(peers, 2, blocks, blk, tokens),
            vmem(peers, own_rows, own_step, tokens),
            vmem(2, rank, tokens),
            vmem(peers, 2, rank, tokens),
            vmem(2, rank, tokens),
            vmem(peers, 2, rank, tokens),
            vmem(2, bps, blk, tokens),
            vmem(pairs, half, blk),
            vmem(pairs, half, blk),
            vmem(feats, rank),
            vmem(rank, feats),
            DMA((17,)),
            pltpu.SMEM((slots,), jnp.int32), pltpu.SMEM((slots,), jnp.int32),
            vmem(tokens, feats), vmem(tokens, feats), vmem(rank, width), vmem(width, rank), DMA((8,)),
            vmem(slots + 1, blk, blk), vmem(slots + 1, blk, blk), DMA((2,)),
            pltpu.VMEM((2, 8, 128), jnp.int32), pltpu.SMEM((2, 8, 128), jnp.int32),
            DMA((1,)),
            vmem(2, rank, tokens), vmem(1, rank, tokens), vmem(rank // 2, tokens), vmem(rank, tokens),
            vmem(rank // 2, tokens), vmem(A, rank // 2, tokens),
            vmem(2, rank, tokens), vmem(1, rank, tokens), vmem(rank // 2, tokens), vmem(rank, tokens),
            vmem(rank // 2, tokens), vmem(A, rank // 2, tokens),
            vmem(blocks, blk, tokens),
            pltpu.VMEM((blocks, 3 * blk, tokens), bf16),
            pltpu.VMEM((blocks, 3 * blk, tokens), bf16),
            vmem(A, 2, 2, 2, bps, blk, tokens),
            vmem(A, 2, 2, bps, blk, tokens),
            vmem(A, 2, bps, blk, tokens),
            vmem(A, 2, bps, blk, tokens),
            vmem(A, 2, bps, blk, tokens),
            vmem(A, 2, bps, blk, tokens),
            vmem(peers, spare, blocks, half, blk), vmem(peers, spare, blocks, half, blk), DMA((peers,)),
            DMA((sends,)), DMA((T, 2)), DMA((peers, T)), DMA((peers, T)), DMA((peers, own_rows)),
            DMA((4,)), DMA((A,)), DMA((peers, 2)),
            DMA((4,)), DMA((A,)), DMA((peers, 2)), DMA((peers, 2, 2)),
            DMA((A, 2)), DMA((A, 2)), DMA((A, 2)),
        ],
        compiler_params=pltpu.CompilerParams(collective_id=0, has_side_effects=True, vmem_limit_bytes=46 << 20),
    )(
        live_slots,
        *(
            pltpu.with_memory_space_constraint(v, pltpu.HBM)
            for v in (
                model_block, hidden_block, inputs, out_grad, up_weight, down_weight,
                up_left, up_right, down_left, down_right,
            )
        )
    )
    return pl.pallas_call(
        functools.partial(grads_kernel, dp),
        out_shape=(
            sds(tokens, feats),
            sds(tokens, feats),
            sds(slots, half, blk),
            sds(slots, half, blk),
            sds(feats // dp, rank),
            sds(rank // dp, width),
            sds(width // dp, rank),
            sds(rank // dp, feats),
        ),
        in_specs=[VM] * 14 + [SM],
        out_specs=[VM] * 8,
        compiler_params=pltpu.CompilerParams(vmem_limit_bytes=24 << 20),
    )(*outs)


def solution(mesh):
    return jax.shard_map(
        functools.partial(shards, mesh.shape["dp"], mesh.shape["tensor"]),
        mesh=mesh,
        in_specs=(
            P("dp", "tensor"),
            P("dp", "tensor"),
            P("tensor", None, None),
            P("tensor", None, None),
            P("tensor", None),
            P(None, "tensor"),
            P("tensor", None),
            P(None, "tensor"),
            P("tensor"),
            P("tensor"),
            P("tensor"),
        ),
        out_specs=(
            P("dp", "tensor"),
            P("dp", "tensor"),
            P("tensor", "dp", None),
            P("tensor", "dp", None),
            P(("tensor", "dp"), None),
            P("dp", "tensor"),
            P(("tensor", "dp"), None),
            P("dp", "tensor"),
        ),
        check_vma=False,
    )
```

```python
import functools

import jax
import jax.numpy as jnp
from jax import lax
from jax.experimental import pallas as pl
from jax.experimental.pallas import tpu as pltpu
from jax.sharding import PartitionSpec as P

MESH = pl.DeviceIdType.MESH
VM = pl.BlockSpec(memory_space=pltpu.VMEM)
HB = pl.BlockSpec(memory_space=pltpu.HBM)
SM = pl.BlockSpec(memory_space=pltpu.SMEM)
f32 = jnp.float32


def halves(v):
    hi = v.astype(jnp.bfloat16)
    lo = (v - hi.astype(f32)).astype(jnp.bfloat16)
    return hi, lo


def left3(v, axis):
    hi, lo = halves(v)
    return jnp.concatenate([hi, hi, lo], axis=axis)


def right3(v, axis):
    hi, lo = halves(v)
    return jnp.concatenate([hi, lo, hi], axis=axis)


def contract(a, b, da, db):
    return lax.dot_general(a, b, (((da,), (db,)), ((), ())), preferred_element_type=f32)


def dot3(a, b, da, db):
    return contract(left3(a, da), right3(b, db), da, db)


def flip(a, k, size):
    out, bit = 0, 1
    while bit < size:
        out = out + (((a // bit) % 2 + (k // bit) % 2) % 2) * bit
        bit *= 2
    return out


class Copies:
    def __init__(self, sems):
        self.sems, self.count, self.made = sems, 0, []

    def send(self, src, dst, recv, where, cond=None):
        sem = self.sems.at[self.count]
        self.count += 1
        copy = pltpu.make_async_remote_copy(
            src_ref=src, dst_ref=dst, send_sem=sem, recv_sem=recv, device_id=where, device_id_type=MESH
        )
        if cond is None:
            copy.start()
        else:
            pl.when(cond)(copy.start)
        self.made.append((copy, cond))

    def drain(self):
        for copy, cond in self.made:
            if cond is None:
                copy.wait_send()
            else:
                pl.when(cond)(copy.wait_send)


def arrived(ref, recv, where, cond=None):
    copy = pltpu.make_async_remote_copy(
        src_ref=ref, dst_ref=ref, send_sem=recv, recv_sem=recv, device_id=where, device_id_type=MESH
    )
    if cond is None:
        copy.wait_recv()
    else:
        pl.when(cond)(copy.wait_recv)


def line_steps(a, A):
    out = [(a, 0, None)]
    for k in range(1, A):
        out.append(((a + A - k) % A, -1, a >= k))
        out.append(((a + k) % A, 1, a + k < A))
    return out


def greet(d, t, dp, T):
    barrier = pltpu.get_barrier_semaphore()
    A = T // 4
    c, b, a = t % 2, (t // 2) % 2, t // 4
    whom = [(d, a * 4 + b * 2 + 1 - c), (d, a * 4 + (1 - b) * 2 + c)]
    whom += [(d, (t + 4 * k) % T) for k in range(1, A)]
    whom += [(lax.rem(d + k, dp), t) for k in range(1, dp)]
    for where in whom:
        pl.semaphore_signal(barrier, inc=1, device_id=where, device_id_type=MESH)
    pl.semaphore_wait(barrier, len(whom))


class Total:
    def __init__(self, out, peer_out, dp, d, t, T, part, mid, mine, core_in, side_in, line_in, copies, sems):
        self.out, self.peer_out, self.dp, self.d, self.t, self.A = out, peer_out, dp, d, t, T // 4
        self.part, self.mid, self.mine, self.core_in, self.side_in, self.line_in = part, mid, mine, core_in, side_in, line_in
        self.copies = copies
        self.one_sem, self.line_sem, self.peer_sem = sems
        self.c, self.b, self.a = t % 2, (t // 2) % 2, t // 4
        self.half = part.shape[1] // 2
        self.core, self.side = (d, self.place(self.a, 0, 1)), (d, self.place(self.a, 1, 0))

    def place(self, row, b, c):
        return row * 4 + (self.b + b) % 2 * 2 + (self.c + c) % 2

    def to_core(self):
        self.copies.send(self.part.at[1 - self.c], self.core_in, self.one_sem.at[0], self.core)

    def to_side(self):
        arrived(self.core_in, self.one_sem.at[0], self.core)
        self.mid[0] = self.part[self.c] + self.core_in[...]
        self.copies.send(self.mid.at[0, self.rows(1 - self.b)], self.side_in, self.one_sem.at[1], self.side)

    def rows(self, b):
        return pl.ds(pl.multiple_of(b * self.half, self.half), self.half)

    def to_line(self):
        arrived(self.side_in, self.one_sem.at[1], self.side)
        self.mine[...] = self.mid[0, self.rows(self.b), :] + self.side_in[...]
        for k in range(1, self.A):
            row = (self.a + k) % self.A
            self.copies.send(
                self.mine, self.line_in.at[self.A - k], self.line_sem.at[self.A - k],
                (self.d, self.place(row, 0, 0)),
            )

    def reduce(self):
        total = self.mine[...]
        for k in range(1, self.A):
            arrived(self.line_in.at[k], self.line_sem.at[k], self.core)
            total = total + self.line_in[k]
        self.out[self.c, self.rows(self.b), :] = total
        piece = self.out.at[self.c, self.rows(self.b)]
        self.copies.send(piece, piece, self.one_sem.at[3], self.side)

    def share(self):
        arrived(self.out.at[self.c, self.rows(1 - self.b)], self.one_sem.at[3], self.side)
        whole = self.out.at[self.c]
        self.copies.send(whole, whole, self.one_sem.at[2], self.core)
        for p in range(self.dp - 1):
            self.copies.send(
                whole, self.peer_out.at[p, self.c], self.peer_sem.at[p, self.c],
                (lax.rem(self.d + p + 1, self.dp), self.t),
            )

    def finish(self):
        arrived(self.out.at[1 - self.c], self.one_sem.at[2], self.core)

    def pass_peers(self):
        for p in range(self.dp - 1):
            box = self.peer_out.at[p, self.c]
            arrived(box, self.peer_sem.at[p, self.c], self.core)
            self.copies.send(box, box, self.peer_sem.at[p, self.c], self.core)

    def finish_peers(self):
        for p in range(self.dp - 1):
            arrived(self.peer_out.at[p, 1 - self.c], self.peer_sem.at[p, 1 - self.c], self.core)


def power(r):
    return r > 0 and r & (r - 1) == 0


def mine(r):
    return r == 0 or power(r)


def pair_of(m, g, levels):
    diff = m ^ g
    return sum((diff >= (1 << k)).astype(jnp.int32) for k in range(levels))


def by_distance(a, A):
    table = [sorted(range(A), key=lambda r: (abs(r - v), r)) for v in range(A)]
    rows = []
    for i in range(A):
        row = table[0][i]
        for v in range(1, A):
            row = jnp.where(a == v, table[v][i], row)
        rows.append(row)
    return rows


def layer_kernel(
    dp, T, live_ref, mb_any, hb_any, inp_any, og_any, upw_ref, dnw_ref, upl_any, upr_any, dnl_any, dnr_any,
    own_out, peer_g_out, hd_out, peer_hd_out, peer_own_out, red_out, peer_red_out,
    low_out, peer_low_out, summed_out, dpair_out, upair_out, upl_out, dnr_out, ps,
    full, peer_g, peer_x, hd, peer_hd, peer_own, red, peer_red, low, peer_low, summed, dpair, upair, upl_ref, dnr_ref, keep_sem,
    mb_ref, hb_ref, inp_ref, og_ref, upr, dnl, small_sem,
    wup, wdn, wsem, idx_v, idx_s, isem,
    part, mid, own_half, core_in, side_in, line_in, lpart, lmid, lown_half, lcore_in, lside_in, lline_in, slope, split_x, split_hd,
    terms, core_box, stage, side_box, acc, line_box, far_part, far_box, far_sem,
    send_sem, full_sem, pg_sem, px_sem, po_sem, one_sem, tline_sem, pr_sem,
    lone_sem, lline_sem, pl_sem, hd_sem, core_sem, side_sem, line_sem,
):
    d, t = lax.axis_index("dp"), lax.axis_index("tensor")
    c, b, a = t % 2, (t // 2) % 2, t // 4
    A = T // 4
    q = t % A
    slots, blk = upw_ref.shape[0], upw_ref.shape[1]
    bps, n = full.shape[2], full.shape[4]
    blocks = hd.shape[1]
    rank = red.shape[1]
    half = dpair.shape[1]
    total_blocks = T * bps
    levels = total_blocks.bit_length() - 1
    low_levels = blocks.bit_length() - 1
    J = levels + 1
    U = 4 if blocks % 4 == 0 else 1
    V = 2 if blocks % 2 == 0 else 1
    peers = dp - 1
    core, side = (d, a * 4 + b * 2 + 1 - c), (d, a * 4 + (1 - b) * 2 + c)
    copies = Copies(send_sem)
    kept = []

    def keep(src, dst):
        copy = pltpu.make_async_copy(src, dst, keep_sem.at[len(kept)])
        copy.start()
        kept.append(copy)

    pairs = (
        (inp_any, inp_ref), (og_any, og_ref), (upl_any, upl_ref), (dnr_any, dnr_ref),
        (mb_any, mb_ref), (hb_any, hb_ref), (upr_any, upr), (dnl_any, dnl),
    )
    loads = [pltpu.make_async_copy(src, dst, small_sem.at[i]) for i, (src, dst) in enumerate(pairs)]
    for load in loads:
        load.start()
    load_up = pltpu.make_async_copy(upw_ref, wup.at[pl.ds(0, slots)], wsem.at[0])
    load_dn = pltpu.make_async_copy(dnw_ref, wdn.at[pl.ds(0, slots)], wsem.at[1])
    load_up.start()
    load_dn.start()
    loads[0].wait()
    loads[1].wait()
    for j in range(bps):
        full[t, 0, j] = inp_ref[:, j * blk : (j + 1) * blk].T
        full[t, 1, j] = og_ref[:, j * blk : (j + 1) * blk].T
    loads[2].wait()
    loads[3].wait()
    part[0] = dot3(upl_ref[...], full[t, 0].reshape(bps * blk, n), 0, 0)
    part[1] = dot3(dnr_ref[...], full[t, 1].reshape(bps * blk, n), 1, 0)
    greet(d, t, dp, T)

    def other(k):
        return lax.rem(d + k + 1, dp)

    def send(i, s, where, cond=None):
        copies.send(full.at[s, i], full.at[s, i], full_sem.at[s, i], where, cond)

    def got(i, s, where, cond=None):
        arrived(full.at[s, i], full_sem.at[s, i], where, cond)

    def across(i, s, cond=None):
        for k in range(peers):
            o = other(k)
            if i:
                copies.send(full.at[s, 1], peer_g.at[k, s], pg_sem.at[k, s], (o, t), cond)
            else:
                rows = pl.ds(pl.multiple_of(o * half, half), half)
                copies.send(full.at[s, 0, :, rows, :], peer_x.at[k, s], px_sem.at[k, s], (o, t), cond)

    own_rows = peer_own.shape[1]

    rows_near = by_distance(a, A)

    def gap(row):
        return jnp.where(row > a, row - a, a - row)

    at_end = (a == 0) | (a == A - 1)
    at_middle = (a > 0) & (a < A - 1)

    def down_line(i, rows, cond):
        for row in rows:
            send(i, t, (d, row * 4 + b * 2 + c), cond)

    def near(s):
        return s // 8 == q // 2

    near_rows = [q // 2 * 2, q // 2 * 2 + 1]

    def place(k, col):
        return rows_near[k] * 4 + col * 2 + c

    def from_line(i, k):
        s = place(k, b)
        got(i, s, side)
        onward = jnp.where(rows_near[k] > a, a - 1, a + 1)
        inside = (onward >= 0) & (onward < A)
        send(i, s, (d, lax.rem(onward + A, A) * 4 + b * 2 + c), inside)
        send(i, s, side)
        across(i, s, near(s) if i else None)
        send(i, s, core)

    def from_side(i, k):
        s = place(k, 1 - b)
        got(i, s, side)
        across(i, s, near(s) if i else None)
        send(i, s, core)

    my_places = [t, place(0, 1 - b)]
    for k in range(1, A):
        my_places += [place(k, b), place(k, 1 - b)]

    total = Total(
        red, peer_red, dp, d, t, T, part, mid, own_half, core_in, side_in, line_in, copies,
        (one_sem, tline_sem, pr_sem),
    )
    total.to_core()
    down_line(0, rows_near[1:2], None)
    down_line(0, rows_near[2:3], at_middle)
    across(0, t)
    total.to_side()
    send(0, t, side)
    send(0, t, core)
    total.to_line()
    send(1, t, side)
    across(1, t)
    send(1, t, core)
    for k in range(peers):
        o = other(k)
        at = o * own_rows * peer_own.shape[2]
        for j in range(own_rows):
            pos = at + j * peer_own.shape[2]
            inner = pl.ds(pl.multiple_of(pos % blk, peer_own.shape[2]), peer_own.shape[2])
            copies.send(full.at[t, 0, pos // blk, inner, :], peer_own.at[k, j], po_sem.at[k, j], (o, t))

    for load in loads[4:]:
        load.wait()

    lane = lax.broadcasted_iota(jnp.int32, (8, 128), 1)
    wide = 8 if slots % 8 == 0 else 1

    def number(s, v):
        h = hb_ref[s]
        p = h * J + pair_of(mb_ref[s], (t * blocks + h) % total_blocks, levels)
        p = jnp.where(s < live_ref[0], p, -1)
        ps[s] = p
        return jnp.where(lane == s, p, v)

    row_of = lax.fori_loop(0, slots, number, jnp.full((8, 128), -2, jnp.int32), unroll=wide)

    def link(s, v):
        prev, last = v
        p = ps[s]
        prev = jnp.where((lane > s) & (row_of == p), s, prev)
        last = jnp.where(lane == p, s, last)
        return prev, last

    none = jnp.full((8, 128), slots, jnp.int32)
    prev, last = lax.fori_loop(0, slots, link, (none, none), unroll=wide)
    idx_v[0] = prev
    idx_v[1] = last
    to_scalar = pltpu.make_async_copy(idx_v, idx_s, isem.at[0])
    to_scalar.start()
    keep(upl_ref, upl_out)
    keep(dnr_ref, dnr_out)
    from_line(0, 1)
    down_line(1, rows_near[1:2], at_end)
    from_side(0, 0)
    for k in range(2, A):
        from_line(0, k)
    down_line(1, rows_near[1:3], at_middle)
    total.reduce()
    from_side(0, 1)
    from_side(1, 0)
    from_side(0, 2)
    from_line(1, 1)
    for k in range(3, A):
        from_side(0, k)
    to_scalar.wait()
    load_up.wait()
    load_dn.wait()
    wup[slots] = jnp.zeros((blk, blk), f32)
    wdn[slots] = jnp.zeros((blk, blk), f32)

    @pl.loop(0, slots)
    def _(s):
        before_it = idx_s[0, 0, s]
        wup[s] = wup[s] + wup[before_it]
        wdn[s] = wdn[s] + wdn[before_it]

    from_line(1, 2)
    total.share()

    def from_core(i):
        for k in range(2 * A):
            got(i, k * 2 + 1 - c, core)

    far = [1 << k for k in range(levels - low_levels)]

    def weight(w, h, j):
        return w[idx_s[1, 0, h * J + j]]

    def split_in(i):
        @pl.loop(0, blocks)
        def _(m):
            split_x[m] = right3(full[q * 4 + m // bps, i, m % bps], 0)

    def gather_up(i, h, w, axis, start):
        v = start + contract(left3(weight(w, h, 0), axis), split_x[h], axis, 0)
        for k in range(low_levels):
            v = v + contract(left3(weight(w, h, 1 + k), axis), split_x[flip(h, 1 << k, blocks)], axis, 0)
        for k, r in enumerate(far):
            x = right3(full[flip(q, r, A) * 4 + h // bps, i, h % bps], 0)
            v = v + contract(left3(weight(w, h, 1 + low_levels + k), axis), x, axis, 0)
        return v

    def span(h):
        return pl.ds(pl.multiple_of(h * blk, blk), blk)

    from_core(0)
    total.finish()
    split_in(0)
    low_in = right3(red[0], 0)
    scale = 0.7978845608028654

    @pl.loop(0, blocks // U)
    def _(i):
        for j in range(U):
            h = i * U + j
            v = gather_up(0, h, wup, 0, contract(left3(upr[:, span(h)], 0), low_in, 0, 0))
            th = jnp.tanh(scale * (v + 0.044715 * (v * v * v)))
            hidden = 0.5 * v * (1.0 + th)
            slope[h] = 0.5 * (1.0 + th) + 0.5 * v * (1.0 - th * th) * (scale * (1.0 + 3 * 0.044715 * (v * v)))
            hd[0, h] = hidden
            split_hd[h] = right3(hidden, 0)

    part_blocks = blocks // 2
    halved = dp == 2 and blocks % 2 == 0

    def hidden_parts(p, o):
        if p == 0 and halved:
            rows = pl.ds(pl.multiple_of(o * half, half), half)
            return [(pl.ds(o * part_blocks, part_blocks),), (pl.ds((1 - o) * part_blocks, part_blocks), rows)]
        return [(pl.ds(j * part_blocks, part_blocks),) for j in range(2)]

    def send_hidden(p):
        for k in range(peers):
            for j, at in enumerate(hidden_parts(p, other(k))):
                copies.send(hd.at[(p,) + at], peer_hd.at[(k, p) + at], hd_sem.at[k, p, j], (other(k), t))

    def to_partner(p, rows):
        for r in rows:
            row = flip(q, r, A)
            copies.send(terms.at[row, p, 1 - c], core_box.at[row, p], core_sem.at[row, p], core)

    def spread_far(p, w, axis):
        rows = [flip(q, r, A) for r in far]

        @pl.loop(0, blocks // U)
        def _(i):
            for j in range(U):
                h = i * U + j
                u = h // bps
                for k, row in enumerate(rows):
                    terms[row, p, u % 2, u // 2, h % bps] = contract(
                        left3(weight(w, h, 1 + low_levels + k), axis), split_hd[h], axis, 0
                    )

        to_partner(p, far)

    def spread_near(p, w, axis):
        @pl.loop(0, blocks // U)
        def _(i):
            for j in range(U):
                m = i * U + j
                u = m // bps
                v = contract(left3(weight(w, m, 0), axis), split_hd[m], axis, 0)
                for k in range(low_levels):
                    h = flip(m, 1 << k, blocks)
                    v = v + contract(left3(weight(w, h, 1 + k), axis), split_hd[h], axis, 0)
                terms[q, p, u % 2, u // 2, m % bps] = v

        to_partner(p, [0])

    order = []
    for r in range(A):
        if r % 4 < 2:
            order += [r + 2, r] if A > 2 else [r]

    def to_side(p, some):
        for r in some:
            row = flip(q, r, A)
            theirs = mine(r ^ 1)
            if theirs:
                arrived(core_box.at[row, p], core_sem.at[row, p], core)
            if mine(r) and not theirs:
                src = terms.at[row, p, c, 1 - b]
            elif theirs and not mine(r):
                src = core_box.at[row, p, 1 - b]
            else:
                src = stage.at[row, p]
                if theirs:
                    stage[row, p] = terms[row, p, c, 1 - b] + core_box[row, p, 1 - b]
                else:
                    stage[row, p] = jnp.zeros(stage.shape[2:], f32)
            copies.send(src, side_box.at[row, p], side_sem.at[row, p], side)

    def to_line(p, some):
        for r in some:
            row = flip(q, r, A)
            arrived(side_box.at[row, p], side_sem.at[row, p], side)
            v = side_box[row, p]
            if mine(r):
                v = v + terms[row, p, c, b]
            if mine(r ^ 1):
                v = v + core_box[row, p, b]
            acc[row, p] = v
            k = flip(row, a, A)
            copies.send(
                acc.at[row, p], line_box.at[k, p], line_sem.at[k, p], (d, row * 4 + b * 2 + c), row != a
            )

    def pass_stage(box, sem, places):
        for s in places:
            for k in range(peers):
                arrived(box.at[k, s], sem.at[k, s], core)
                copies.send(box.at[k, s], box.at[k, s], sem.at[k, s], core)

    def passed_stage(box, sem, rows):
        for k in range(peers):
            for row in rows:
                for col in range(2):
                    s = row * 4 + col * 2 + 1 - c
                    arrived(box.at[k, s], sem.at[k, s], core)

    def far_stage():
        for i, r in enumerate(far[1:]):
            row = flip(q, r, A)

            @pl.loop(0, blocks)
            def _(h):
                g = right3(full[row * 4 + h // bps, 1, h % bps], 1)
                for k in range(peers):
                    rows = pl.ds(pl.multiple_of(other(k) * half, half), half)
                    far_part[k, i, h] = contract(left3(hd[0, h, rows, :], 1), g, 1, 1)

        for k in range(peers):
            copies.send(far_part.at[k], far_box.at[k], far_sem.at[k], (other(k), t))

    def far_wait_stage():
        for k in range(peers):
            arrived(far_box.at[k], far_sem.at[k], core)

    def hidden_stage(p):
        for k in range(peers):
            for j, at in enumerate(hidden_parts(p, d)):
                arrived(peer_hd.at[(k, p) + at], hd_sem.at[k, p, j], core)

    here_rows = pl.ds(pl.multiple_of(d * half, half), half)

    def hidden_rows(h):
        rows = [hd[0, h, here_rows, :]] + [peer_hd[k, 0, h, here_rows, :] for k in range(peers)]
        return left3(jnp.concatenate(rows, axis=1), 1)

    def grad_cols(plane, m):
        s = plane * 4 + m // bps
        g = [full[s, 1, m % bps]] + [peer_g[k, s, m % bps] for k in range(peers)]
        return right3(jnp.concatenate(g, axis=1), 1)

    def down_stage():
        def one(m):
            g = grad_cols(q, m)
            left = jnp.concatenate(
                [hidden_rows(m)] + [hidden_rows(flip(m, 1 << k, blocks)) for k in range(low_levels)], axis=0
            )
            v = contract(left, g, 1, 1)
            dpair[m * J] = v[:half]
            for k in range(low_levels):
                dpair[flip(m, 1 << k, blocks) * J + 1 + k] = v[(k + 1) * half : (k + 2) * half]
            dpair[m * J + 1 + low_levels] = contract(hidden_rows(m), grad_cols(flip(q, 1, A), m), 1, 1)
            own_hidden = left3(hd[0, m, here_rows, :], 1)
            for i, r in enumerate(far[1:]):
                g = right3(full[flip(q, r, A) * 4 + m // bps, 1, m % bps], 1)
                v = contract(own_hidden, g, 1, 1)
                for k in range(peers):
                    v = v + far_box[k, i, m]
                dpair[m * J + 2 + low_levels + i] = v

        @pl.loop(0, blocks // V)
        def _(i):
            for j in range(V):
                one(i * V + j)

    def data_rows(plane, m):
        s = plane * 4 + m // bps
        x = [full[s, 0, m % bps, here_rows, :]] + [peer_x[k, s, m % bps] for k in range(peers)]
        return left3(jnp.concatenate(x, axis=1), 1)

    def up_stage():
        def one(h):
            back = [hd[1, h]] + [peer_hd[k, 1, h] for k in range(peers)]
            back = right3(jnp.concatenate(back, axis=1), 1)
            left = [data_rows(q, h)] + [data_rows(q, flip(h, 1 << k, blocks)) for k in range(low_levels)]
            left += [data_rows(flip(q, r, A), h) for r in far]
            v = contract(jnp.concatenate(left, axis=0), back, 1, 1)
            for j in range(J):
                upair[h * J + j] = v[j * half : (j + 1) * half]

        @pl.loop(0, blocks // V)
        def _(i):
            for j in range(V):
                one(i * V + j)

    def sum_stage():
        for p in range(2):
            v = acc[a, p]
            for k in range(1, A):
                arrived(line_box.at[k, p], line_sem.at[k, p], core)
                v = v + line_box[k, p]
            summed[p] = v

    def own_stage():
        for k in range(peers):
            for j in range(own_rows):
                arrived(peer_own.at[k, j], po_sem.at[k, j], core)

    send_hidden(0)
    keep(hd.at[0], hd_out.at[0])
    for k in range(3, A):
        from_line(1, k)
    spread_far(0, wdn, 0)
    to_side(0, order[:1])
    spread_near(0, wdn, 0)
    to_side(0, order[1:])
    for k in range(1, A):
        from_side(1, k)
    lpart[0] = jnp.zeros((rank, n), f32)
    lpart[1] = jnp.zeros((rank, n), f32)
    from_core(1)
    split_in(1)
    back_mid = right3(red[1], 0)

    @pl.loop(0, blocks // U)
    def _(i):
        for j in range(U):
            h = i * U + j
            lpart[0] += contract(left3(dnl[span(h), :], 0), split_hd[h], 0, 0)
            v = gather_up(1, h, wdn, 1, contract(left3(dnl[span(h), :], 1), back_mid, 1, 0))
            back = v * slope[h]
            hd[1, h] = back
            bs = right3(back, 0)
            split_hd[h] = bs
            lpart[1] += contract(left3(upr[:, span(h)], 1), bs, 1, 0)

    send_hidden(1)
    low_total = Total(
        low, peer_low, dp, d, t, T, lpart, lmid, lown_half, lcore_in, lside_in, lline_in, copies,
        (lone_sem, lline_sem, pl_sem),
    )
    low_total.to_core()
    keep(hd.at[1], hd_out.at[1])
    to_line(0, order[:2])
    spread_far(1, wup, 1)
    low_total.to_side()
    to_side(1, order[:1])
    spread_near(1, wup, 1)
    to_line(0, order[2:])
    to_side(1, order[1:])
    low_total.to_line()
    far_stage()

    pass_stage(peer_x, px_sem, my_places)
    total.pass_peers()
    to_line(1, order[:2])
    pass_stage(peer_g, pg_sem, [row * 4 + col * 2 + c for row in near_rows for col in range(2)])
    for k in range(peers):
        arrived(peer_g.at[k, t], pg_sem.at[k, t], core, (t // 8 < q // 2) | (t // 8 > q // 2))
    passed_stage(peer_x, px_sem, range(A))
    passed_stage(peer_g, pg_sem, near_rows)
    keep(full.at[t], own_out)
    keep(peer_g.at[:, t], peer_g_out)
    to_line(1, order[2:])
    own_stage()
    total.finish_peers()
    keep(red, red_out)
    keep(peer_red, peer_red_out)
    keep(peer_own, peer_own_out)
    hidden_stage(0)
    if halved:
        blocks_here = pl.ds(d * part_blocks, part_blocks)
        keep(peer_hd.at[:, 0, blocks_here], peer_hd_out.at[:, 0, blocks_here])
    else:
        keep(peer_hd.at[:, 0], peer_hd_out.at[:, 0])
    low_total.reduce()
    hidden_stage(1)
    keep(peer_hd.at[:, 1], peer_hd_out.at[:, 1])
    up_stage()
    keep(upair, upair_out)
    low_total.share()
    far_wait_stage()
    down_stage()
    keep(dpair, dpair_out)
    low_total.finish()
    keep(low, low_out)
    low_total.pass_peers()
    sum_stage()
    keep(summed, summed_out)
    low_total.finish_peers()
    keep(peer_low, peer_low_out)
    for copy in kept:
        copy.wait()
    copies.drain()
    if copies.count != send_sem.shape[0]:
        raise ValueError(copies.count, send_sem.shape[0])


def grads_kernel(
    dp, own_in, peer_g, hd, peer_hd,
    peer_own, red, peer_red, low, peer_low, summed, dpair, upair, upl, dnr, ps,
    res, ing, upg, dng, uplg, uprg, dnlg, dnrg,
):
    slots, half, blk = upg.shape
    bps = own_in.shape[1]
    blocks = hd.shape[1]
    d = lax.axis_index("dp")
    peers = range(dp - 1)

    def cat(first, rest):
        return jnp.concatenate([first] + rest, axis=1)

    unroll = 4 if slots % 4 == 0 else 1

    @pl.loop(0, slots // unroll)
    def _(i):
        for j in range(unroll):
            s = i * unroll + j
            p = ps[s]
            keep = (p >= 0).astype(f32)
            p = jnp.maximum(p, 0)
            upg[s] = upair[p] * keep
            dng[s] = dpair[p] * keep

    for j in range(bps):
        span = slice(j * blk, (j + 1) * blk)
        res[:, span] = (summed[0, j] + dot3(dnr[:, span], low[0], 0, 0)).T
        ing[:, span] = (summed[1, j] + dot3(upl[span, :], low[1], 1, 0)).T
    back_in = right3(cat(low[1], [peer_low[k, 1] for k in peers]), 1)
    n = uplg.shape[0]
    step = min(n, blk)
    for j in range(n // step):
        at = d * n + j * step
        inner = pl.ds(pl.multiple_of(at % blk, step), step)
        x = cat(own_in[0, at // blk, inner, :], [peer_own[k, j] for k in peers])
        uplg[j * step : (j + 1) * step, :] = contract(left3(x, 1), back_in, 1, 1)
    n = uprg.shape[0]
    span = pl.ds(pl.multiple_of(d * n, n), n)
    left_in = left3(cat(red[0, span, :], [peer_red[k, 0, span, :] for k in peers]), 1)
    left_mid = left3(cat(low[0, span, :], [peer_low[k, 0, span, :] for k in peers]), 1)
    for h in range(blocks):
        back = cat(hd[1, h], [peer_hd[k, 1, h] for k in peers])
        uprg[:, h * blk : (h + 1) * blk] = contract(left_in, right3(back, 1), 1, 1)
    for j in range(bps):
        g = cat(own_in[1, j], [peer_g[k, j] for k in peers])
        dnrg[:, j * blk : (j + 1) * blk] = contract(left_mid, right3(g, 1), 1, 1)
    back_mid = right3(cat(red[1], [peer_red[k, 1] for k in peers]), 1)
    n = dnlg.shape[0]
    step = min(n, blk)
    for j in range(n // step):
        at = d * n + j * step
        inner = pl.ds(pl.multiple_of(at % blk, step), step)
        hidden = cat(hd[0, at // blk, inner, :], [peer_hd[k, 0, at // blk, inner, :] for k in peers])
        dnlg[j * step : (j + 1) * step, :] = contract(left3(hidden, 1), back_mid, 1, 1)


def shards(
    dp, T,
    inputs, out_grad, up_weight, down_weight, up_left, up_right, down_left, down_right,
    model_block, hidden_block, live_slots,
):
    tokens, feats = inputs.shape
    slots, blk = up_weight.shape[0], up_weight.shape[1]
    width = up_right.shape[1]
    rank = up_left.shape[1]
    blocks = width // blk
    bps = feats // blk
    A = T // 4
    peers = dp - 1
    half = blk // dp
    pairs = blocks * (T * bps).bit_length()
    own = feats // dp
    own_step = min(own, blk)
    own_rows = own // own_step
    DMA = pltpu.SemaphoreType.DMA
    sds = lambda *shape: jax.ShapeDtypeStruct(shape, f32)
    vmem = lambda *shape: pltpu.VMEM(shape, f32)
    bf16 = jnp.bfloat16
    spare = A.bit_length() - 2
    gather = 2 + peers + (A - 1) * (3 + peers) + A * (1 + peers)
    total = 4 + A - 1 + 2 * peers
    scatter = 2 * (1 + A.bit_length() - 1) + 4 * A
    sends = 2 * gather + 5 + 2 * total + scatter + peers * (own_rows + 2 * A + 9)
    outs = pl.pallas_call(
        functools.partial(layer_kernel, dp, T),
        out_shape=(
            sds(2, bps, blk, tokens),
            sds(peers, bps, blk, tokens),
            sds(2, blocks, blk, tokens),
            sds(peers, 2, blocks, blk, tokens),
            sds(peers, own_rows, own_step, tokens),
            sds(2, rank, tokens),
            sds(peers, 2, rank, tokens),
            sds(2, rank, tokens),
            sds(peers, 2, rank, tokens),
            sds(2, bps, blk, tokens),
            sds(pairs, half, blk),
            sds(pairs, half, blk),
            sds(feats, rank),
            sds(rank, feats),
            jax.ShapeDtypeStruct((slots,), jnp.int32),
        ),
        in_specs=[SM] + [HB] * 10,
        out_specs=[pl.BlockSpec(memory_space=pl.ANY)] * 14 + [SM],
        scratch_shapes=[
            vmem(T, 2, bps, blk, tokens),
            vmem(peers, T, bps, blk, tokens),
            vmem(peers, T, bps, half, tokens),
            vmem(2, blocks, blk, tokens),
            vmem(peers, 2, blocks, blk, tokens),
            vmem(peers, own_rows, own_step, tokens),
            vmem(2, rank, tokens),
            vmem(peers, 2, rank, tokens),
            vmem(2, rank, tokens),
            vmem(peers, 2, rank, tokens),
            vmem(2, bps, blk, tokens),
            vmem(pairs, half, blk),
            vmem(pairs, half, blk),
            vmem(feats, rank),
            vmem(rank, feats),
            DMA((17,)),
            pltpu.SMEM((slots,), jnp.int32), pltpu.SMEM((slots,), jnp.int32),
            vmem(tokens, feats), vmem(tokens, feats), vmem(rank, width), vmem(width, rank), DMA((8,)),
            vmem(slots + 1, blk, blk), vmem(slots + 1, blk, blk), DMA((2,)),
            pltpu.VMEM((2, 8, 128), jnp.int32), pltpu.SMEM((2, 8, 128), jnp.int32),
            DMA((1,)),
            vmem(2, rank, tokens), vmem(1, rank, tokens), vmem(rank // 2, tokens), vmem(rank, tokens),
            vmem(rank // 2, tokens), vmem(A, rank // 2, tokens),
            vmem(2, rank, tokens), vmem(1, rank, tokens), vmem(rank // 2, tokens), vmem(rank, tokens),
            vmem(rank // 2, tokens), vmem(A, rank // 2, tokens),
            vmem(blocks, blk, tokens),
            pltpu.VMEM((blocks, 3 * blk, tokens), bf16),
            pltpu.VMEM((blocks, 3 * blk, tokens), bf16),
            vmem(A, 2, 2, 2, bps, blk, tokens),
            vmem(A, 2, 2, bps, blk, tokens),
            vmem(A, 2, bps, blk, tokens),
            vmem(A, 2, bps, blk, tokens),
            vmem(A, 2, bps, blk, tokens),
            vmem(A, 2, bps, blk, tokens),
            vmem(peers, spare, blocks, half, blk), vmem(peers, spare, blocks, half, blk), DMA((peers,)),
            DMA((sends,)), DMA((T, 2)), DMA((peers, T)), DMA((peers, T)), DMA((peers, own_rows)),
            DMA((4,)), DMA((A,)), DMA((peers, 2)),
            DMA((4,)), DMA((A,)), DMA((peers, 2)), DMA((peers, 2, 2)),
            DMA((A, 2)), DMA((A, 2)), DMA((A, 2)),
        ],
        compiler_params=pltpu.CompilerParams(collective_id=0, has_side_effects=True, vmem_limit_bytes=46 << 20),
    )(
        live_slots,
        *(
            pltpu.with_memory_space_constraint(v, pltpu.HBM)
            for v in (
                model_block, hidden_block, inputs, out_grad, up_weight, down_weight,
                up_left, up_right, down_left, down_right,
            )
        )
    )
    return pl.pallas_call(
        functools.partial(grads_kernel, dp),
        out_shape=(
            sds(tokens, feats),
            sds(tokens, feats),
            sds(slots, half, blk),
            sds(slots, half, blk),
            sds(feats // dp, rank),
            sds(rank // dp, width),
            sds(width // dp, rank),
            sds(rank // dp, feats),
        ),
        in_specs=[VM] * 14 + [SM],
        out_specs=[VM] * 8,
        compiler_params=pltpu.CompilerParams(vmem_limit_bytes=24 << 20),
    )(*outs)


def solution(mesh):
    return jax.shard_map(
        functools.partial(shards, mesh.shape["dp"], mesh.shape["tensor"]),
        mesh=mesh,
        in_specs=(
            P("dp", "tensor"),
            P("dp", "tensor"),
            P("tensor", None, None),
            P("tensor", None, None),
            P("tensor", None),
            P(None, "tensor"),
            P("tensor", None),
            P(None, "tensor"),
            P("tensor"),
            P("tensor"),
            P("tensor"),
        ),
        out_specs=(
            P("dp", "tensor"),
            P("dp", "tensor"),
            P("tensor", "dp", None),
            P("tensor", "dp", None),
            P(("tensor", "dp"), None),
            P("dp", "tensor"),
            P(("tensor", "dp"), None),
            P("dp", "tensor"),
        ),
        check_vma=False,
    )
```

```python
import functools

import jax
import jax.numpy as jnp
from jax import lax
from jax.experimental import pallas as pl
from jax.experimental.pallas import tpu as pltpu
from jax.sharding import PartitionSpec as P

MESH = pl.DeviceIdType.MESH
VM = pl.BlockSpec(memory_space=pltpu.VMEM)
HB = pl.BlockSpec(memory_space=pltpu.HBM)
SM = pl.BlockSpec(memory_space=pltpu.SMEM)
f32 = jnp.float32


def halves(v):
    hi = v.astype(jnp.bfloat16)
    lo = (v - hi.astype(f32)).astype(jnp.bfloat16)
    return hi, lo


def left3(v, axis):
    hi, lo = halves(v)
    return jnp.concatenate([hi, hi, lo], axis=axis)


def right3(v, axis):
    hi, lo = halves(v)
    return jnp.concatenate([hi, lo, hi], axis=axis)


def contract(a, b, da, db):
    return lax.dot_general(a, b, (((da,), (db,)), ((), ())), preferred_element_type=f32)


def dot3(a, b, da, db):
    return contract(left3(a, da), right3(b, db), da, db)


def flip(a, k, size):
    out, bit = 0, 1
    while bit < size:
        out = out + (((a // bit) % 2 + (k // bit) % 2) % 2) * bit
        bit *= 2
    return out


class Copies:
    def __init__(self, sems):
        self.sems, self.count, self.made = sems, 0, []

    def send(self, src, dst, recv, where, cond=None):
        sem = self.sems.at[self.count]
        self.count += 1
        copy = pltpu.make_async_remote_copy(
            src_ref=src, dst_ref=dst, send_sem=sem, recv_sem=recv, device_id=where, device_id_type=MESH
        )
        if cond is None:
            copy.start()
        else:
            pl.when(cond)(copy.start)
        self.made.append((copy, cond))

    def drain(self):
        for copy, cond in self.made:
            if cond is None:
                copy.wait_send()
            else:
                pl.when(cond)(copy.wait_send)


def arrived(ref, recv, where, cond=None):
    copy = pltpu.make_async_remote_copy(
        src_ref=ref, dst_ref=ref, send_sem=recv, recv_sem=recv, device_id=where, device_id_type=MESH
    )
    if cond is None:
        copy.wait_recv()
    else:
        pl.when(cond)(copy.wait_recv)


def line_steps(a, A):
    out = [(a, 0, None)]
    for k in range(1, A):
        out.append(((a + A - k) % A, -1, a >= k))
        out.append(((a + k) % A, 1, a + k < A))
    return out


def greet(d, t, dp, T):
    barrier = pltpu.get_barrier_semaphore()
    A = T // 4
    c, b, a = t % 2, (t // 2) % 2, t // 4
    whom = [(d, a * 4 + b * 2 + 1 - c), (d, a * 4 + (1 - b) * 2 + c)]
    whom += [(d, (t + 4 * k) % T) for k in range(1, A)]
    whom += [(lax.rem(d + k, dp), t) for k in range(1, dp)]
    for where in whom:
        pl.semaphore_signal(barrier, inc=1, device_id=where, device_id_type=MESH)
    pl.semaphore_wait(barrier, len(whom))


class Total:
    def __init__(self, out, peer_out, dp, d, t, T, part, mid, mine, core_in, side_in, line_in, copies, sems):
        self.out, self.peer_out, self.dp, self.d, self.t, self.A = out, peer_out, dp, d, t, T // 4
        self.part, self.mid, self.mine, self.core_in, self.side_in, self.line_in = part, mid, mine, core_in, side_in, line_in
        self.copies = copies
        self.one_sem, self.line_sem, self.peer_sem = sems
        self.c, self.b, self.a = t % 2, (t // 2) % 2, t // 4
        self.half = part.shape[1] // 2
        self.core, self.side = (d, self.place(self.a, 0, 1)), (d, self.place(self.a, 1, 0))

    def place(self, row, b, c):
        return row * 4 + (self.b + b) % 2 * 2 + (self.c + c) % 2

    def to_core(self):
        self.copies.send(self.part.at[1 - self.c], self.core_in, self.one_sem.at[0], self.core)

    def to_side(self):
        arrived(self.core_in, self.one_sem.at[0], self.core)
        self.mid[0] = self.part[self.c] + self.core_in[...]
        self.copies.send(self.mid.at[0, self.rows(1 - self.b)], self.side_in, self.one_sem.at[1], self.side)

    def rows(self, b):
        return pl.ds(pl.multiple_of(b * self.half, self.half), self.half)

    def to_line(self):
        arrived(self.side_in, self.one_sem.at[1], self.side)
        self.mine[...] = self.mid[0, self.rows(self.b), :] + self.side_in[...]
        for k in range(1, self.A):
            row = (self.a + k) % self.A
            self.copies.send(
                self.mine, self.line_in.at[self.A - k], self.line_sem.at[self.A - k],
                (self.d, self.place(row, 0, 0)),
            )

    def reduce(self):
        total = self.mine[...]
        for k in range(1, self.A):
            arrived(self.line_in.at[k], self.line_sem.at[k], self.core)
            total = total + self.line_in[k]
        self.out[self.c, self.rows(self.b), :] = total
        piece = self.out.at[self.c, self.rows(self.b)]
        self.copies.send(piece, piece, self.one_sem.at[3], self.side)

    def share(self):
        arrived(self.out.at[self.c, self.rows(1 - self.b)], self.one_sem.at[3], self.side)
        whole = self.out.at[self.c]
        self.copies.send(whole, whole, self.one_sem.at[2], self.core)
        for p in range(self.dp - 1):
            self.copies.send(
                whole, self.peer_out.at[p, self.c], self.peer_sem.at[p, self.c],
                (lax.rem(self.d + p + 1, self.dp), self.t),
            )

    def finish(self):
        arrived(self.out.at[1 - self.c], self.one_sem.at[2], self.core)

    def pass_peers(self):
        for p in range(self.dp - 1):
            box = self.peer_out.at[p, self.c]
            arrived(box, self.peer_sem.at[p, self.c], self.core)
            self.copies.send(box, box, self.peer_sem.at[p, self.c], self.core)

    def finish_peers(self):
        for p in range(self.dp - 1):
            arrived(self.peer_out.at[p, 1 - self.c], self.peer_sem.at[p, 1 - self.c], self.core)


def power(r):
    return r > 0 and r & (r - 1) == 0


def mine(r):
    return r == 0 or power(r)


def pair_of(m, g, levels):
    diff = m ^ g
    return sum((diff >= (1 << k)).astype(jnp.int32) for k in range(levels))


def by_distance(a, A):
    table = [sorted(range(A), key=lambda r: (abs(r - v), r)) for v in range(A)]
    rows = []
    for i in range(A):
        row = table[0][i]
        for v in range(1, A):
            row = jnp.where(a == v, table[v][i], row)
        rows.append(row)
    return rows


def layer_kernel(
    dp, T, live_ref, mb_any, hb_any, inp_any, og_any, upw_ref, dnw_ref, upl_any, upr_any, dnl_any, dnr_any,
    own_out, peer_g_out, hd_out, peer_hd_out, peer_own_out, red_out, peer_red_out,
    low_out, peer_low_out, summed_out, dpair_out, upair_out, upl_out, dnr_out, ps,
    full, peer_g, peer_x, hd, peer_hd, peer_own, red, peer_red, low, peer_low, summed, dpair, upair, upl_ref, dnr_ref, keep_sem,
    mb_ref, hb_ref, inp_ref, og_ref, upr, dnl, small_sem,
    wup, wdn, wsem, idx_v, idx_s, isem,
    part, mid, own_half, core_in, side_in, line_in, lpart, lmid, lown_half, lcore_in, lside_in, lline_in, slope, split_x, split_hd,
    terms, core_box, stage, side_box, acc, line_box, far_part, far_box, far_sem,
    send_sem, full_sem, pg_sem, px_sem, po_sem, one_sem, tline_sem, pr_sem,
    lone_sem, lline_sem, pl_sem, hd_sem, core_sem, side_sem, line_sem,
):
    d, t = lax.axis_index("dp"), lax.axis_index("tensor")
    c, b, a = t % 2, (t // 2) % 2, t // 4
    A = T // 4
    q = t % A
    slots, blk = upw_ref.shape[0], upw_ref.shape[1]
    bps, n = full.shape[2], full.shape[4]
    blocks = hd.shape[1]
    rank = red.shape[1]
    half = dpair.shape[1]
    total_blocks = T * bps
    levels = total_blocks.bit_length() - 1
    low_levels = blocks.bit_length() - 1
    J = levels + 1
    U = 4 if blocks % 4 == 0 else 1
    V = 4 if blocks % 4 == 0 else 1
    peers = dp - 1
    core, side = (d, a * 4 + b * 2 + 1 - c), (d, a * 4 + (1 - b) * 2 + c)
    copies = Copies(send_sem)
    kept = []

    def keep(src, dst):
        copy = pltpu.make_async_copy(src, dst, keep_sem.at[len(kept)])
        copy.start()
        kept.append(copy)

    pairs = (
        (inp_any, inp_ref), (og_any, og_ref), (upl_any, upl_ref), (dnr_any, dnr_ref),
        (mb_any, mb_ref), (hb_any, hb_ref), (upr_any, upr), (dnl_any, dnl),
    )
    loads = [pltpu.make_async_copy(src, dst, small_sem.at[i]) for i, (src, dst) in enumerate(pairs)]
    for load in loads:
        load.start()
    load_up = pltpu.make_async_copy(upw_ref, wup.at[pl.ds(0, slots)], wsem.at[0])
    load_dn = pltpu.make_async_copy(dnw_ref, wdn.at[pl.ds(0, slots)], wsem.at[1])
    load_up.start()
    load_dn.start()
    loads[0].wait()
    loads[1].wait()
    for j in range(bps):
        full[t, 0, j] = inp_ref[:, j * blk : (j + 1) * blk].T
        full[t, 1, j] = og_ref[:, j * blk : (j + 1) * blk].T
    loads[2].wait()
    loads[3].wait()
    part[0] = dot3(upl_ref[...], full[t, 0].reshape(bps * blk, n), 0, 0)
    part[1] = dot3(dnr_ref[...], full[t, 1].reshape(bps * blk, n), 1, 0)
    greet(d, t, dp, T)

    def other(k):
        return lax.rem(d + k + 1, dp)

    def send(i, s, where, cond=None):
        copies.send(full.at[s, i], full.at[s, i], full_sem.at[s, i], where, cond)

    def got(i, s, where, cond=None):
        arrived(full.at[s, i], full_sem.at[s, i], where, cond)

    def across(i, s, cond=None):
        for k in range(peers):
            o = other(k)
            if i:
                copies.send(full.at[s, 1], peer_g.at[k, s], pg_sem.at[k, s], (o, t), cond)
            else:
                rows = pl.ds(pl.multiple_of(o * half, half), half)
                copies.send(full.at[s, 0, :, rows, :], peer_x.at[k, s], px_sem.at[k, s], (o, t), cond)

    own_rows = peer_own.shape[1]

    rows_near = by_distance(a, A)

    def gap(row):
        return jnp.where(row > a, row - a, a - row)

    at_end = (a == 0) | (a == A - 1)
    at_middle = (a > 0) & (a < A - 1)

    def down_line(i, rows, cond):
        for row in rows:
            send(i, t, (d, row * 4 + b * 2 + c), cond)

    def near(s):
        return s // 8 == q // 2

    near_rows = [q // 2 * 2, q // 2 * 2 + 1]

    def place(k, col):
        return rows_near[k] * 4 + col * 2 + c

    def from_line(i, k):
        s = place(k, b)
        got(i, s, side)
        onward = jnp.where(rows_near[k] > a, a - 1, a + 1)
        inside = (onward >= 0) & (onward < A)
        send(i, s, (d, lax.rem(onward + A, A) * 4 + b * 2 + c), inside)
        send(i, s, side)
        across(i, s, near(s) if i else None)
        send(i, s, core)

    def from_side(i, k):
        s = place(k, 1 - b)
        got(i, s, side)
        across(i, s, near(s) if i else None)
        send(i, s, core)

    my_places = [t, place(0, 1 - b)]
    for k in range(1, A):
        my_places += [place(k, b), place(k, 1 - b)]

    total = Total(
        red, peer_red, dp, d, t, T, part, mid, own_half, core_in, side_in, line_in, copies,
        (one_sem, tline_sem, pr_sem),
    )
    total.to_core()
    down_line(0, rows_near[1:2], None)
    down_line(0, rows_near[2:3], at_middle)
    across(0, t)
    total.to_side()
    send(0, t, side)
    send(0, t, core)
    total.to_line()
    send(1, t, side)
    across(1, t)
    send(1, t, core)
    for k in range(peers):
        o = other(k)
        at = o * own_rows * peer_own.shape[2]
        for j in range(own_rows):
            pos = at + j * peer_own.shape[2]
            inner = pl.ds(pl.multiple_of(pos % blk, peer_own.shape[2]), peer_own.shape[2])
            copies.send(full.at[t, 0, pos // blk, inner, :], peer_own.at[k, j], po_sem.at[k, j], (o, t))

    for load in loads[4:]:
        load.wait()

    lane = lax.broadcasted_iota(jnp.int32, (8, 128), 1)
    wide = 8 if slots % 8 == 0 else 1

    def number(s, v):
        h = hb_ref[s]
        p = h * J + pair_of(mb_ref[s], (t * blocks + h) % total_blocks, levels)
        p = jnp.where(s < live_ref[0], p, -1)
        ps[s] = p
        return jnp.where(lane == s, p, v)

    row_of = lax.fori_loop(0, slots, number, jnp.full((8, 128), -2, jnp.int32), unroll=wide)

    def link(s, v):
        prev, last = v
        p = ps[s]
        prev = jnp.where((lane > s) & (row_of == p), s, prev)
        last = jnp.where(lane == p, s, last)
        return prev, last

    none = jnp.full((8, 128), slots, jnp.int32)
    prev, last = lax.fori_loop(0, slots, link, (none, none), unroll=wide)
    idx_v[0] = prev
    idx_v[1] = last
    to_scalar = pltpu.make_async_copy(idx_v, idx_s, isem.at[0])
    to_scalar.start()
    keep(upl_ref, upl_out)
    keep(dnr_ref, dnr_out)
    from_line(0, 1)
    down_line(1, rows_near[1:2], at_end)
    from_side(0, 0)
    for k in range(2, A):
        from_line(0, k)
    down_line(1, rows_near[1:3], at_middle)
    total.reduce()
    from_side(0, 1)
    from_side(1, 0)
    from_side(0, 2)
    from_line(1, 1)
    for k in range(3, A):
        from_side(0, k)
    to_scalar.wait()
    load_up.wait()
    load_dn.wait()
    wup[slots] = jnp.zeros((blk, blk), f32)
    wdn[slots] = jnp.zeros((blk, blk), f32)

    @pl.loop(0, slots)
    def _(s):
        before_it = idx_s[0, 0, s]
        wup[s] = wup[s] + wup[before_it]
        wdn[s] = wdn[s] + wdn[before_it]

    from_line(1, 2)
    total.share()

    def from_core(i):
        for k in range(2 * A):
            got(i, k * 2 + 1 - c, core)

    far = [1 << k for k in range(levels - low_levels)]

    def weight(w, h, j):
        return w[idx_s[1, 0, h * J + j]]

    def split_in(i):
        @pl.loop(0, blocks)
        def _(m):
            split_x[m] = right3(full[q * 4 + m // bps, i, m % bps], 0)

    def gather_up(i, h, w, axis, start):
        v = start + contract(left3(weight(w, h, 0), axis), split_x[h], axis, 0)
        for k in range(low_levels):
            v = v + contract(left3(weight(w, h, 1 + k), axis), split_x[flip(h, 1 << k, blocks)], axis, 0)
        for k, r in enumerate(far):
            x = right3(full[flip(q, r, A) * 4 + h // bps, i, h % bps], 0)
            v = v + contract(left3(weight(w, h, 1 + low_levels + k), axis), x, axis, 0)
        return v

    def span(h):
        return pl.ds(pl.multiple_of(h * blk, blk), blk)

    from_core(0)
    total.finish()
    split_in(0)
    low_in = right3(red[0], 0)
    scale = 0.7978845608028654

    @pl.loop(0, blocks // U)
    def _(i):
        for j in range(U):
            h = i * U + j
            v = gather_up(0, h, wup, 0, contract(left3(upr[:, span(h)], 0), low_in, 0, 0))
            th = jnp.tanh(scale * (v + 0.044715 * (v * v * v)))
            hidden = 0.5 * v * (1.0 + th)
            slope[h] = 0.5 * (1.0 + th) + 0.5 * v * (1.0 - th * th) * (scale * (1.0 + 3 * 0.044715 * (v * v)))
            hd[0, h] = hidden
            split_hd[h] = right3(hidden, 0)

    part_blocks = blocks // 2
    halved = dp == 2 and blocks % 2 == 0

    def hidden_parts(p, o):
        if p == 0 and halved:
            rows = pl.ds(pl.multiple_of(o * half, half), half)
            return [(pl.ds(o * part_blocks, part_blocks),), (pl.ds((1 - o) * part_blocks, part_blocks), rows)]
        return [(pl.ds(j * part_blocks, part_blocks),) for j in range(2)]

    def send_hidden(p):
        for k in range(peers):
            for j, at in enumerate(hidden_parts(p, other(k))):
                copies.send(hd.at[(p,) + at], peer_hd.at[(k, p) + at], hd_sem.at[k, p, j], (other(k), t))

    def to_partner(p, rows):
        for r in rows:
            row = flip(q, r, A)
            copies.send(terms.at[row, p, 1 - c], core_box.at[row, p], core_sem.at[row, p], core)

    def spread_far(p, w, axis):
        rows = [flip(q, r, A) for r in far]

        @pl.loop(0, blocks // U)
        def _(i):
            for j in range(U):
                h = i * U + j
                u = h // bps
                for k, row in enumerate(rows):
                    terms[row, p, u % 2, u // 2, h % bps] = contract(
                        left3(weight(w, h, 1 + low_levels + k), axis), split_hd[h], axis, 0
                    )

        to_partner(p, far)

    def spread_near(p, w, axis):
        @pl.loop(0, blocks // U)
        def _(i):
            for j in range(U):
                m = i * U + j
                u = m // bps
                v = contract(left3(weight(w, m, 0), axis), split_hd[m], axis, 0)
                for k in range(low_levels):
                    h = flip(m, 1 << k, blocks)
                    v = v + contract(left3(weight(w, h, 1 + k), axis), split_hd[h], axis, 0)
                terms[q, p, u % 2, u // 2, m % bps] = v

        to_partner(p, [0])

    order = []
    for r in range(A):
        if r % 4 < 2:
            order += [r + 2, r] if A > 2 else [r]

    def to_side(p, some):
        for r in some:
            row = flip(q, r, A)
            theirs = mine(r ^ 1)
            if theirs:
                arrived(core_box.at[row, p], core_sem.at[row, p], core)
            if mine(r) and not theirs:
                src = terms.at[row, p, c, 1 - b]
            elif theirs and not mine(r):
                src = core_box.at[row, p, 1 - b]
            else:
                src = stage.at[row, p]
                if theirs:
                    stage[row, p] = terms[row, p, c, 1 - b] + core_box[row, p, 1 - b]
                else:
                    stage[row, p] = jnp.zeros(stage.shape[2:], f32)
            copies.send(src, side_box.at[row, p], side_sem.at[row, p], side)

    def to_line(p, some):
        for r in some:
            row = flip(q, r, A)
            arrived(side_box.at[row, p], side_sem.at[row, p], side)
            v = side_box[row, p]
            if mine(r):
                v = v + terms[row, p, c, b]
            if mine(r ^ 1):
                v = v + core_box[row, p, b]
            acc[row, p] = v
            k = flip(row, a, A)
            copies.send(
                acc.at[row, p], line_box.at[k, p], line_sem.at[k, p], (d, row * 4 + b * 2 + c), row != a
            )

    def pass_stage(box, sem, places):
        for s in places:
            for k in range(peers):
                arrived(box.at[k, s], sem.at[k, s], core)
                copies.send(box.at[k, s], box.at[k, s], sem.at[k, s], core)

    def passed_stage(box, sem, rows):
        for k in range(peers):
            for row in rows:
                for col in range(2):
                    s = row * 4 + col * 2 + 1 - c
                    arrived(box.at[k, s], sem.at[k, s], core)

    def far_stage():
        for i, r in enumerate(far[1:]):
            row = flip(q, r, A)

            @pl.loop(0, blocks)
            def _(h):
                g = right3(full[row * 4 + h // bps, 1, h % bps], 1)
                for k in range(peers):
                    rows = pl.ds(pl.multiple_of(other(k) * half, half), half)
                    far_part[k, i, h] = contract(left3(hd[0, h, rows, :], 1), g, 1, 1)

        for k in range(peers):
            copies.send(far_part.at[k], far_box.at[k], far_sem.at[k], (other(k), t))

    def far_wait_stage():
        for k in range(peers):
            arrived(far_box.at[k], far_sem.at[k], core)

    def hidden_stage(p):
        for k in range(peers):
            for j, at in enumerate(hidden_parts(p, d)):
                arrived(peer_hd.at[(k, p) + at], hd_sem.at[k, p, j], core)

    here_rows = pl.ds(pl.multiple_of(d * half, half), half)

    def hidden_rows(h):
        rows = [hd[0, h, here_rows, :]] + [peer_hd[k, 0, h, here_rows, :] for k in range(peers)]
        return left3(jnp.concatenate(rows, axis=1), 1)

    def grad_cols(plane, m):
        s = plane * 4 + m // bps
        g = [full[s, 1, m % bps]] + [peer_g[k, s, m % bps] for k in range(peers)]
        return right3(jnp.concatenate(g, axis=1), 1)

    def down_stage():
        def one(m):
            g = grad_cols(q, m)
            left = jnp.concatenate(
                [hidden_rows(m)] + [hidden_rows(flip(m, 1 << k, blocks)) for k in range(low_levels)], axis=0
            )
            v = contract(left, g, 1, 1)
            dpair[m * J] = v[:half]
            for k in range(low_levels):
                dpair[flip(m, 1 << k, blocks) * J + 1 + k] = v[(k + 1) * half : (k + 2) * half]
            dpair[m * J + 1 + low_levels] = contract(hidden_rows(m), grad_cols(flip(q, 1, A), m), 1, 1)
            own_hidden = left3(hd[0, m, here_rows, :], 1)
            for i, r in enumerate(far[1:]):
                g = right3(full[flip(q, r, A) * 4 + m // bps, 1, m % bps], 1)
                v = contract(own_hidden, g, 1, 1)
                for k in range(peers):
                    v = v + far_box[k, i, m]
                dpair[m * J + 2 + low_levels + i] = v

        @pl.loop(0, blocks // V)
        def _(i):
            for j in range(V):
                one(i * V + j)

    def data_rows(plane, m):
        s = plane * 4 + m // bps
        x = [full[s, 0, m % bps, here_rows, :]] + [peer_x[k, s, m % bps] for k in range(peers)]
        return left3(jnp.concatenate(x, axis=1), 1)

    def up_stage():
        def one(h):
            back = [hd[1, h]] + [peer_hd[k, 1, h] for k in range(peers)]
            back = right3(jnp.concatenate(back, axis=1), 1)
            left = [data_rows(q, h)] + [data_rows(q, flip(h, 1 << k, blocks)) for k in range(low_levels)]
            left += [data_rows(flip(q, r, A), h) for r in far]
            v = contract(jnp.concatenate(left, axis=0), back, 1, 1)
            for j in range(J):
                upair[h * J + j] = v[j * half : (j + 1) * half]

        @pl.loop(0, blocks // V)
        def _(i):
            for j in range(V):
                one(i * V + j)

    def sum_stage():
        for p in range(2):
            v = acc[a, p]
            for k in range(1, A):
                arrived(line_box.at[k, p], line_sem.at[k, p], core)
                v = v + line_box[k, p]
            summed[p] = v

    def own_stage():
        for k in range(peers):
            for j in range(own_rows):
                arrived(peer_own.at[k, j], po_sem.at[k, j], core)

    send_hidden(0)
    keep(hd.at[0], hd_out.at[0])
    for k in range(3, A):
        from_line(1, k)
    spread_far(0, wdn, 0)
    to_side(0, order[:1])
    spread_near(0, wdn, 0)
    to_side(0, order[1:])
    for k in range(1, A):
        from_side(1, k)
    lpart[0] = jnp.zeros((rank, n), f32)
    lpart[1] = jnp.zeros((rank, n), f32)
    from_core(1)
    split_in(1)
    back_mid = right3(red[1], 0)

    @pl.loop(0, blocks // U)
    def _(i):
        for j in range(U):
            h = i * U + j
            lpart[0] += contract(left3(dnl[span(h), :], 0), split_hd[h], 0, 0)
            v = gather_up(1, h, wdn, 1, contract(left3(dnl[span(h), :], 1), back_mid, 1, 0))
            back = v * slope[h]
            hd[1, h] = back
            bs = right3(back, 0)
            split_hd[h] = bs
            lpart[1] += contract(left3(upr[:, span(h)], 1), bs, 1, 0)

    send_hidden(1)
    low_total = Total(
        low, peer_low, dp, d, t, T, lpart, lmid, lown_half, lcore_in, lside_in, lline_in, copies,
        (lone_sem, lline_sem, pl_sem),
    )
    low_total.to_core()
    keep(hd.at[1], hd_out.at[1])
    to_line(0, order[:2])
    spread_far(1, wup, 1)
    low_total.to_side()
    to_side(1, order[:1])
    spread_near(1, wup, 1)
    to_line(0, order[2:])
    to_side(1, order[1:])
    low_total.to_line()
    far_stage()

    pass_stage(peer_x, px_sem, my_places)
    total.pass_peers()
    to_line(1, order[:2])
    pass_stage(peer_g, pg_sem, [row * 4 + col * 2 + c for row in near_rows for col in range(2)])
    for k in range(peers):
        arrived(peer_g.at[k, t], pg_sem.at[k, t], core, (t // 8 < q // 2) | (t // 8 > q // 2))
    passed_stage(peer_x, px_sem, range(A))
    passed_stage(peer_g, pg_sem, near_rows)
    keep(full.at[t], own_out)
    keep(peer_g.at[:, t], peer_g_out)
    to_line(1, order[2:])
    own_stage()
    total.finish_peers()
    keep(red, red_out)
    keep(peer_red, peer_red_out)
    keep(peer_own, peer_own_out)
    hidden_stage(0)
    if halved:
        blocks_here = pl.ds(d * part_blocks, part_blocks)
        keep(peer_hd.at[:, 0, blocks_here], peer_hd_out.at[:, 0, blocks_here])
    else:
        keep(peer_hd.at[:, 0], peer_hd_out.at[:, 0])
    low_total.reduce()
    hidden_stage(1)
    keep(peer_hd.at[:, 1], peer_hd_out.at[:, 1])
    up_stage()
    keep(upair, upair_out)
    low_total.share()
    far_wait_stage()
    down_stage()
    keep(dpair, dpair_out)
    low_total.finish()
    keep(low, low_out)
    low_total.pass_peers()
    sum_stage()
    keep(summed, summed_out)
    low_total.finish_peers()
    keep(peer_low, peer_low_out)
    for copy in kept:
        copy.wait()
    copies.drain()
    if copies.count != send_sem.shape[0]:
        raise ValueError(copies.count, send_sem.shape[0])


def grads_kernel(
    dp, own_in, peer_g, hd, peer_hd,
    peer_own, red, peer_red, low, peer_low, summed, dpair, upair, upl, dnr, ps,
    res, ing, upg, dng, uplg, uprg, dnlg, dnrg,
):
    slots, half, blk = upg.shape
    bps = own_in.shape[1]
    blocks = hd.shape[1]
    d = lax.axis_index("dp")
    peers = range(dp - 1)

    def cat(first, rest):
        return jnp.concatenate([first] + rest, axis=1)

    unroll = 4 if slots % 4 == 0 else 1

    @pl.loop(0, slots // unroll)
    def _(i):
        for j in range(unroll):
            s = i * unroll + j
            p = ps[s]
            keep = (p >= 0).astype(f32)
            p = jnp.maximum(p, 0)
            upg[s] = upair[p] * keep
            dng[s] = dpair[p] * keep

    for j in range(bps):
        span = slice(j * blk, (j + 1) * blk)
        res[:, span] = (summed[0, j] + dot3(dnr[:, span], low[0], 0, 0)).T
        ing[:, span] = (summed[1, j] + dot3(upl[span, :], low[1], 1, 0)).T
    back_in = right3(cat(low[1], [peer_low[k, 1] for k in peers]), 1)
    n = uplg.shape[0]
    step = min(n, blk)
    for j in range(n // step):
        at = d * n + j * step
        inner = pl.ds(pl.multiple_of(at % blk, step), step)
        x = cat(own_in[0, at // blk, inner, :], [peer_own[k, j] for k in peers])
        uplg[j * step : (j + 1) * step, :] = contract(left3(x, 1), back_in, 1, 1)
    n = uprg.shape[0]
    span = pl.ds(pl.multiple_of(d * n, n), n)
    left_in = left3(cat(red[0, span, :], [peer_red[k, 0, span, :] for k in peers]), 1)
    left_mid = left3(cat(low[0, span, :], [peer_low[k, 0, span, :] for k in peers]), 1)
    for h in range(blocks):
        back = cat(hd[1, h], [peer_hd[k, 1, h] for k in peers])
        uprg[:, h * blk : (h + 1) * blk] = contract(left_in, right3(back, 1), 1, 1)
    for j in range(bps):
        g = cat(own_in[1, j], [peer_g[k, j] for k in peers])
        dnrg[:, j * blk : (j + 1) * blk] = contract(left_mid, right3(g, 1), 1, 1)
    back_mid = right3(cat(red[1], [peer_red[k, 1] for k in peers]), 1)
    n = dnlg.shape[0]
    step = min(n, blk)
    for j in range(n // step):
        at = d * n + j * step
        inner = pl.ds(pl.multiple_of(at % blk, step), step)
        hidden = cat(hd[0, at // blk, inner, :], [peer_hd[k, 0, at // blk, inner, :] for k in peers])
        dnlg[j * step : (j + 1) * step, :] = contract(left3(hidden, 1), back_mid, 1, 1)


def shards(
    dp, T,
    inputs, out_grad, up_weight, down_weight, up_left, up_right, down_left, down_right,
    model_block, hidden_block, live_slots,
):
    tokens, feats = inputs.shape
    slots, blk = up_weight.shape[0], up_weight.shape[1]
    width = up_right.shape[1]
    rank = up_left.shape[1]
    blocks = width // blk
    bps = feats // blk
    A = T // 4
    peers = dp - 1
    half = blk // dp
    pairs = blocks * (T * bps).bit_length()
    own = feats // dp
    own_step = min(own, blk)
    own_rows = own // own_step
    DMA = pltpu.SemaphoreType.DMA
    sds = lambda *shape: jax.ShapeDtypeStruct(shape, f32)
    vmem = lambda *shape: pltpu.VMEM(shape, f32)
    bf16 = jnp.bfloat16
    spare = A.bit_length() - 2
    gather = 2 + peers + (A - 1) * (3 + peers) + A * (1 + peers)
    total = 4 + A - 1 + 2 * peers
    scatter = 2 * (1 + A.bit_length() - 1) + 4 * A
    sends = 2 * gather + 5 + 2 * total + scatter + peers * (own_rows + 2 * A + 9)
    outs = pl.pallas_call(
        functools.partial(layer_kernel, dp, T),
        out_shape=(
            sds(2, bps, blk, tokens),
            sds(peers, bps, blk, tokens),
            sds(2, blocks, blk, tokens),
            sds(peers, 2, blocks, blk, tokens),
            sds(peers, own_rows, own_step, tokens),
            sds(2, rank, tokens),
            sds(peers, 2, rank, tokens),
            sds(2, rank, tokens),
            sds(peers, 2, rank, tokens),
            sds(2, bps, blk, tokens),
            sds(pairs, half, blk),
            sds(pairs, half, blk),
            sds(feats, rank),
            sds(rank, feats),
            jax.ShapeDtypeStruct((slots,), jnp.int32),
        ),
        in_specs=[SM] + [HB] * 10,
        out_specs=[pl.BlockSpec(memory_space=pl.ANY)] * 14 + [SM],
        scratch_shapes=[
            vmem(T, 2, bps, blk, tokens),
            vmem(peers, T, bps, blk, tokens),
            vmem(peers, T, bps, half, tokens),
            vmem(2, blocks, blk, tokens),
            vmem(peers, 2, blocks, blk, tokens),
            vmem(peers, own_rows, own_step, tokens),
            vmem(2, rank, tokens),
            vmem(peers, 2, rank, tokens),
            vmem(2, rank, tokens),
            vmem(peers, 2, rank, tokens),
            vmem(2, bps, blk, tokens),
            vmem(pairs, half, blk),
            vmem(pairs, half, blk),
            vmem(feats, rank),
            vmem(rank, feats),
            DMA((17,)),
            pltpu.SMEM((slots,), jnp.int32), pltpu.SMEM((slots,), jnp.int32),
            vmem(tokens, feats), vmem(tokens, feats), vmem(rank, width), vmem(width, rank), DMA((8,)),
            vmem(slots + 1, blk, blk), vmem(slots + 1, blk, blk), DMA((2,)),
            pltpu.VMEM((2, 8, 128), jnp.int32), pltpu.SMEM((2, 8, 128), jnp.int32),
            DMA((1,)),
            vmem(2, rank, tokens), vmem(1, rank, tokens), vmem(rank // 2, tokens), vmem(rank, tokens),
            vmem(rank // 2, tokens), vmem(A, rank // 2, tokens),
            vmem(2, rank, tokens), vmem(1, rank, tokens), vmem(rank // 2, tokens), vmem(rank, tokens),
            vmem(rank // 2, tokens), vmem(A, rank // 2, tokens),
            vmem(blocks, blk, tokens),
            pltpu.VMEM((blocks, 3 * blk, tokens), bf16),
            pltpu.VMEM((blocks, 3 * blk, tokens), bf16),
            vmem(A, 2, 2, 2, bps, blk, tokens),
            vmem(A, 2, 2, bps, blk, tokens),
            vmem(A, 2, bps, blk, tokens),
            vmem(A, 2, bps, blk, tokens),
            vmem(A, 2, bps, blk, tokens),
            vmem(A, 2, bps, blk, tokens),
            vmem(peers, spare, blocks, half, blk), vmem(peers, spare, blocks, half, blk), DMA((peers,)),
            DMA((sends,)), DMA((T, 2)), DMA((peers, T)), DMA((peers, T)), DMA((peers, own_rows)),
            DMA((4,)), DMA((A,)), DMA((peers, 2)),
            DMA((4,)), DMA((A,)), DMA((peers, 2)), DMA((peers, 2, 2)),
            DMA((A, 2)), DMA((A, 2)), DMA((A, 2)),
        ],
        compiler_params=pltpu.CompilerParams(collective_id=0, has_side_effects=True, vmem_limit_bytes=46 << 20),
    )(
        live_slots,
        *(
            pltpu.with_memory_space_constraint(v, pltpu.HBM)
            for v in (
                model_block, hidden_block, inputs, out_grad, up_weight, down_weight,
                up_left, up_right, down_left, down_right,
            )
        )
    )
    return pl.pallas_call(
        functools.partial(grads_kernel, dp),
        out_shape=(
            sds(tokens, feats),
            sds(tokens, feats),
            sds(slots, half, blk),
            sds(slots, half, blk),
            sds(feats // dp, rank),
            sds(rank // dp, width),
            sds(width // dp, rank),
            sds(rank // dp, feats),
        ),
        in_specs=[VM] * 14 + [SM],
        out_specs=[VM] * 8,
        compiler_params=pltpu.CompilerParams(vmem_limit_bytes=24 << 20),
    )(*outs)


def solution(mesh):
    return jax.shard_map(
        functools.partial(shards, mesh.shape["dp"], mesh.shape["tensor"]),
        mesh=mesh,
        in_specs=(
            P("dp", "tensor"),
            P("dp", "tensor"),
            P("tensor", None, None),
            P("tensor", None, None),
            P("tensor", None),
            P(None, "tensor"),
            P("tensor", None),
            P(None, "tensor"),
            P("tensor"),
            P("tensor"),
            P("tensor"),
        ),
        out_specs=(
            P("dp", "tensor"),
            P("dp", "tensor"),
            P("tensor", "dp", None),
            P("tensor", "dp", None),
            P(("tensor", "dp"), None),
            P("dp", "tensor"),
            P(("tensor", "dp"), None),
            P("dp", "tensor"),
        ),
        check_vma=False,
    )
```
